32 devices in a mesh: parts: 2 (over x), view: 16 (over z, y, core).
Axes of the slice: x: 2, y: 2, z: 4, core: 2. Of those that a mesh axis runs over, the one named last changes fastest.
Arguments:
- volume: bfloat16 [32, 4, 32, 512], P(None, 'parts', 'view'), parts along dimension 1, may hold values from -6 to 6
- dual_state: bfloat16 [32, 4, 16, 512], P(None, 'parts', 'view'), parts along dimension 1, may hold values from -6 to 6
- sinogram: bfloat16 [4, 4, 16, 512], P(None, 'parts', 'view'), parts along dimension 1, may hold values from -6 to 6
- cot_volume: bfloat16 [32, 4, 32, 512], P(None, 'parts', 'view'), parts along dimension 1, may hold values from -6 to 6
- cot_dual: bfloat16 [32, 4, 16, 512], P(None, 'parts', 'view'), parts along dimension 1, may hold values from -6 to 6
- basis_table: bfloat16 [8, 32], replicated, may hold values from -1 to 1
- bin_energy: int32 [4], replicated, may hold values from 0 to 7
- footprint_table: bfloat16 [4, 1024, 128], replicated, may hold values from -0.0625 to 0.0625
- hit_tile: int32 [16, 12], replicated, may hold values from 0 to 15, as said below
- hit_table: int32 [16, 12], replicated, may hold values from 0 to 3
- hit_column: int32 [16, 12], replicated, may hold values from 0 to 3
- hit_count: int32 [16], replicated, may hold values from 2 to 12, as said below
- primal_inner: bfloat16 [27, 32, 36], replicated, may hold values from -0.1875 to 0.1875
- primal_inner_bias: float32 [32], replicated, may hold values from -3 to 3
- primal_outer: bfloat16 [27, 32, 32], replicated, may hold values from -0.21875 to 0.21875
- primal_outer_bias: float32 [32], replicated, may hold values from -3 to 3
- dual_inner: bfloat16 [27, 32, 40], replicated, may hold values from -0.1875 to 0.1875
- dual_inner_bias: float32 [32], replicated, may hold values from -3 to 3
- dual_outer: bfloat16 [27, 32, 32], replicated, may hold values from -0.21875 to 0.21875
- dual_outer_bias: float32 [32], replicated, may hold values from -3 to 3
Outputs:
- new_volume: bfloat16 [32, 4, 32, 512], P(None, 'parts', 'view'), parts along dimension 1
- new_dual: bfloat16 [32, 4, 16, 512], P(None, 'parts', 'view'), parts along dimension 1
- volume_grad: bfloat16 [32, 4, 32, 512], P(None, 'parts', 'view'), parts along dimension 1
- dual_grad: bfloat16 [32, 4, 16, 512], P(None, 'parts', 'view'), parts along dimension 1
- primal_inner_grad: float32 [54, 32, 36], P('parts'), parts along dimension 0
- primal_outer_grad: float32 [54, 32, 32], P('parts'), parts along dimension 0
- dual_inner_grad: float32 [54, 32, 40], P('parts'), parts along dimension 0
- dual_outer_grad: float32 [54, 32, 32], P('parts'), parts along dimension 0
The draws below stay inside these ranges and needn't reach their ends.
There are 2 independent parts, one for each index of `parts`. The reference program is written for one: setup_inputs(seed, part) draws one part's arguments, and reference() takes and returns one part's arrays. A program takes and returns all parts, laid end to end along the dimension named above; an argument that names none is the same for every part. Nothing has to cross between parts.
Inputs may be any that keep to these rules, and one draw needn't show every extreme that they name: `hit_tile`: each row holds 12 different tiles; a view block's rays cross the tiles of the first hit_count entries of its row. `hit_table`: only the live entries of a row matter. `hit_column`: only the live entries of a row matter. `hit_count`: some view block has exactly 12 live entries.
All inputs are finite; a program needn't handle non-finite values.
Results may differ from the reference program's by a relative error of at most 0.006.
Values may be sent and summed in bfloat16 or wider, within the bound.
No kernel may reach another device: no remote copies, remote signals or barrier semaphores. Data moves between devices by JAX's collectives and lax.ppermute only.
A program may use at most 64 MiB of HBM per device.

```python
import jax
import jax.numpy as jnp
from jax import lax

C = 32
NB = 4
NE = 8
X = 512
U = 512
UW = 128
NOFF = 4
VB = 1
Z = 2
YT = 2
BLOCKS = 16
Y = 32
V = 16
K_MAX = 12


def draw_hit_tile(key, part):
    subkeys = jax.random.split(jax.random.fold_in(key, 11), BLOCKS)
    shuffled = jax.vmap(lambda subkey: jax.random.permutation(subkey, BLOCKS))(subkeys)
    return shuffled[:, :K_MAX].astype(jnp.int32)


def draw_hit_count(key, part):
    lowest = BLOCKS // 8
    counts_drawn = jax.random.randint(jax.random.fold_in(key, 23), (BLOCKS,), lowest, K_MAX + 1)
    fullest = jax.random.randint(jax.random.fold_in(key, 29), (), 0, BLOCKS)
    return jnp.where(jnp.arange(BLOCKS) == fullest, K_MAX, counts_drawn).astype(jnp.int32)


def with_ends(values, own_key, least, largest):
    longest = values.shape.index(max(values.shape))
    spots = []
    for shift in (0, 1):
        where = [jax.random.randint(jax.random.fold_in(own_key, axis), (), 0, length) for axis, length in enumerate(values.shape)]
        where[longest] = (where[longest] + shift) % values.shape[longest]
        spots.append(tuple(where))
    return values.at[spots[0]].set(least).at[spots[1]].set(largest)


def steps_of(rng, shape, cuts, least, largest):
    def one(position, shards_of):
        steps = jax.random.uniform(jax.random.fold_in(jax.random.fold_in(rng, 6), position), (shards_of,), jnp.float32, least / len(cuts), largest / len(cuts))
        return jnp.repeat(jnp.exp(steps), shape[position] // shards_of).reshape((-1,) + (1,) * (len(shape) - position - 1))

    factor_of = one(*cuts[0])
    for cut in cuts[1:]:
        factor_of = factor_of * one(*cut)
    return factor_of


def centred(rng, extent, scale, bound, pieces=(), kind=jnp.bfloat16):
    level = steps_of(rng, extent, pieces, -0.22, 0.18) if pieces else 1.0
    drawn = jax.random.normal(rng, extent, jnp.float32) * scale * level
    return jnp.minimum(jnp.maximum(drawn, -bound), bound).astype(kind)


def setup_inputs(seed: int = 0, part: int = 0) -> dict:
    key_of = jax.random.split(jax.random.key(seed), 21)
    part_splits = jax.random.split(jax.random.fold_in(key_of[20], part), 21)
    volume = centred(part_splits[0], (C, Z, Y, X), 1.0, 6.0, ((2, 16),))
    dual_state = centred(part_splits[1], (C, Z, V, U), 1.0, 6.0, ((2, 16),))
    sinogram = centred(part_splits[2], (NB, Z, V, U), 1.0, 6.0, ((2, 16),))
    cot_volume = centred(part_splits[3], (C, Z, Y, X), 1.0, 6.0, ((2, 16),))
    cot_dual = centred(part_splits[4], (C, Z, V, U), 1.0, 6.0, ((2, 16),))
    basis_table = centred(key_of[5], (NE, C), C ** -0.5, 1.0)
    bin_energy = with_ends(jax.random.randint(key_of[6], (NB,), 0, NE), jax.random.fold_in(key_of[6], 1), 0, NE - 1).astype(jnp.int32)
    footprint_table = centred(key_of[7], (NOFF, YT * X, VB * UW), (8 * YT * X) ** -0.5, 0.0625)
    hit_tile = draw_hit_tile(jax.random.fold_in(key_of[20], 71), part)
    hit_table = with_ends(jax.random.randint(key_of[9], (BLOCKS, K_MAX), 0, NOFF), jax.random.fold_in(key_of[9], 1), 0, NOFF - 1).astype(jnp.int32)
    hit_column = with_ends(jax.random.randint(key_of[10], (BLOCKS, K_MAX), 0, U // UW), jax.random.fold_in(key_of[10], 1), 0, (U // UW) - 1).astype(jnp.int32)
    hit_count = draw_hit_count(jax.random.fold_in(key_of[20], 71), part)
    primal_inner = centred(key_of[12], (27, C, C + NB), (27 * (C + NB)) ** -0.5, 0.1875)
    primal_inner_bias = centred(key_of[13], (C,), 0.5, 3.0, (), jnp.float32)
    primal_outer = centred(key_of[14], (27, C, C), (27 * C) ** -0.5, 0.21875)
    primal_outer_bias = centred(key_of[15], (C,), 0.5, 3.0, (), jnp.float32)
    dual_inner = centred(key_of[16], (27, C, C + 2 * NB), (27 * (C + 2 * NB)) ** -0.5, 0.1875)
    dual_inner_bias = centred(key_of[17], (C,), 0.5, 3.0, (), jnp.float32)
    dual_outer = centred(key_of[18], (27, C, C), (27 * C) ** -0.5, 0.21875)
    dual_outer_bias = centred(key_of[19], (C,), 0.5, 3.0, (), jnp.float32)
    return dict(volume=volume, dual_state=dual_state, sinogram=sinogram, cot_volume=cot_volume, cot_dual=cot_dual, basis_table=basis_table, bin_energy=bin_energy, footprint_table=footprint_table, hit_tile=hit_tile, hit_table=hit_table, hit_column=hit_column, hit_count=hit_count, primal_inner=primal_inner, primal_inner_bias=primal_inner_bias, primal_outer=primal_outer, primal_outer_bias=primal_outer_bias, dual_inner=dual_inner, dual_inner_bias=dual_inner_bias, dual_outer=dual_outer, dual_outer_bias=dual_outer_bias)


precise = lax.Precision.HIGHEST

def hit_pairs(hit_tile, hit_table, hit_column, hit_count, tables, columns):
    blocks = hit_tile.shape[0]
    entries = hit_tile.shape[1]
    live_mask = (jnp.arange(entries)[None, :] < hit_count[:, None]).astype(jnp.float32)
    tile_onehot = (hit_tile[:, :, None] == jnp.arange(blocks)[None, None, :]).astype(jnp.float32)
    table_onehot = (hit_table[:, :, None] == jnp.arange(tables)[None, None, :]).astype(jnp.float32)
    column_onehot = (hit_column[:, :, None] == jnp.arange(columns)[None, None, :]).astype(jnp.float32)
    return jnp.einsum('bk,bkt,bko,bkc->btoc', live_mask, tile_onehot, table_onehot, column_onehot, precision=precise)

def silu_slope(pre_values):
    sigmoid = jax.nn.sigmoid(pre_values)
    return sigmoid * (1.0 + pre_values * (1.0 - sigmoid))

def volume_pad(source):
    return jnp.pad(source, ((0, 0), (1, 1), (1, 1), (1, 1)))

def cycle_pad(source):
    wrapped = jnp.concatenate([source[:, :, -1:], source, source[:, :, :1]], axis=2)
    return jnp.pad(wrapped, ((0, 0), (1, 1), (0, 0), (1, 1)))

def conv_apply(padded, weight, bias_vector):
    slices = padded.shape[1] - 2
    height = padded.shape[2] - 2
    breadth = padded.shape[3] - 2
    padded_wide = padded.astype(jnp.float32)
    weight_wide = weight.astype(jnp.float32)
    running = jnp.zeros((weight.shape[1], slices, height, breadth), jnp.float32)
    for tap_index in range(27):
        shift_z, shift_y, shift_x = (tap_index // 9, tap_index // 3 % 3, tap_index % 3)
        window = padded_wide[:, shift_z:shift_z + slices, shift_y:shift_y + height, shift_x:shift_x + breadth]
        running = running + jnp.einsum('oc,czyx->ozyx', weight_wide[tap_index], window, precision=precise)
    return running + bias_vector[:, None, None, None]

def conv_adjoint(padded, weight):
    slices = padded.shape[1] - 2
    height = padded.shape[2] - 2
    breadth = padded.shape[3] - 2
    padded_wide = padded.astype(jnp.float32)
    weight_wide = weight.astype(jnp.float32)
    running = jnp.zeros((weight.shape[2], slices, height, breadth), jnp.float32)
    for tap_index in range(27):
        shift_z, shift_y, shift_x = (tap_index // 9, tap_index // 3 % 3, tap_index % 3)
        window = padded_wide[:, 2 - shift_z:2 - shift_z + slices, 2 - shift_y:2 - shift_y + height, 2 - shift_x:2 - shift_x + breadth]
        running = running + jnp.einsum('oc,ozyx->czyx', weight_wide[tap_index], window, precision=precise)
    return running

def weight_grad(cotangent, padded):
    slices = cotangent.shape[1]
    height = cotangent.shape[2]
    breadth = cotangent.shape[3]
    padded_wide = padded.astype(jnp.float32)
    cot_wide = cotangent.astype(jnp.float32)
    per_tap = []
    for tap_index in range(27):
        shift_z, shift_y, shift_x = (tap_index // 9, tap_index // 3 % 3, tap_index % 3)
        window = padded_wide[:, shift_z:shift_z + slices, shift_y:shift_y + height, shift_x:shift_x + breadth]
        per_tap.append(jnp.einsum('ozyx,czyx->oc', cot_wide, window, precision=precise))
    return jnp.stack(per_tap)

def project(bin_images, footprint_table, pairs):
    bin_count, slices, ycells, xcells = bin_images.shape
    blocks = pairs.shape[0]
    columns = pairs.shape[3]
    row_count = ycells // blocks
    height = bin_count * slices
    tile_rows = bin_images.reshape(bin_count, slices, blocks, row_count, xcells).transpose(2, 0, 1, 3, 4)
    tile_rows = tile_rows.reshape(blocks, height, row_count * xcells).astype(jnp.float32)
    table_wide = footprint_table.astype(jnp.float32)
    footprints = jnp.einsum('tqs,osw->toqw', tile_rows, table_wide, precision=precise)
    windows = jnp.einsum('btoc,toqw->bcqw', pairs, footprints, precision=precise)
    view_count = footprint_table.shape[2] // UW
    layout = windows.reshape(blocks, columns, bin_count, slices, view_count, UW).transpose(2, 3, 0, 4, 1, 5)
    return layout.reshape(bin_count, slices, blocks * view_count, columns * UW)

def backproject(signal, footprint_table, pairs):
    bin_count, slices, all_views, detector = signal.shape
    blocks = pairs.shape[0]
    view_count = all_views // blocks
    columns = detector // UW
    height = bin_count * slices
    windows = signal.reshape(bin_count, slices, blocks, view_count, columns, UW).transpose(2, 4, 0, 1, 3, 5)
    windows = windows.reshape(blocks, columns, height, view_count * UW).astype(jnp.float32)
    grouped = jnp.einsum('btoc,bcqw->toqw', pairs, windows, precision=precise)
    tile_sums = jnp.einsum('toqw,osw->tqs', grouped, footprint_table.astype(jnp.float32), precision=precise)
    cell_count = tile_sums.shape[2] // YT
    layout = tile_sums.reshape(blocks, bin_count, slices, YT, cell_count).transpose(1, 2, 0, 3, 4)
    return layout.reshape(bin_count, slices, blocks * YT, cell_count)

def reference(volume, dual_state, sinogram, cot_volume, cot_dual, basis_table, bin_energy, footprint_table, hit_tile, hit_table, hit_column, hit_count, primal_inner, primal_inner_bias, primal_outer, primal_outer_bias, dual_inner, dual_inner_bias, dual_outer, dual_outer_bias):
    channels = volume.shape[0]
    bin_count = sinogram.shape[0]
    columns = dual_state.shape[3] // UW
    pairs = hit_pairs(hit_tile, hit_table, hit_column, hit_count, footprint_table.shape[0], columns)
    energy_onehot = (bin_energy[:, None] == jnp.arange(basis_table.shape[0])[None, :]).astype(jnp.float32)
    mixing = jnp.dot(energy_onehot, basis_table.astype(jnp.float32), precision=precise).astype(jnp.bfloat16)
    mixing_wide = mixing.astype(jnp.float32)
    bin_images = jnp.einsum('nc,czyx->nzyx', mixing_wide, volume.astype(jnp.float32), precision=precise).astype(jnp.bfloat16)
    projected = project(bin_images, footprint_table, pairs).astype(jnp.bfloat16)
    dual_in = jnp.concatenate([dual_state, projected, sinogram], axis=0)
    dual_in_pad = cycle_pad(dual_in)
    dual_pre = conv_apply(dual_in_pad, dual_inner, dual_inner_bias)
    dual_hidden = jax.nn.silu(dual_pre).astype(jnp.bfloat16)
    dual_hidden_pad = cycle_pad(dual_hidden)
    dual_update = conv_apply(dual_hidden_pad, dual_outer, dual_outer_bias)
    new_dual = (dual_state.astype(jnp.float32) + dual_update).astype(jnp.bfloat16)
    backprojected = backproject(new_dual[:bin_count], footprint_table, pairs).astype(jnp.bfloat16)
    primal_in = jnp.concatenate([volume, backprojected], axis=0)
    primal_in_pad = volume_pad(primal_in)
    primal_pre = conv_apply(primal_in_pad, primal_inner, primal_inner_bias)
    primal_hidden = jax.nn.silu(primal_pre).astype(jnp.bfloat16)
    primal_hidden_pad = volume_pad(primal_hidden)
    primal_update = conv_apply(primal_hidden_pad, primal_outer, primal_outer_bias)
    new_volume = (volume.astype(jnp.float32) + primal_update).astype(jnp.bfloat16)
    hidden_grad = conv_adjoint(volume_pad(cot_volume), primal_outer)
    pre_grad = (hidden_grad * silu_slope(primal_pre)).astype(jnp.bfloat16)
    in_grad = conv_adjoint(volume_pad(pre_grad), primal_inner)
    back_grad = in_grad[channels:].astype(jnp.bfloat16)
    toward_dual = project(back_grad, footprint_table, pairs)
    dual_total = jnp.concatenate([cot_dual[:bin_count].astype(jnp.float32) + toward_dual, cot_dual[bin_count:].astype(jnp.float32)], axis=0)
    dual_cot = dual_total.astype(jnp.bfloat16)
    dual_hidden_grad = conv_adjoint(cycle_pad(dual_cot), dual_outer)
    dual_pre_grad = (dual_hidden_grad * silu_slope(dual_pre)).astype(jnp.bfloat16)
    dual_in_grad = conv_adjoint(cycle_pad(dual_pre_grad), dual_inner)
    dual_grad = (dual_total + dual_in_grad[:channels]).astype(jnp.bfloat16)
    projected_grad = dual_in_grad[channels:channels + bin_count].astype(jnp.bfloat16)
    bins_grad = backproject(projected_grad, footprint_table, pairs)
    volume_grad = (cot_volume.astype(jnp.float32) + in_grad[:channels] + jnp.einsum('nc,nzyx->czyx', mixing_wide, bins_grad, precision=precise)).astype(jnp.bfloat16)
    primal_inner_grad = weight_grad(pre_grad, primal_in_pad)
    primal_outer_grad = weight_grad(cot_volume, primal_hidden_pad)
    dual_inner_grad = weight_grad(dual_pre_grad, dual_in_pad)
    dual_outer_grad = weight_grad(dual_cot, dual_hidden_pad)
    return (new_volume, new_dual, volume_grad, dual_grad, primal_inner_grad, primal_outer_grad, dual_inner_grad, dual_outer_grad)
```

```python
import functools

import jax
import jax.numpy as jnp
from jax import lax
from jax.experimental import pallas as pl
from jax.experimental.pallas import tpu as pltpu
from jax.sharding import PartitionSpec as P

UW = 128
TILE = 128
F32 = jnp.float32
BF16 = jnp.bfloat16
VMEM = pltpu.VMEM
SMEM = pltpu.SMEM


def call(kernel, operands, places, out_shapes, out_places, scratch=(), flops=10**8, size=10**6):
    return pl.pallas_call(
        kernel,
        out_shape=out_shapes,
        in_specs=[pl.BlockSpec(memory_space=place) for place in places],
        out_specs=[pl.BlockSpec(memory_space=place) for place in out_places],
        scratch_shapes=scratch,
        compiler_params=pltpu.CompilerParams(vmem_limit_bytes=24 * 1024 * 1024),
        cost_estimate=pl.CostEstimate(flops=flops, bytes_accessed=size, transcendentals=0),
    )(*operands)


def shape_of(dims, kind):
    return jax.ShapeDtypeStruct(dims, kind)


def dot(left, right):
    return jnp.dot(left, right, preferred_element_type=F32)


def dot_nt(left, right):
    return lax.dot_general(left, right, (((1,), (1,)), ((), ())), preferred_element_type=F32)


def shifted(wide):
    lanes = wide.shape[1]
    lane = lax.broadcasted_iota(jnp.int32, wide.shape, 1)
    low = jnp.where(lane == 0, 0.0, pltpu.roll(wide, 1, 1))
    high = jnp.where(lane == lanes - 1, 0.0, pltpu.roll(wide, lanes - 1, 1))
    return low, wide, high


def put_columns(column_ref, row, plane, slices):
    channels = plane.shape[0] // slices
    block = 3 * plane.shape[0]
    for tap, moved in enumerate(shifted(plane.astype(F32))):
        moved = moved.astype(BF16)
        for z in range(slices):
            start = row * block + (z * 3 + tap) * channels
            column_ref[start : start + channels, :] = moved[z * channels : (z + 1) * channels]


def window(column_ref, row, block):
    return column_ref[(row - 1) * block : (row + 2) * block, :]


def sigmoid(values):
    return 1.0 / (1.0 + jnp.exp(-values))


def spread_lists(gradient, slices, taps_z=3):
    channels = gradient.shape[0] // slices
    parts = []
    for z_in in range(slices):
        rows = []
        for i in range(taps_z):
            z_out = z_in - i + 1
            if 0 <= z_out < slices:
                rows.append(gradient[z_out * channels : (z_out + 1) * channels])
            else:
                rows.append(jnp.zeros((channels, gradient.shape[1]), BF16))
        parts.append(jnp.concatenate(rows, axis=0))
    return parts


def state_wgrad(gradient, column_ref, row, slices):
    channels = gradient.shape[0] // slices
    parts = spread_lists(gradient, slices)
    block = 3 * channels * slices
    pieces = []
    for j in range(3):
        total = None
        for z in range(slices):
            start = (row + j - 1) * block + z * 3 * channels
            term = dot_nt(parts[z], column_ref[start : start + 3 * channels, :])
            total = term if total is None else total + term
        pieces.append(total)
    return pieces


def prep_kernel(
    slices,
    bins,
    di,
    do,
    pi,
    po,
    dit,
    dot_,
    pit,
    pot,
    tile_ref,
    table_ref,
    column_ref,
    count_ref,
    pos_ref,
    d1s,
    d1e,
    d2,
    d2t,
    d1t,
    d1x,
    p1s,
    p1e,
    p2,
    p2t,
    p1t,
    p1x,
    code_ref,
    found_ref,
):
    channels = do.shape[1]

    def tap_of(i, j, l):
        return (i * 3 + j) * 3 + l

    def forward(weight, low, high, order):
        rows = []
        for z in range(slices):
            pieces = []
            for j in range(3):
                pairs = [(zi, l) for zi in range(slices) for l in range(3)]
                if order:
                    pairs = [(zi, l) for l in range(3) for zi in range(slices)]
                for zi, l in pairs:
                    i = zi - z + 1
                    if 0 <= i < 3:
                        pieces.append(weight[tap_of(i, j, l)].astype(F32)[:, low:high])
                    else:
                        pieces.append(jnp.zeros((weight.shape[1], high - low), F32))
            rows.append(jnp.concatenate(pieces, axis=1))
        return jnp.concatenate(rows, axis=0).astype(BF16)

    def adjoint(weight, low, high):
        rows = []
        for zi in range(slices):
            pieces = []
            for j in range(3):
                for z in range(slices):
                    for l in range(3):
                        i = zi - z + 1
                        if 0 <= i < 3:
                            pieces.append(weight[tap_of(i, 2 - j, 2 - l)].astype(F32)[low:high])
                        else:
                            pieces.append(jnp.zeros((high - low, weight.shape[2]), F32))
            rows.append(jnp.concatenate(pieces, axis=1))
        return jnp.concatenate(rows, axis=0).astype(BF16)

    d1s[...] = forward(di, 0, channels, False)
    d1e[...] = forward(di, channels, di.shape[2], True)
    d2[...] = forward(do, 0, channels, False)
    p1s[...] = forward(pi, 0, channels, False)
    p1e[...] = forward(pi, channels, pi.shape[2], True)
    p2[...] = forward(po, 0, channels, False)
    d2t[...] = adjoint(dot_, 0, channels)
    d1t[...] = adjoint(dit, 0, channels)
    d1x[...] = adjoint(dit, channels, channels + bins)
    p2t[...] = adjoint(pot, 0, channels)
    p1t[...] = adjoint(pit, 0, channels)
    p1x[...] = adjoint(pit, channels, channels + bins)

    blocks = tile_ref.shape[0]
    position = pos_ref[0]
    columns = 16
    for slot in range(3):
        found_ref[slot] = 0

    def each_block(b, carry):
        def each_entry(k, inner):
            slot = tile_ref[b, k] - position + 1

            @pl.when((slot >= 0) & (slot < 3))
            def _():
                at = found_ref[slot]
                code_ref[slot, at] = (b * columns + table_ref[b, k]) * columns + column_ref[b, k]
                found_ref[slot] = at + 1

            return inner

        return lax.fori_loop(0, count_ref[b], each_entry, carry)

    lax.fori_loop(0, blocks, each_block, 0)


def mixing_of(energy_ref, basis_ref, bins):
    energies = basis_ref.shape[0]
    row = lax.broadcasted_iota(jnp.int32, (bins, energies), 0)
    col = lax.broadcasted_iota(jnp.int32, (bins, energies), 1)
    onehot = jnp.zeros((bins, energies), F32)
    for n in range(bins):
        onehot = jnp.where((row == n) & (col == energy_ref[n]), 1.0, onehot)
    return dot(onehot.astype(BF16), basis_ref[...])


def send_rays(images, footprint_ref, send_ref):
    for table in range(footprint_ref.shape[0]):
        rays = dot(images, footprint_ref[table]).astype(BF16)
        for target in range(send_ref.shape[0]):
            send_ref[target, table] = rays


def bins_kernel(slices, bins, energy_ref, basis_ref, volume_ref, footprint_ref, send_ref):
    mixing = mixing_of(energy_ref, basis_ref, bins).astype(BF16)
    images = dot(mixing, volume_ref[...])
    cells = images.shape[1] // slices
    images = jnp.concatenate([images[:, z * cells : (z + 1) * cells] for z in range(slices)], axis=0)
    send_rays(images.astype(BF16), footprint_ref, send_ref)


def ray_windows(rays_ref, tile_ref, table_ref, column_ref, count_ref, pos_ref, sums_ref, views):
    blocks = tile_ref.shape[0]
    columns = sums_ref.shape[0] // len(views)
    sums_ref[...] = jnp.zeros_like(sums_ref)
    for place, offset in enumerate(views):
        view = lax.rem(pos_ref[0] + offset + blocks, blocks)

        def each_entry(k, carry):
            at = place * columns + column_ref[view, k]
            sums_ref[at] += rays_ref[tile_ref[view, k], table_ref[view, k]].astype(F32)
            return carry

        lax.fori_loop(0, count_ref[view], each_entry, 0)
    return [
        jnp.concatenate([sums_ref[place * columns + c] for c in range(columns)], axis=1)
        for place in range(len(views))
    ]


def view_plane(ref, slices, low, high):
    lanes = ref.shape[1] // slices
    return jnp.concatenate(
        [ref[low:high, z * lanes : (z + 1) * lanes] for z in range(slices)], axis=0
    )


def extra_rows(projected, sino_ref, slices, channels, bins):
    lanes = sino_ref.shape[1] // slices
    rows = []
    for z in range(slices):
        rows.append(projected[z * bins : (z + 1) * bins])
        rows.append(
            sino_ref[channels : channels + bins, z * lanes : (z + 1) * lanes].astype(F32)
        )
    return jnp.concatenate(rows, axis=0)


def extra_columns(pieces):
    return jnp.concatenate([piece for triple in pieces for piece in triple], axis=0).astype(BF16)


def dual_forward_kernel(
    slices,
    bins,
    rays_ref,
    tile_ref,
    table_ref,
    column_ref,
    count_ref,
    pos_ref,
    a0,
    a1,
    a2,
    a3,
    a4,
    w1s,
    w1e,
    w2,
    bias_ref,
    send_ref,
    new_ref,
    hidden_ref,
    slope_ref,
    extra_ref,
    sums_ref,
    columns_ref,
    hidden_columns,
):
    around = (a0, a1, a2, a3, a4)
    channels = new_ref.shape[0]
    block = 3 * channels * slices
    rows = channels * slices
    bias_inner = jnp.concatenate([bias_ref[:, 0:1]] * slices, axis=0)
    bias_outer = jnp.concatenate([bias_ref[:, 1:2]] * slices, axis=0)
    for row in range(5):
        put_columns(columns_ref, row, view_plane(around[row], slices, 0, channels), slices)
    projected = ray_windows(
        rays_ref, tile_ref, table_ref, column_ref, count_ref, pos_ref, sums_ref, (-2, -1, 0, 1, 2)
    )
    pieces = []
    for row in range(5):
        extra = extra_rows(
            projected[row].astype(BF16).astype(F32), around[row], slices, channels, bins
        )
        if 1 <= row <= 3:
            extra_ref[(row - 1) * extra.shape[0] : row * extra.shape[0], :] = extra.astype(BF16)
        pieces.append(shifted(extra))
    for row in range(1, 4):
        pre = dot(w1s[...], window(columns_ref, row, block))
        pre = pre + dot(w1e[...], extra_columns(pieces[row - 1 : row + 2])) + bias_inner
        gate = sigmoid(pre)
        hidden = (pre * gate).astype(BF16)
        at = (row - 1) * rows
        hidden_ref[at : at + rows, :] = hidden
        slope_ref[at : at + rows, :] = gate * (1.0 + pre * (1.0 - gate))
        put_columns(hidden_columns, row - 1, hidden, slices)
    update = dot(w2[...], hidden_columns[...]) + bias_outer
    fresh = (view_plane(a2, slices, 0, channels).astype(F32) + update).astype(BF16)
    lanes = fresh.shape[1]
    out = []
    for z in range(slices):
        plane = fresh[z * channels : (z + 1) * channels]
        new_ref[:, z * lanes : (z + 1) * lanes] = plane
        out.append(plane.astype(F32)[:bins])
    out = jnp.concatenate(out, axis=0).astype(BF16)
    for target in range(send_ref.shape[0]):
        send_ref[target] = out


def gather_signals(signal_ref, code_ref, found_ref, slots, footprint_ref, sums_ref):
    tables = footprint_ref.shape[0]
    sums_ref[...] = jnp.zeros_like(sums_ref)
    for place, slot in enumerate(slots):

        def each_hit(k, carry):
            code = code_ref[slot, k]
            at = place * tables + lax.rem(lax.div(code, 16), 16)
            lane = pl.multiple_of(lax.rem(code, 16) * UW, UW)
            sums_ref[at] += signal_ref[lax.div(code, 256), :, pl.ds(lane, UW)].astype(F32)
            return carry

        lax.fori_loop(0, found_ref[slot], each_hit, 0)
    total = None
    for table in range(tables):
        grouped = jnp.concatenate(
            [sums_ref[place * tables + table] for place in range(len(slots))], axis=0
        )
        high = grouped.astype(BF16).astype(F32)
        both = jnp.concatenate([high, grouped - high], axis=0).astype(BF16)
        term = dot_nt(both, footprint_ref[table])
        total = term if total is None else total + term
    half = total.shape[0] // 2
    return total[:half] + total[half:]


def put_payload(payload_ref, first, array):
    per = payload_ref.shape[2] // TILE
    flat = first
    width = array.shape[1]
    for group in range(array.shape[0] // 8):
        for tile in range(pl.cdiv(width, TILE)):
            last = min(width, (tile + 1) * TILE)
            lane = (flat % per) * TILE
            payload_ref[flat // per, :, lane : lane + last - tile * TILE] = array[
                group * 8 : group * 8 + 8, tile * TILE : last
            ].astype(BF16)
            flat += 1
    return flat


def take_payload(payload_ref, first, rows, width):
    per = payload_ref.shape[2] // TILE
    flat = first
    groups = []
    for _ in range(rows // 8):
        tiles = []
        for _ in range(pl.cdiv(width, TILE)):
            lane = (flat % per) * TILE
            tiles.append(payload_ref[flat // per, :, lane : lane + TILE].astype(F32))
            flat += 1
        groups.append(jnp.concatenate(tiles, axis=1) if len(tiles) > 1 else tiles[0])
    return jnp.concatenate(groups, axis=0), flat


def primal_kernel(
    slices,
    bins,
    rows_tile,
    signal_ref,
    code_ref,
    found_ref,
    pos_ref,
    v0,
    v1,
    v2,
    footprint_ref,
    w1s,
    w1e,
    w2,
    w2t,
    w1t,
    w1x,
    bias_ref,
    send_ref,
    new_ref,
    state_ref,
    inner_ref,
    outer_ref,
    extra_grad_ref,
    sums_ref,
    columns_ref,
    cot_columns,
    hidden_columns,
    grad_columns,
):
    blocks = send_ref.shape[0]
    channels = new_ref.shape[0]
    lanes = new_ref.shape[1] // (slices * rows_tile)
    block = 3 * channels * slices
    rows = channels * slices
    position = pos_ref[0]
    bias_inner = jnp.concatenate([bias_ref[:, 2:3]] * slices, axis=0)
    bias_outer = jnp.concatenate([bias_ref[:, 3:4]] * slices, axis=0)
    tiles = (v0, v1, v2)
    total_rows = 3 * rows_tile

    def plane_of(row, low):
        ref, r = tiles[row // rows_tile], row % rows_tile
        return jnp.concatenate(
            [
                ref[
                    low : low + channels,
                    (z * rows_tile + r) * lanes : (z * rows_tile + r + 1) * lanes,
                ]
                for z in range(slices)
            ],
            axis=0,
        )

    first, last = rows_tile, 2 * rows_tile
    used = range(first - 2, last + 2)
    for row in used:
        put_columns(columns_ref, row, plane_of(row, 0), slices)
        put_columns(cot_columns, row, plane_of(row, channels), slices)
    back = gather_signals(signal_ref, code_ref, found_ref, (0, 1, 2), footprint_ref, sums_ref)
    back = back.astype(BF16).astype(F32)
    height = slices * bins
    pieces = {}
    for row in used:
        tile, r = row // rows_tile, row % rows_tile
        pieces[row] = shifted(
            back[tile * height : (tile + 1) * height, r * lanes : (r + 1) * lanes]
        )
    extras = {}
    gradients = {}
    for row in range(first - 1, last + 1):
        extras[row] = extra_columns([pieces[row - 1], pieces[row], pieces[row + 1]])
        pre = dot(w1s[...], window(columns_ref, row, block))
        pre = pre + dot(w1e[...], extras[row]) + bias_inner
        gate = sigmoid(pre)
        hidden = pre * gate
        slope = gate * (1.0 + pre * (1.0 - gate))
        gradient = dot(w2t[...], window(cot_columns, row, block)) * slope
        if row < first:
            hidden = jnp.where(position > 0, hidden, 0.0)
            gradient = jnp.where(position > 0, gradient, 0.0)
        if row >= last:
            hidden = jnp.where(position < blocks - 1, hidden, 0.0)
            gradient = jnp.where(position < blocks - 1, gradient, 0.0)
        gradient = gradient.astype(BF16)
        gradients[row] = gradient
        put_columns(hidden_columns, row, hidden.astype(BF16), slices)
        put_columns(grad_columns, row, gradient, slices)
    parts = []
    for row in range(first, last):
        parts.append(dot(w1x[...], window(grad_columns, row, block)))
    send_rays(jnp.concatenate(parts, axis=1).astype(BF16), footprint_ref, send_ref)
    inner = None
    outer = None
    extra_total = None
    for row in range(first, last):
        r = row - first
        state = dot(w1t[...], window(grad_columns, row, block))
        state = state + plane_of(row, channels).astype(F32)
        update = dot(w2[...], window(hidden_columns, row, block)) + bias_outer
        fresh = (plane_of(row, 0).astype(F32) + update).astype(BF16)
        for z in range(slices):
            lane = (z * rows_tile + r) * lanes
            state_ref[:, lane : lane + lanes] = state[z * channels : (z + 1) * channels]
            new_ref[:, lane : lane + lanes] = fresh[z * channels : (z + 1) * channels]
        term = state_wgrad(gradients[row], columns_ref, row, slices)
        inner = term if inner is None else [a + b for a, b in zip(inner, term)]
        term = state_wgrad(plane_of(row, channels), hidden_columns, row, slices)
        outer = term if outer is None else [a + b for a, b in zip(outer, term)]
        term = dot_nt(gradients[row], extras[row])
        extra_total = term if extra_total is None else extra_total + term
    inner_ref[...] = jnp.concatenate(inner, axis=1)
    outer_ref[...] = jnp.concatenate(outer, axis=1)
    extra_grad_ref[...] = extra_total


def dual_backward_kernel(
    slices,
    bins,
    rays_ref,
    tile_ref,
    table_ref,
    column_ref,
    count_ref,
    pos_ref,
    c0,
    c1,
    c2,
    c3,
    c4,
    a1,
    a2,
    a3,
    hidden_ref,
    slope_ref,
    extra_ref,
    w2t,
    w1t,
    w1x,
    primal_inner,
    primal_outer,
    primal_extra,
    send_ref,
    grad_ref,
    payload_ref,
    sums_ref,
    columns_ref,
    grad_columns,
):
    around = (c0, c1, c2, c3, c4)
    channels = grad_ref.shape[0]
    block = 3 * channels * slices
    rows = channels * slices
    toward = ray_windows(
        rays_ref, tile_ref, table_ref, column_ref, count_ref, pos_ref, sums_ref, (-2, -1, 0, 1, 2)
    )
    own_total = None
    own_cot = None
    for row in range(5):
        lanes = toward[row].shape[1]
        spread = []
        for z in range(slices):
            spread.append(toward[row][z * bins : (z + 1) * bins])
            spread.append(jnp.zeros((channels - bins, lanes), F32))
        total = view_plane(around[row], slices, 0, channels).astype(F32)
        total = total + jnp.concatenate(spread, axis=0)
        put_columns(columns_ref, row, total.astype(BF16), slices)
        if row == 2:
            own_total = total
            own_cot = total.astype(BF16)
    own_gradient = None
    for row in range(1, 4):
        at = (row - 1) * rows
        gradient = dot(w2t[...], window(columns_ref, row, block)) * slope_ref[at : at + rows, :]
        gradient = gradient.astype(BF16)
        put_columns(grad_columns, row - 1, gradient, slices)
        if row == 2:
            own_gradient = gradient
    out = dot(w1x[...], grad_columns[...]).astype(BF16)
    width = out.shape[1]
    for target in range(send_ref.shape[0]):
        send_ref[target, :, 0:width] = out
    state = (dot(w1t[...], grad_columns[...]) + own_total).astype(BF16)
    for z in range(slices):
        grad_ref[:, z * width : (z + 1) * width] = state[z * channels : (z + 1) * channels]
    for row, ref in enumerate((a1, a2, a3)):
        put_columns(columns_ref, row, view_plane(ref, slices, 0, channels), slices)
        put_columns(
            grad_columns, row, hidden_ref[row * rows : (row + 1) * rows, :], slices
        )
    inner = jnp.concatenate(state_wgrad(own_gradient, columns_ref, 1, slices), axis=1)
    outer = jnp.concatenate(state_wgrad(own_cot, grad_columns, 1, slices), axis=1)
    height = extra_ref.shape[0] // 3
    pieces = [
        shifted(extra_ref[row * height : (row + 1) * height, :].astype(F32)) for row in range(3)
    ]
    extra = dot_nt(own_gradient, extra_columns(pieces))
    payload = payload_ref
    flat = put_payload(payload, 0, jnp.concatenate([inner, outer], axis=1))
    flat = put_payload(payload, flat, extra)
    flat = put_payload(
        payload, flat, jnp.concatenate([primal_inner[...], primal_outer[...]], axis=1)
    )
    put_payload(payload, flat, primal_extra[...])


def sum_kernel(payload_ref, send_ref):
    total = payload_ref[0].astype(F32)
    for source in range(1, payload_ref.shape[0]):
        total = total + payload_ref[source].astype(F32)
    total = total.astype(BF16)
    for target in range(send_ref.shape[0]):
        send_ref[target] = total


def volume_grad_kernel(
    slices,
    bins,
    signal_ref,
    code_ref,
    found_ref,
    energy_ref,
    basis_ref,
    footprint_ref,
    state_ref,
    out_ref,
    sums_ref,
):
    back = gather_signals(signal_ref, code_ref, found_ref, (1,), footprint_ref, sums_ref)
    mixing = mixing_of(energy_ref, basis_ref, bins)
    cells = back.shape[1]
    for z in range(slices):
        part = back[z * bins : (z + 1) * bins]
        high = part.astype(BF16).astype(F32)
        low = part - high
        spread = lax.dot_general(
            jnp.concatenate([mixing, mixing], axis=0).astype(BF16),
            jnp.concatenate([high, low], axis=0).astype(BF16),
            (((0,), (0,)), ((), ())),
            preferred_element_type=F32,
        )
        lane = z * cells
        out_ref[:, lane : lane + cells] = (state_ref[:, lane : lane + cells] + spread).astype(BF16)


def unpack_kernel(slices, payload_ref, primal_inner, primal_outer, dual_inner, dual_outer):
    channels = dual_outer.shape[1]
    flat = 0
    for inner_ref, outer_ref in ((dual_inner, dual_outer), (primal_inner, primal_outer)):
        extra_count = inner_ref.shape[2] - channels
        state, flat = take_payload(payload_ref, flat, 3 * channels, 18 * channels)
        extra, flat = take_payload(payload_ref, flat, slices * channels, 9 * slices * extra_count)
        for i in range(3):
            for j in range(3):
                for l in range(3):
                    tap = (i * 3 + j) * 3 + l
                    lane = (j * 3 + l) * channels
                    rows = state[i * channels : (i + 1) * channels]
                    more = None
                    for z in range(slices):
                        z_in = z + i - 1
                        if 0 <= z_in < slices:
                            at = ((j * 3 + l) * slices + z_in) * extra_count
                            term = extra[z * channels : (z + 1) * channels, at : at + extra_count]
                            more = term if more is None else more + term
                    inner_ref[tap] = jnp.concatenate(
                        [rows[:, lane : lane + channels], more], axis=1
                    )
                    lane = lane + 9 * channels
                    outer_ref[tap] = rows[:, lane : lane + channels]


def shards(
    volume,
    dual_state,
    sinogram,
    cot_volume,
    cot_dual,
    basis_table,
    bin_energy,
    footprint_table,
    hit_tile,
    hit_table,
    hit_column,
    hit_count,
    primal_inner,
    primal_inner_bias,
    primal_outer,
    primal_outer_bias,
    dual_inner,
    dual_inner_bias,
    dual_outer,
    dual_outer_bias,
):
    count = lax.axis_size("view")
    position = lax.axis_index("view").astype(jnp.int32).reshape(1)
    channels, slices, rows_tile, cells = volume.shape
    bins = sinogram.shape[0]
    detector = dual_state.shape[3]
    columns = detector // UW
    tables = footprint_table.shape[0]
    blocks, entries = hit_tile.shape
    height = slices * bins
    rows = slices * channels
    lists = (hit_tile, hit_table, hit_column, hit_count, position)
    list_places = (SMEM,) * 5

    def exchange(array):
        return lax.all_to_all(array, "view", split_axis=0, concat_axis=0)

    def neighbour(array, offset, periodic):
        pairs = []
        for source in range(count):
            target = source - offset
            if periodic:
                target %= count
            if 0 <= target < count:
                pairs.append((source, target))
        return lax.ppermute(array, "view", pairs)

    volume_flat = volume.reshape(channels, slices * rows_tile * cells)
    (rays,) = call(
        functools.partial(bins_kernel, slices, bins),
        (bin_energy, basis_table, volume_flat, footprint_table),
        (SMEM, VMEM, VMEM, VMEM),
        [shape_of((count, tables, height, UW), BF16)],
        [VMEM],
    )
    rays = exchange(rays)
    state = dual_state.reshape(channels, slices * detector)
    measured = sinogram.reshape(bins, slices * detector)
    own_a = jnp.concatenate([state, measured, jnp.zeros_like(measured)], axis=0)
    around_a = [neighbour(own_a, d, True) if d else own_a for d in (-2, -1, 0, 1, 2)]
    own_v = jnp.concatenate(
        [volume_flat, cot_volume.reshape(channels, slices * rows_tile * cells)], axis=0
    )
    around_v = [neighbour(own_v, d, False) if d else own_v for d in (-1, 0, 1)]
    own_c = cot_dual.reshape(channels, slices * detector)
    around_c = [neighbour(own_c, d, True) if d else own_c for d in (-2, -1, 0, 1, 2)]

    wide = shape_of((rows, 9 * rows), BF16)
    narrow = shape_of((height, 9 * rows), BF16)
    extra_dual = dual_inner.shape[2] - channels
    extra_primal = primal_inner.shape[2] - channels
    turned = [
        jnp.transpose(w, (0, 2, 1)) for w in (dual_inner, dual_outer, primal_inner, primal_outer)
    ]
    prepared = call(
        functools.partial(prep_kernel, slices, bins),
        (dual_inner, dual_outer, primal_inner, primal_outer, *turned, *lists),
        (VMEM,) * 8 + list_places,
        [
            wide,
            shape_of((rows, 9 * slices * extra_dual), BF16),
            wide,
            wide,
            wide,
            narrow,
            wide,
            shape_of((rows, 9 * slices * extra_primal), BF16),
            wide,
            wide,
            wide,
            narrow,
            shape_of((3, blocks), jnp.int32),
            shape_of((3,), jnp.int32),
        ],
        [VMEM] * 12 + [SMEM] * 2,
    )
    d1s, d1e, d2, d2t, d1t, d1x, p1s, p1e, p2, p2t, p1t, p1x, codes, found = prepared
    biases = jnp.stack(
        [dual_inner_bias, dual_outer_bias, primal_inner_bias, primal_outer_bias], axis=1
    )

    block = 3 * rows
    signal, new_dual, hidden, slope, extras = call(
        functools.partial(dual_forward_kernel, slices, bins),
        (rays, *lists, *around_a, d1s, d1e, d2, biases),
        (VMEM,) + list_places + (VMEM,) * 9,
        [
            shape_of((count, height, detector), BF16),
            shape_of((channels, slices * detector), BF16),
            shape_of((3 * rows, detector), BF16),
            shape_of((3 * rows, detector), F32),
            shape_of((3 * 2 * height, detector), BF16),
        ],
        [VMEM] * 5,
        [
            VMEM((5 * columns, height, UW), F32),
            VMEM((5 * block, detector), BF16),
            VMEM((3 * block, detector), BF16),
        ],
    )
    signal = exchange(signal)
    total_rows = 3 * rows_tile
    rays, new_volume, state_grad, grad_inner, grad_outer, grad_extra = call(
        functools.partial(primal_kernel, slices, bins, rows_tile),
        (signal, codes, found, position, *around_v, footprint_table)
        + (p1s, p1e, p2, p2t, p1t, p1x, biases),
        (VMEM, SMEM, SMEM, SMEM) + (VMEM,) * 11,
        [
            shape_of((count, tables, height, UW), BF16),
            shape_of(volume_flat.shape, BF16),
            shape_of(volume_flat.shape, F32),
            shape_of((3 * channels, 9 * channels), F32),
            shape_of((3 * channels, 9 * channels), F32),
            shape_of((rows, 9 * height), F32),
        ],
        [VMEM] * 6,
        [VMEM((3 * tables, height, UW), F32)] + [VMEM((total_rows * block, cells), BF16)] * 4,
    )
    rays = exchange(rays)
    state_tiles = 3 * channels // 8 * pl.cdiv(18 * channels, TILE)
    tiles = 2 * state_tiles
    tiles += rows // 8 * pl.cdiv(9 * slices * extra_dual, TILE)
    tiles += rows // 8 * pl.cdiv(9 * slices * extra_primal, TILE)
    per = pl.cdiv(tiles, count)
    signal, dual_grad, payload = call(
        functools.partial(dual_backward_kernel, slices, bins),
        (rays, *lists, *around_c, *around_a[1:4], hidden, slope, extras, d2t, d1t, d1x)
        + (grad_inner, grad_outer, grad_extra),
        (VMEM,) + list_places + (VMEM,) * 17,
        [
            shape_of((count, height, detector), BF16),
            shape_of((channels, slices * detector), BF16),
            shape_of((count, 8, per * TILE), BF16),
        ],
        [VMEM] * 3,
        [
            VMEM((5 * columns, height, UW), F32),
            VMEM((5 * block, detector), BF16),
            VMEM((3 * block, detector), BF16),
        ],
    )
    signal = exchange(signal)
    payload = exchange(payload)
    (payload,) = call(
        sum_kernel, (payload,), (VMEM,), [shape_of((count, 8, per * TILE), BF16)], [VMEM]
    )
    payload = exchange(payload)
    (volume_grad,) = call(
        functools.partial(volume_grad_kernel, slices, bins),
        (signal, codes, found, bin_energy, basis_table, footprint_table, state_grad),
        (VMEM, SMEM, SMEM, SMEM, VMEM, VMEM, VMEM),
        [shape_of(volume_flat.shape, BF16)],
        [VMEM],
        [VMEM((tables, height, UW), F32)],
    )
    gradients = call(
        functools.partial(unpack_kernel, slices),
        (payload,),
        (VMEM,),
        [shape_of(w.shape, F32) for w in (primal_inner, primal_outer, dual_inner, dual_outer)],
        [VMEM] * 4,
    )
    return (
        new_volume.reshape(volume.shape),
        new_dual.reshape(dual_state.shape),
        volume_grad.reshape(volume.shape),
        dual_grad.reshape(dual_state.shape),
        *gradients,
    )


def solution(mesh):
    split = P(None, "parts", "view", None)
    in_specs = (split,) * 5 + (P(),) * 15
    out_specs = (split,) * 4 + (P("parts", None, None),) * 4
    return jax.shard_map(shards, mesh=mesh, in_specs=in_specs, out_specs=out_specs, check_vma=False)
```

```python
import functools

import jax
import jax.numpy as jnp
from jax import lax
from jax.experimental import pallas as pl
from jax.experimental.pallas import tpu as pltpu
from jax.sharding import PartitionSpec as P


UW = 128
TILE = 128
F32 = jnp.float32
BF16 = jnp.bfloat16
VMEM = pltpu.VMEM
SMEM = pltpu.SMEM


class Late:
    def __init__(self, ref, copy):
        self.ref, self.copy, self.shape = ref, copy, ref.shape

    def ready(self):
        if self.copy is not None:
            self.copy.wait()
            self.copy = None
        return self.ref

    def __getitem__(self, index):
        return self.ready()[index]


class Out:
    def __init__(self, ref, copy):
        self.ref, self.copy, self.shape, self.left = ref, copy, ref.shape, False

    def __getitem__(self, index):
        return self.ref[index]

    def __setitem__(self, index, value):
        self.ref[index] = value

    def flush(self):
        if not self.left:
            self.copy.start()
            self.left = True


class Wider:
    def __init__(self, far, sem):
        self.far, self.sem, self.copy = far, sem, None

    def flush_from(self, out):
        self.copy = pltpu.make_async_copy(out.ref, self.far.at[0 : out.shape[0]], self.sem)
        self.copy.start()


class Choice:
    def __init__(self, even, yes, no):
        self.even, self.yes, self.no, self.shape = even, yes, no, yes.shape

    def __getitem__(self, index):
        yes, no = self.yes[index], self.no[index]
        return jnp.where(self.even, yes.astype(F32), no.astype(F32)).astype(yes.dtype)


HERE = "vmem"
WIDER = "wider"
PASS = "pass"
LISTS = "smem"
FAR = "hbm"


def call(kernel, operands, places, out_shapes, out_places, scratch=(), limit=67_000_000, alias=None):
    total_in, total_out = len(operands), len(out_shapes)
    buffers = []
    for place, array in zip(list(places) + list(out_places), list(operands) + list(out_shapes)):
        if place not in (HERE, PASS, WIDER):
            kind = SMEM if place == LISTS else VMEM
            dims = array.shape
            if isinstance(place, tuple):
                dims = (place[1] - place[0],) + tuple(dims[1:])
            buffers.append(kind(dims, array.dtype))

    def body(*refs):
        given = refs[: total_in + total_out]
        own = refs[total_in + total_out :]
        local, sems, rest = own[: len(buffers)], own[len(buffers)], own[len(buffers) + 1 :]
        seen = []
        used = 0
        for index, place in enumerate(list(places) + list(out_places)):
            if place in (HERE, PASS):
                seen.append(given[index])
                continue
            if place == WIDER:
                seen.append(Wider(given[index], sems.at[len(buffers)]))
                continue
            near = local[used]
            far = given[index]
            if isinstance(place, tuple):
                far = far.at[place[0] : place[1]]
            if index < total_in:
                copy = pltpu.make_async_copy(far, near, sems.at[used])
                copy.start()
                seen.append(Late(near, copy))
            else:
                seen.append(Out(near, pltpu.make_async_copy(near, far, sems.at[used])))
            used += 1
        kernel(*seen, *rest)
        for item in seen[:total_in]:
            if isinstance(item, Late):
                item.ready()
        for item in seen[total_in:]:
            if isinstance(item, Out):
                item.flush()
        for item in seen[total_in:]:
            if isinstance(item, (Out, Wider)):
                item.copy.wait()

    def spec(place):
        return pl.BlockSpec(memory_space=VMEM if place == HERE else pltpu.HBM)

    return pl.pallas_call(
        body,
        out_shape=out_shapes,
        in_specs=[spec(place) for place in places],
        out_specs=[spec(place) for place in out_places],
        scratch_shapes=buffers + [pltpu.SemaphoreType.DMA((len(buffers) + 1,))] + list(scratch),
        compiler_params=pltpu.CompilerParams(vmem_limit_bytes=limit),
        cost_estimate=pl.CostEstimate(flops=10**8, bytes_accessed=10**6, transcendentals=0),
        input_output_aliases=alias or {},
    )(*operands)


def shape_of(dims, kind):
    return jax.ShapeDtypeStruct(dims, kind)


def dot(left, right):
    return jnp.dot(left, right, preferred_element_type=F32)


def dot_nt(left, right):
    return lax.dot_general(left, right, (((1,), (1,)), ((), ())), preferred_element_type=F32)


def shifted(wide):
    lanes = wide.shape[1]
    lane = lax.broadcasted_iota(jnp.int32, wide.shape, 1)
    low = jnp.where(lane == 0, 0.0, pltpu.roll(wide, 1, 1))
    high = jnp.where(lane == lanes - 1, 0.0, pltpu.roll(wide, lanes - 1, 1))
    return low, wide, high


def put_columns(column_ref, row, plane, slices):
    channels = plane.shape[0] // slices
    block = 3 * plane.shape[0]
    for tap, moved in enumerate(shifted(plane.astype(F32))):
        moved = moved.astype(BF16)
        for z in range(slices):
            start = row * block + (z * 3 + tap) * channels
            column_ref[start : start + channels, :] = moved[z * channels : (z + 1) * channels]


def window(column_ref, row, block):
    return column_ref[(row - 1) * block : (row + 2) * block, :]


def sigmoid(values):
    return 1.0 / (1.0 + jnp.exp(-values))


def spread_lists(gradient, slices, taps_z=3):
    channels = gradient.shape[0] // slices
    parts = []
    for z_in in range(slices):
        rows = []
        for i in range(taps_z):
            z_out = z_in - i + 1
            if 0 <= z_out < slices:
                rows.append(gradient[z_out * channels : (z_out + 1) * channels])
            else:
                rows.append(jnp.zeros((channels, gradient.shape[1]), BF16))
        parts.append(jnp.concatenate(rows, axis=0))
    return parts


def state_wgrad(gradient, column_ref, row, slices):
    channels = gradient.shape[0] // slices
    parts = spread_lists(gradient, slices)
    block = 3 * channels * slices
    pieces = []
    for j in range(3):
        total = None
        for z in range(slices):
            start = (row + j - 1) * block + z * 3 * channels
            term = dot_nt(parts[z], column_ref[start : start + 3 * channels, :])
            total = term if total is None else total + term
        pieces.append(total)
    return pieces


def tap_of(i, j, l):
    return (i * 3 + j) * 3 + l


def forward_weight(weight_ref, slices, low, high, lane_major):
    rows = []
    for z in range(slices):
        pieces = []
        for j in range(3):
            pairs = [(zi, l) for zi in range(slices) for l in range(3)]
            if lane_major:
                pairs = [(zi, l) for l in range(3) for zi in range(slices)]
            for zi, l in pairs:
                i = zi - z + 1
                if 0 <= i < 3:
                    pieces.append(weight_ref[tap_of(i, j, l)].astype(F32)[:, low:high])
                else:
                    pieces.append(jnp.zeros((weight_ref.shape[1], high - low), F32))
        rows.append(jnp.concatenate(pieces, axis=1))
    return jnp.concatenate(rows, axis=0).astype(BF16)


def adjoint_weight(weight_ref, slices, low, high, first=0, last=None, lane_major=False):
    last = weight_ref.shape[1] if last is None else last
    rows = []
    for j in range(3):
        pairs = [(z, l) for z in range(slices) for l in range(3)]
        if lane_major:
            pairs = [(z, l) for l in range(3) for z in range(slices)]
        for z, l in pairs:
            pieces = []
            for zi in range(slices):
                i = zi - z + 1
                if 0 <= i < 3:
                    tap = weight_ref[tap_of(i, 2 - j, 2 - l)].astype(F32)
                    pieces.append(tap[first:last, low:high])
                else:
                    pieces.append(jnp.zeros((last - first, high - low), F32))
            rows.append(jnp.concatenate(pieces, axis=1))
    return jnp.concatenate(rows, axis=0).T.astype(BF16)


def arrived(*refs):
    return [ref.ready() if isinstance(ref, Late) else ref for ref in refs]


def invert_lists(tile_ref, table_ref, column_ref, count_ref, code_ref, found_ref):
    tile_ref, table_ref, column_ref, count_ref = arrived(
        tile_ref, table_ref, column_ref, count_ref
    )
    blocks = tile_ref.shape[0]
    position = lax.axis_index("view")
    for slot in range(3):
        found_ref[slot] = 0

    def each_block(b, carry):
        def each_entry(k, inner):
            slot = tile_ref[b, k] - position + 1

            @pl.when((slot >= 0) & (slot < 3))
            def _():
                at = found_ref[slot]
                code_ref[slot, at] = (b * 16 + table_ref[b, k]) * 16 + column_ref[b, k]
                found_ref[slot] = at + 1

            return inner

        return lax.fori_loop(0, count_ref[b], each_entry, carry)

    lax.fori_loop(0, blocks, each_block, 0)


def mixing_of(energy_ref, basis_ref, bins):
    (energy_ref,) = arrived(energy_ref)
    energies = basis_ref.shape[0]
    row = lax.broadcasted_iota(jnp.int32, (bins, energies), 0)
    col = lax.broadcasted_iota(jnp.int32, (bins, energies), 1)
    onehot = jnp.zeros((bins, energies), F32)
    for n in range(bins):
        onehot = jnp.where((row == n) & (col == energy_ref[n]), 1.0, onehot)
    return dot(onehot.astype(BF16), basis_ref[...])


def send_rays(images, footprint_ref, send_ref):
    for table in range(footprint_ref.shape[0]):
        rays = dot(images, footprint_ref[table]).astype(BF16)
        for target in range(send_ref.shape[0]):
            send_ref[target, table] = rays


def pack_kernel(
    volume_ref, cot_volume_ref, dual_ref, cot_dual_ref, sino_ref, pack_ref, near_ref
):
    channels, slices, rows_tile, _ = volume_ref.shape
    bins = sino_ref.shape[0]
    rows = slices * channels
    head = head_rows(rows, slices * bins)
    sino_rows = []
    for z in range(slices):
        at = z * channels
        pack_ref[at : at + channels, :] = dual_ref[:, z, :]
        at = head + z * channels
        pack_ref[at : at + channels, :] = cot_dual_ref[:, z, :]
        sino_rows.append(sino_ref[:, z, :].astype(F32))
    sino_rows.append(jnp.zeros((head - rows - slices * bins, sino_ref.shape[2]), F32))
    pack_ref[rows:head, :] = jnp.concatenate(sino_rows, axis=0).astype(BF16)
    at = head + rows
    for source in (volume_ref, cot_volume_ref):
        for r in range(rows_tile):
            for z in range(slices):
                pack_ref[at : at + channels, :] = source[:, z, r, :]
                at += channels
    near_ref.flush_from(pack_ref)


def head_rows(rows, height):
    return rows + pl.cdiv(height, 16) * 16


def bins_kernel(
    slices,
    bins,
    rows_tile,
    energy_ref,
    basis_ref,
    volume_ref,
    footprint_ref,
    beside_ref,
    near_in,
    send_ref,
    near_ref,
    sem,
):
    del near_in
    first = near_ref.shape[0] - beside_ref.shape[0]
    copy = pltpu.make_async_copy(
        beside_ref.ready(), near_ref.at[first : near_ref.shape[0]], sem.at[0]
    )
    copy.start()
    channels = basis_ref.shape[1]
    mixing = mixing_of(energy_ref, basis_ref, bins).astype(BF16)
    images = []
    for z in range(slices):
        cells = []
        for r in range(rows_tile):
            at = (r * slices + z) * channels
            cells.append(dot(mixing, volume_ref[at : at + channels, :]))
        images.append(jnp.concatenate(cells, axis=1))
    send_rays(jnp.concatenate(images, axis=0).astype(BF16), footprint_ref, send_ref)
    copy.wait()


def weights_kernel(
    slices,
    tile_ref,
    table_ref,
    column_ref,
    count_ref,
    di,
    do,
    d1s,
    d1e,
    d2,
    code_ref,
    found_ref,
):
    channels = do.shape[1]
    invert_lists(tile_ref, table_ref, column_ref, count_ref, code_ref, found_ref)
    d1s[...] = forward_weight(di, slices, 0, channels, False)
    d1e[...] = forward_weight(di, slices, channels, di.shape[2], True)
    d2[...] = forward_weight(do, slices, 0, channels, False)


def ray_windows(rays_ref, tile_ref, table_ref, column_ref, count_ref, sums_ref, views):
    rays_ref, tile_ref, table_ref, column_ref, count_ref = arrived(
        rays_ref, tile_ref, table_ref, column_ref, count_ref
    )
    blocks = tile_ref.shape[0]
    columns = sums_ref.shape[0] // len(views)
    sums_ref[...] = jnp.zeros_like(sums_ref)
    for place, offset in enumerate(views):
        view = lax.rem(lax.axis_index("view") + offset + blocks, blocks)

        def each_entry(k, carry):
            at = place * columns + column_ref[view, k]
            sums_ref[at] += rays_ref[tile_ref[view, k], table_ref[view, k]].astype(F32)
            return carry

        lax.fori_loop(0, count_ref[view], each_entry, 0)
    return [
        jnp.concatenate([sums_ref[place * columns + c] for c in range(columns)], axis=1)
        for place in range(len(views))
    ]


def extra_rows(projected, sino, slices, bins):
    rows = []
    for z in range(slices):
        rows.append(projected[z * bins : (z + 1) * bins])
        rows.append(sino[z * bins : (z + 1) * bins])
    return jnp.concatenate(rows, axis=0)


def extra_columns(pieces):
    return jnp.concatenate([piece for triple in pieces for piece in triple], axis=0).astype(BF16)


def column_bias(bias_ref, which, slices):
    return jnp.concatenate([bias_ref[:, which : which + 1]] * slices, axis=0)


def five_views(own, beside, across, two, over):
    even = lax.rem(lax.axis_index("view"), 2) == 0
    return (
        Choice(even, two, over),
        Choice(even, across, beside),
        own,
        Choice(even, beside, across),
        Choice(even, over, two),
    )


def three_views(own, beside, across):
    even = lax.rem(lax.axis_index("view"), 2) == 0
    return Choice(even, across, beside), own, Choice(even, beside, across)


class Valid:
    def __init__(self, valid, source):
        self.valid, self.source, self.shape = valid, source, source.shape

    def __getitem__(self, index):
        values = self.source[index]
        return jnp.where(self.valid, values.astype(F32), 0.0).astype(values.dtype)


def three_tiles(blocks, own, beside, across):
    even = lax.rem(lax.axis_index("view"), 2) == 0
    return (
        Valid(lax.axis_index("view") > 0, Choice(even, across, beside)),
        own,
        Valid(lax.axis_index("view") < blocks - 1, Choice(even, beside, across)),
    )


def dual_forward_kernel(
    slices,
    bins,
    tile_ref,
    table_ref,
    column_ref,
    count_ref,
    a0,
    a1,
    a2,
    a3,
    a4,
    w1s,
    rays_ref,
    w1e,
    w2,
    bias_ref,
    send_ref,
    slope_ref,
    hidden_ref,
    extra_ref,
    new_ref,
    sums_ref,
    columns_ref,
    hidden_columns,
):
    around = five_views(a0, a1, a2, a3, a4)
    channels = new_ref.shape[0]
    rows = channels * slices
    height = slices * bins
    bias_inner = column_bias(bias_ref, 0, slices)
    bias_outer = column_bias(bias_ref, 1, slices)
    for row in range(5):
        put_columns(columns_ref, row, around[row][0:rows, :], slices)
    projected = ray_windows(
        rays_ref, tile_ref, table_ref, column_ref, count_ref, sums_ref, (-2, -1, 0, 1, 2)
    )
    pieces = []
    for row in range(5):
        extra = extra_rows(
            projected[row].astype(BF16).astype(F32),
            around[row][rows : rows + height, :].astype(F32),
            slices,
            bins,
        )
        if 1 <= row <= 3:
            extra_ref[(row - 1) * extra.shape[0] : row * extra.shape[0], :] = extra.astype(BF16)
        pieces.append(shifted(extra))
    for row in range(3):
        at = row * rows
        pre = dot(w1s[...], window(columns_ref, row + 1, 3 * rows))
        pre = pre + dot(w1e[...], extra_columns(pieces[row : row + 3])) + bias_inner
        gate = sigmoid(pre)
        hidden = (pre * gate).astype(BF16)
        hidden_ref[at : at + rows, :] = hidden
        slope_ref[at : at + rows, :] = gate * (1.0 + pre * (1.0 - gate))
        put_columns(hidden_columns, row, hidden, slices)
    update = dot(w2[...], hidden_columns[...]) + bias_outer
    fresh = (around[2][0:rows, :].astype(F32) + update).astype(BF16)
    out = []
    for z in range(slices):
        plane = fresh[z * channels : (z + 1) * channels]
        new_ref[:, z, :] = plane
        out.append(plane.astype(F32)[:bins])
    out = jnp.concatenate(out, axis=0).astype(BF16)
    for target in range(send_ref.shape[0]):
        send_ref[target] = out
    send_ref.flush()


def gather_signals(
    signal_ref, code_ref, found_ref, slots, footprint_ref, sums_ref, chosen=False
):
    signal_ref, code_ref, found_ref = arrived(signal_ref, code_ref, found_ref)
    tables = footprint_ref.shape[0]
    sums_ref[...] = jnp.zeros_like(sums_ref)
    for place, slot in enumerate(slots):

        def each_hit(k, carry):
            code = code_ref[slot, k]
            at = place * tables + lax.rem(lax.div(code, 16), 16)
            lane = 0
            if not chosen:
                lane = pl.multiple_of(lax.rem(code, 16) * UW, UW)
            sums_ref[at] += signal_ref[lax.div(code, 256), :, pl.ds(lane, UW)].astype(F32)
            return carry

        lax.fori_loop(0, found_ref[slot], each_hit, 0)
    total = None
    for table in range(tables):
        grouped = jnp.concatenate(
            [sums_ref[place * tables + table] for place in range(len(slots))], axis=0
        )
        high = grouped.astype(BF16).astype(F32)
        both = jnp.concatenate([high, grouped - high], axis=0).astype(BF16)
        term = dot_nt(both, footprint_ref[table])
        total = term if total is None else total + term
    half = total.shape[0] // 2
    return total[:half] + total[half:]


def fold_lanes(array):
    full = array.shape[1] // TILE * TILE
    rest = array.shape[1] - full
    if rest == 0:
        return [array]
    copies = TILE // rest
    while array.shape[0] % (8 * copies):
        copies -= 1
    rows = array.shape[0] // copies
    side = [array[c * rows : (c + 1) * rows, full:] for c in range(copies)]
    side = jnp.concatenate(side, axis=1) if copies > 1 else side[0]
    return ([array[:, :full]] if full else []) + [side]


def fold_shapes(rows, width):
    full = width // TILE * TILE
    rest = width - full
    if rest == 0:
        return [(rows, width)], 1
    copies = TILE // rest
    while rows % (8 * copies):
        copies -= 1
    return ([(rows, full)] if full else []) + [(rows // copies, rest * copies)], copies


def tile_count(rows, width):
    shapes, _ = fold_shapes(rows, width)
    return sum(r // 8 * pl.cdiv(w, TILE) for r, w in shapes)


def put_payload(payload_ref, per, first, array):
    flat = first
    for part in fold_lanes(array):
        width = part.shape[1]
        for group in range(part.shape[0] // 8):
            for tile in range(pl.cdiv(width, TILE)):
                last = min(width, (tile + 1) * TILE)
                lane = (flat % per) * TILE
                payload_ref[flat // per, :, lane : lane + last - tile * TILE] = part[
                    group * 8 : group * 8 + 8, tile * TILE : last
                ].astype(BF16)
                flat += 1
    return flat


def take_payload(payload_ref, per, first, rows, width):
    flat = first
    shapes, copies = fold_shapes(rows, width)
    parts = []
    for part_rows, part_width in shapes:
        groups = []
        for _ in range(part_rows // 8):
            tiles = []
            for _ in range(pl.cdiv(part_width, TILE)):
                lane = (flat % per) * TILE
                tiles.append(payload_ref[flat // per, :, lane : lane + TILE].astype(F32))
                flat += 1
            groups.append(jnp.concatenate(tiles, axis=1) if len(tiles) > 1 else tiles[0])
        parts.append(jnp.concatenate(groups, axis=0))
    rest = width % TILE
    if rest:
        side = parts.pop()
        parts.append(
            jnp.concatenate([side[:, c * rest : (c + 1) * rest] for c in range(copies)], axis=0)
        )
    return (jnp.concatenate(parts, axis=1) if len(parts) > 1 else parts[0]), flat


def row_plane(tiles, row, which, rows, rows_tile):
    ref, r = tiles[row // rows_tile], row % rows_tile
    at = (which * rows_tile + r) * rows
    return ref[at : at + rows, :]


def primal_state_kernel(
    slices,
    rows_tile,
    blocks,
    v0,
    v1,
    v2,
    inner_ref,
    outer_ref,
    bias_ref,
    pre_ref,
    hidden_grad_ref,
    w1e,
    w1x,
    w2,
    w1t,
    columns_ref,
    cot_columns,
):
    tiles = three_tiles(blocks, v0, v1, v2)
    channels = outer_ref.shape[1]
    rows = channels * slices
    bins = inner_ref.shape[2] - channels
    w1s = forward_weight(inner_ref, slices, 0, channels, False)
    w2t = adjoint_weight(outer_ref, slices, 0, channels)
    w1e[...] = forward_weight(inner_ref, slices, channels, inner_ref.shape[2], True)
    w1x[...] = adjoint_weight(inner_ref, slices, channels, channels + bins)
    w2[...] = forward_weight(outer_ref, slices, 0, channels, False)
    w1t[...] = adjoint_weight(inner_ref, slices, 0, channels)
    bias = column_bias(bias_ref, 2, slices)
    first = rows_tile - 2
    for row in range(rows_tile + 4):
        at = first + row
        put_columns(columns_ref, row, row_plane(tiles, at, 0, rows, rows_tile), slices)
        put_columns(cot_columns, row, row_plane(tiles, at, 1, rows, rows_tile), slices)
    for row in range(rows_tile + 2):
        pre = dot(w1s, window(columns_ref, row + 1, 3 * rows)) + bias
        pre_ref[row * rows : (row + 1) * rows, :] = pre
        gradient = dot(w2t, window(cot_columns, row + 1, 3 * rows))
        hidden_grad_ref[row * rows : (row + 1) * rows, :] = gradient


def primal_kernel(
    slices,
    bins,
    rows_tile,
    signal_ref,
    code_ref,
    found_ref,
    footprint_ref,
    pre_ref,
    hidden_grad_ref,
    w1e,
    w1x,
    send_ref,
    hidden_ref,
    gradient_ref,
    extra_ref,
    sums_ref,
    grad_columns,
):
    blocks = send_ref.shape[0]
    lanes = pre_ref.shape[1]
    rows = w1e.shape[0]
    position = lax.axis_index("view")
    height = slices * bins
    back = gather_signals(signal_ref, code_ref, found_ref, (0, 1, 2), footprint_ref, sums_ref)
    back = back.astype(BF16).astype(F32)
    pieces = []
    for row in range(rows_tile + 4):
        at = row + rows_tile - 2
        tile, r = at // rows_tile, at % rows_tile
        extra = back[tile * height : (tile + 1) * height, r * lanes : (r + 1) * lanes]
        extra_ref[row * height : (row + 1) * height, :] = extra
        pieces.append(shifted(extra))
    for row in range(rows_tile + 2):
        at = row * rows
        pre = pre_ref[at : at + rows, :] + dot(w1e[...], extra_columns(pieces[row : row + 3]))
        gate = sigmoid(pre)
        hidden = pre * gate
        gradient = hidden_grad_ref[at : at + rows, :] * (gate * (1.0 + pre * (1.0 - gate)))
        if row == 0:
            hidden = jnp.where(position > 0, hidden, 0.0)
            gradient = jnp.where(position > 0, gradient, 0.0)
        if row == rows_tile + 1:
            hidden = jnp.where(position < blocks - 1, hidden, 0.0)
            gradient = jnp.where(position < blocks - 1, gradient, 0.0)
        gradient = gradient.astype(BF16)
        hidden_ref[at : at + rows, :] = hidden.astype(BF16)
        gradient_ref[at : at + rows, :] = gradient
        put_columns(grad_columns, row, gradient, slices)
    parts = []
    for row in range(rows_tile):
        parts.append(dot(w1x[...], window(grad_columns, row + 1, 3 * rows)))
    send_rays(jnp.concatenate(parts, axis=1).astype(BF16), footprint_ref, send_ref)


def primal_rest_kernel(
    slices,
    rows_tile,
    blocks,
    hidden_ref,
    gradient_ref,
    v0,
    v1,
    v2,
    extra_ref,
    w2,
    w1t,
    bias_ref,
    new_ref,
    state_ref,
    payload_ref,
    columns_ref,
    hidden_columns,
    grad_columns,
    ready_ref,
    sem,
):
    tiles = three_tiles(blocks, v0, v1, v2)
    channels = new_ref.shape[0]
    rows = channels * slices
    height = extra_ref.shape[0] // (rows_tile + 4)
    bias = column_bias(bias_ref, 3, slices)
    for row in range(rows_tile + 2):
        at = row * rows
        put_columns(hidden_columns, row, hidden_ref[at : at + rows, :], slices)
        put_columns(grad_columns, row, gradient_ref[at : at + rows, :], slices)
        plane = row_plane(tiles, rows_tile - 1 + row, 0, rows, rows_tile)
        put_columns(columns_ref, row, plane, slices)
    pieces = [
        shifted(extra_ref[row * height : (row + 1) * height, :])
        for row in range(1, rows_tile + 3)
    ]
    inner = None
    outer = None
    extra_total = None
    for r in range(rows_tile):
        at = (r + 1) * rows
        cot = row_plane(tiles, rows_tile + r, 1, rows, rows_tile)
        own = row_plane(tiles, rows_tile + r, 0, rows, rows_tile)
        gradient = gradient_ref[at : at + rows, :]
        state = dot(w1t[...], window(grad_columns, r + 1, 3 * rows)) + cot.astype(F32)
        update = dot(w2[...], window(hidden_columns, r + 1, 3 * rows)) + bias
        fresh = (own.astype(F32) + update).astype(BF16)
        state_ref[r * rows : (r + 1) * rows, :] = state
        for z in range(slices):
            new_ref[:, z, r, :] = fresh[z * channels : (z + 1) * channels]
        term = state_wgrad(gradient, columns_ref, r + 1, slices)
        inner = term if inner is None else [a + b for a, b in zip(inner, term)]
        term = state_wgrad(cot, hidden_columns, r + 1, slices)
        outer = term if outer is None else [a + b for a, b in zip(outer, term)]
        term = dot_nt(gradient, extra_columns(pieces[r : r + 3]))
        extra_total = term if extra_total is None else extra_total + term
    per = ready_ref.shape[2] // TILE
    flat = put_payload(ready_ref, per, 0, jnp.concatenate(inner + outer, axis=1))
    put_payload(ready_ref, per, flat, extra_total)
    copy = pltpu.make_async_copy(ready_ref, payload_ref.at[:, :, 0 : per * TILE], sem.at[0])
    copy.start()
    copy.wait()


def dual_cot_kernel(
    slices,
    bins,
    c0,
    c1,
    c2,
    c3,
    c4,
    inner_ref,
    outer_ref,
    part_ref,
    w2x,
    w1t,
    w1x,
    columns_ref,
):
    around = five_views(c0, c1, c2, c3, c4)
    rows = c0.shape[0]
    channels = rows // slices
    w2t = adjoint_weight(outer_ref, slices, 0, channels)
    w2x[...] = adjoint_weight(outer_ref, slices, 0, channels, 0, bins, True)
    w1t[...] = adjoint_weight(inner_ref, slices, 0, channels)
    w1x[...] = adjoint_weight(inner_ref, slices, channels, channels + bins)
    for row in range(5):
        plane = around[row][0:rows, :].astype(F32)
        channel = lax.broadcasted_iota(jnp.int32, plane.shape, 0)
        plane = jnp.where(lax.rem(channel, channels) < bins, 0.0, plane)
        put_columns(columns_ref, row, plane, slices)
    for row in range(3):
        at = row * rows
        part_ref[at : at + rows, :] = dot(w2t, window(columns_ref, row + 1, 3 * rows))


def dual_backward_kernel(
    slices,
    bins,
    per,
    tile_ref,
    table_ref,
    column_ref,
    count_ref,
    c0,
    c1,
    c2,
    c3,
    c4,
    rays_ref,
    a0,
    a1,
    a2,
    hidden_ref,
    w2x,
    part_ref,
    slope_ref,
    w1x,
    w1t,
    extra_ref,
    payload_in,
    grad_ref,
    payload_ref,
    sums_ref,
    grad_columns,
    state_columns,
    hidden_columns,
    windows_ref,
    ready_ref,
    sem,
):
    del payload_in
    around = five_views(c0, c1, c2, c3, c4)
    states = three_views(a0, a1, a2)
    channels = grad_ref.shape[0]
    rows = channels * slices
    toward = ray_windows(
        rays_ref, tile_ref, table_ref, column_ref, count_ref, sums_ref, (-2, -1, 0, 1, 2)
    )
    for row in range(3):
        put_columns(state_columns, row, states[row][0:rows, :], slices)
        put_columns(hidden_columns, row, hidden_ref[row * rows : (row + 1) * rows, :], slices)
    pieces = []
    own_head = None
    for row in range(5):
        head = jnp.concatenate(
            [
                around[row][z * channels : z * channels + 2 * bins, :].astype(F32)[:bins]
                for z in range(slices)
            ],
            axis=0,
        )
        head = head + toward[row]
        if row == 2:
            own_head = head
        pieces.append(shifted(head.astype(BF16).astype(F32)))
    spread = []
    lanes = own_head.shape[1]
    for z in range(slices):
        spread.append(own_head[z * bins : (z + 1) * bins])
        spread.append(around[2][z * channels : (z + 1) * channels, :].astype(F32)[bins:])
    own_total = jnp.concatenate(spread, axis=0)
    own_cot = own_total.astype(BF16)
    own_gradient = None
    for row in range(3):
        at = row * rows
        gradient = part_ref[at : at + rows, :] + dot(w2x[...], extra_columns(pieces[row : row + 3]))
        gradient = (gradient * slope_ref[at : at + rows, :]).astype(BF16)
        put_columns(grad_columns, row, gradient, slices)
        if row == 1:
            own_gradient = gradient
    out = dot(w1x[...], grad_columns[...]).astype(BF16)
    for column in range(lanes // UW):
        windows_ref[column] = out[:, column * UW : (column + 1) * UW]
    start = per * TILE
    ready_ref[:, :, start : start + UW] = jnp.zeros(
        (ready_ref.shape[0], ready_ref.shape[1], UW), BF16
    )
    view = lax.axis_index("view")
    tile_ref, column_ref, count_ref = arrived(tile_ref, column_ref, count_ref)

    def each_entry(k, carry):
        ready_ref[tile_ref[view, k], :, start : start + UW] = windows_ref[column_ref[view, k]]
        return carry

    lax.fori_loop(0, count_ref[view], each_entry, 0)
    inner = jnp.concatenate(state_wgrad(own_gradient, state_columns, 1, slices), axis=1)
    outer = jnp.concatenate(state_wgrad(own_cot, hidden_columns, 1, slices), axis=1)
    height = extra_ref.shape[0] // 3
    pieces = [
        shifted(extra_ref[row * height : (row + 1) * height, :].astype(F32)) for row in range(3)
    ]
    extra = dot_nt(own_gradient, extra_columns(pieces))
    flat = put_payload(ready_ref, per, 0, jnp.concatenate([inner, outer], axis=1))
    put_payload(ready_ref, per, flat, extra)
    total = payload_ref.shape[2]
    copy = pltpu.make_async_copy(
        ready_ref, payload_ref.at[:, :, total - ready_ref.shape[2] : total], sem.at[0]
    )
    copy.start()
    state = (dot(w1t[...], grad_columns[...]) + own_total).astype(BF16)
    for z in range(slices):
        grad_ref[:, z, :] = state[z * channels : (z + 1) * channels]
    grad_ref.flush()
    copy.wait()


def sum_kernel(payload_ref, send_ref, rays_ref):
    width = send_ref.shape[2]
    total = payload_ref[0, :, 0:width].astype(F32)
    for source in range(1, payload_ref.shape[0]):
        total = total + payload_ref[source, :, 0:width].astype(F32)
    total = total.astype(BF16)
    for target in range(send_ref.shape[0]):
        send_ref[target] = total
    rays_ref[...] = payload_ref[:, :, width:]


def volume_grad_kernel(
    slices,
    bins,
    signal_ref,
    code_ref,
    found_ref,
    energy_ref,
    basis_ref,
    footprint_ref,
    state_ref,
    out_ref,
    sums_ref,
):
    back = gather_signals(
        signal_ref, code_ref, found_ref, (1,), footprint_ref, sums_ref, chosen=True
    )
    mixing = mixing_of(energy_ref, basis_ref, bins)
    channels, _, rows_tile, lanes = out_ref.shape
    for z in range(slices):
        part = back[z * bins : (z + 1) * bins]
        high = part.astype(BF16).astype(F32)
        low = part - high
        spread = lax.dot_general(
            jnp.concatenate([mixing, mixing], axis=0).astype(BF16),
            jnp.concatenate([high, low], axis=0).astype(BF16),
            (((0,), (0,)), ((), ())),
            preferred_element_type=F32,
        )
        for r in range(rows_tile):
            at = (r * slices + z) * channels
            total = state_ref[at : at + channels, :] + spread[:, r * lanes : (r + 1) * lanes]
            out_ref[:, z, r, :] = total.astype(BF16)


class Region:
    def __init__(self, ref, first):
        self.ref, self.first = ref, first

    def __getitem__(self, index):
        chunk, rows, lanes = index
        return self.ref[chunk, rows, lanes.start + self.first : lanes.stop + self.first]


def unpack_kernel(
    slices, per_primal, per_dual, payload_ref, primal_inner, primal_outer, dual_inner, dual_outer
):
    channels = dual_outer.shape[1]
    for inner_ref, outer_ref, per, first in (
        (primal_inner, primal_outer, per_primal, 0),
        (dual_inner, dual_outer, per_dual, per_primal * TILE),
    ):
        region = Region(payload_ref, first)
        flat = 0
        extra_count = inner_ref.shape[2] - channels
        state, flat = take_payload(region, per, flat, 3 * channels, 18 * channels)
        extra, flat = take_payload(region, per, flat, slices * channels, 9 * slices * extra_count)
        for i in range(3):
            for j in range(3):
                for l in range(3):
                    tap = (i * 3 + j) * 3 + l
                    lane = (j * 3 + l) * channels
                    rows = state[i * channels : (i + 1) * channels]
                    more = None
                    for z in range(slices):
                        z_in = z + i - 1
                        if 0 <= z_in < slices:
                            at = ((j * 3 + l) * slices + z_in) * extra_count
                            term = extra[z * channels : (z + 1) * channels, at : at + extra_count]
                            more = term if more is None else more + term
                    inner_ref[tap] = jnp.concatenate(
                        [rows[:, lane : lane + channels], more], axis=1
                    )
                    lane = lane + 9 * channels
                    outer_ref[tap] = rows[:, lane : lane + channels]


def whole(
    volume,
    dual_state,
    sinogram,
    cot_volume,
    cot_dual,
    basis_table,
    bin_energy,
    footprint_table,
    hit_tile,
    hit_table,
    hit_column,
    hit_count,
    primal_inner,
    primal_inner_bias,
    primal_outer,
    primal_outer_bias,
    dual_inner,
    dual_inner_bias,
    dual_outer,
    dual_outer_bias,
):
    count = lax.axis_size("view")
    channels, slices, rows_tile, cells = volume.shape
    bins = sinogram.shape[0]
    detector = dual_state.shape[3]
    columns = detector // UW
    tables = footprint_table.shape[0]
    blocks, _ = hit_tile.shape
    height = slices * bins
    rows = slices * channels
    block = 3 * rows
    lists = (hit_tile, hit_table, hit_column, hit_count)
    list_places = (LISTS,) * 4

    def exchange(array):
        return lax.all_to_all(array, "view", split_axis=0, concat_axis=0)

    def swap(array):
        return lax.ppermute(array, "view", [(k, k ^ 1) for k in range(count)])

    def cross(array):
        pairs = []
        for k in range(1, count, 2):
            pairs += [(k, (k + 1) % count), ((k + 1) % count, k)]
        return lax.ppermute(array, "view", pairs)

    head = head_rows(rows, height)
    near_rows = head + rows
    all_rows = near_rows + 2 * rows_tile * rows
    dual_flat = (channels, slices, detector)
    pack, near = call(
        pack_kernel,
        (volume, cot_volume, dual_state.reshape(dual_flat), cot_dual.reshape(dual_flat))
        + (sinogram.reshape(bins, slices, detector),),
        (FAR,) * 5,
        [shape_of((all_rows, detector), BF16), shape_of((all_rows + near_rows, detector), BF16)],
        [FAR, WIDER],
    )
    beside = swap(pack)
    rays, near = call(
        functools.partial(bins_kernel, slices, bins, rows_tile),
        (bin_energy, basis_table, pack, footprint_table, beside, near),
        (LISTS, FAR, (near_rows, near_rows + rows_tile * rows), FAR, (0, near_rows), PASS),
        [shape_of((count, tables, height, UW), BF16), shape_of(near.shape, BF16)],
        [FAR, PASS],
        [pltpu.SemaphoreType.DMA((1,))],
        alias={5: 1},
    )
    rays = exchange(rays)
    far = cross(near)
    over = swap(far)
    views = (pack, beside, far, far, over)

    def ranges(first, last):
        return (
            (first, last),
            (first, last),
            (first, last),
            (all_rows + first, all_rows + last),
            (first, last),
        )

    state_views = ranges(0, head)
    cot_views = ranges(head, head + rows)
    tiles_all = ((near_rows, all_rows),) * 3
    biases = jnp.stack(
        [dual_inner_bias, dual_outer_bias, primal_inner_bias, primal_outer_bias], axis=1
    )
    wide = shape_of((rows, 9 * rows), BF16)
    narrow = shape_of((height, 9 * rows), BF16)
    extra_dual = dual_inner.shape[2] - channels
    extra_primal = primal_inner.shape[2] - channels
    d1s, d1e, d2, codes, found = call(
        functools.partial(weights_kernel, slices),
        (*lists, dual_inner, dual_outer),
        list_places + (FAR,) * 2,
        [
            wide,
            shape_of((rows, 9 * slices * extra_dual), BF16),
            wide,
            shape_of((3, blocks), jnp.int32),
            shape_of((3,), jnp.int32),
        ],
        [FAR] * 3 + [LISTS] * 2,
    )
    signal, slope, hidden, extras, new_dual = call(
        functools.partial(dual_forward_kernel, slices, bins),
        (*lists, *views, d1s, rays, d1e, d2, biases),
        list_places + state_views + (FAR,) * 5,
        [
            shape_of((count, height, detector), BF16),
            shape_of((3 * rows, detector), F32),
            shape_of((3 * rows, detector), BF16),
            shape_of((3 * 2 * height, detector), BF16),
            shape_of(dual_flat, BF16),
        ],
        [FAR] * 5,
        [
            VMEM((5 * columns, height, UW), F32),
            VMEM((5 * block, detector), BF16),
            VMEM((3 * block, detector), BF16),
        ],
    )
    signal = exchange(signal)
    kept = (rows_tile + 2) * rows
    per_primal = tile_count(3 * channels, 18 * channels)
    per_dual = pl.cdiv(per_primal + tile_count(rows, 9 * slices * extra_dual), count)
    per_primal = pl.cdiv(per_primal + tile_count(rows, 9 * slices * extra_primal), count)
    width = (per_primal + per_dual) * TILE
    primal_pre, hidden_grad, p1e, p1x, p2, p1t = call(
        functools.partial(primal_state_kernel, slices, rows_tile, blocks),
        (pack, beside, far, primal_inner, primal_outer, biases),
        tiles_all + (FAR,) * 3,
        [shape_of((kept, cells), F32)] * 2
        + [shape_of((rows, 9 * slices * extra_primal), BF16), narrow, wide, wide],
        [FAR] * 6,
        [VMEM(((rows_tile + 4) * block, cells), BF16)] * 2,
    )
    rays, primal_hidden, pre_grad, back = call(
        functools.partial(primal_kernel, slices, bins, rows_tile),
        (signal, codes, found, footprint_table, primal_pre, hidden_grad, p1e, p1x),
        (FAR, LISTS, LISTS) + (FAR,) * 5,
        [
            shape_of((count, tables, height, UW), BF16),
            shape_of((kept, cells), BF16),
            shape_of((kept, cells), BF16),
            shape_of(((rows_tile + 4) * height, cells), F32),
        ],
        [FAR] * 4,
        [
            VMEM((3 * tables, height, UW), F32),
            VMEM(((rows_tile + 2) * block, cells), BF16),
        ],
    )
    rays = exchange(rays)
    new_volume, state_grad, payload = call(
        functools.partial(primal_rest_kernel, slices, rows_tile, blocks),
        (primal_hidden, pre_grad, pack, beside, far, back, p2, p1t, biases),
        (FAR, FAR) + tiles_all + (FAR,) * 4,
        [
            shape_of(volume.shape, BF16),
            shape_of((rows_tile * rows, cells), F32),
            shape_of((count, 8, (per_primal + per_dual) * TILE + UW), BF16),
        ],
        [FAR, FAR, PASS],
        [VMEM(((rows_tile + 2) * block, cells), BF16)] * 3
        + [VMEM((count, 8, per_primal * TILE), BF16), pltpu.SemaphoreType.DMA((1,))],
    )
    dual_part, d2x, d1t, d1x = call(
        functools.partial(dual_cot_kernel, slices, bins),
        (*views, dual_inner, dual_outer),
        cot_views + (FAR, FAR),
        [
            shape_of((3 * rows, detector), F32),
            shape_of((rows, 9 * height), BF16),
            wide,
            narrow,
        ],
        [FAR] * 4,
        [VMEM((5 * block, detector), BF16)],
    )
    dual_grad, payload = call(
        functools.partial(dual_backward_kernel, slices, bins, per_dual),
        (*lists, *views, rays, pack, beside, far, hidden, d2x, dual_part, slope, d1x, d1t, extras)
        + (payload,),
        list_places + cot_views + (FAR,) + ((0, rows),) * 3 + (FAR,) * 7 + (PASS,),
        [shape_of(dual_flat, BF16), shape_of(payload.shape, BF16)],
        [FAR, PASS],
        [
            VMEM((5 * columns, height, UW), F32),
            VMEM((3 * block, detector), BF16),
            VMEM((3 * block, detector), BF16),
            VMEM((3 * block, detector), BF16),
            VMEM((columns, height, UW), BF16),
            VMEM((count, 8, per_dual * TILE + UW), BF16),
            pltpu.SemaphoreType.DMA((1,)),
        ],
        alias={20: 1},
    )
    payload = exchange(payload)
    payload, signal = call(
        sum_kernel,
        (payload,),
        (HERE,),
        [shape_of((count, 8, width), BF16), shape_of((count, height, UW), BF16)],
        [HERE, FAR],
        limit=2 * 1024 * 1024,
    )
    payload = exchange(payload)
    (volume_grad,) = call(
        functools.partial(volume_grad_kernel, slices, bins),
        (signal, codes, found, bin_energy, basis_table, footprint_table, state_grad),
        (FAR, LISTS, LISTS, LISTS, FAR, FAR, FAR),
        [shape_of(volume.shape, BF16)],
        [FAR],
        [VMEM((tables, height, UW), F32)],
    )
    gradients = call(
        functools.partial(unpack_kernel, slices, per_primal, per_dual),
        (payload,),
        (HERE,),
        [shape_of(w.shape, F32) for w in (primal_inner, primal_outer, dual_inner, dual_outer)],
        [HERE] * 4,
        limit=8 * 1024 * 1024,
    )
    return (
        new_volume,
        new_dual.reshape(dual_state.shape),
        volume_grad,
        dual_grad.reshape(dual_state.shape),
        *gradients,
    )


def solution(mesh):
    split = P(None, "parts", "view", None)
    in_specs = (split,) * 5 + (P(),) * 15
    out_specs = (split,) * 4 + (P("parts", None, None),) * 4
    return jax.shard_map(whole, mesh=mesh, in_specs=in_specs, out_specs=out_specs, check_vma=False)
```

```python
import functools

import jax
import jax.numpy as jnp
from jax import lax
from jax.experimental import pallas as pl
from jax.experimental.pallas import tpu as pltpu
from jax.sharding import PartitionSpec as P


UW = 128
TILE = 128
F32 = jnp.float32
BF16 = jnp.bfloat16
VMEM = pltpu.VMEM
SMEM = pltpu.SMEM


class Late:
    def __init__(self, ref, copy):
        self.ref, self.copy, self.shape = ref, copy, ref.shape

    def ready(self):
        if self.copy is not None:
            self.copy.wait()
            self.copy = None
        return self.ref

    def __getitem__(self, index):
        return self.ready()[index]


class Out:
    def __init__(self, ref, copy):
        self.ref, self.copy, self.shape, self.left = ref, copy, ref.shape, False

    def __getitem__(self, index):
        return self.ref[index]

    def __setitem__(self, index, value):
        self.ref[index] = value

    def flush(self):
        if not self.left:
            self.copy.start()
            self.left = True


class Wider:
    def __init__(self, far, sem):
        self.far, self.sem, self.copy = far, sem, None

    def flush_from(self, out):
        self.copy = pltpu.make_async_copy(out.ref, self.far.at[0 : out.shape[0]], self.sem)
        self.copy.start()


class Choice:
    def __init__(self, even, yes, no):
        self.even, self.yes, self.no, self.shape = even, yes, no, yes.shape

    def __getitem__(self, index):
        yes, no = self.yes[index], self.no[index]
        return jnp.where(self.even, yes.astype(F32), no.astype(F32)).astype(yes.dtype)


HERE = "vmem"
WIDER = "wider"
PASS = "pass"
LISTS = "smem"
FAR = "hbm"


def call(kernel, operands, places, out_shapes, out_places, scratch=(), limit=67_000_000, alias=None):
    total_in, total_out = len(operands), len(out_shapes)
    buffers = []
    for place, array in zip(list(places) + list(out_places), list(operands) + list(out_shapes)):
        if place not in (HERE, PASS, WIDER):
            kind = SMEM if place == LISTS else VMEM
            dims = array.shape
            if isinstance(place, tuple):
                dims = (place[1] - place[0],) + tuple(dims[1:])
            buffers.append(kind(dims, array.dtype))

    def body(*refs):
        given = refs[: total_in + total_out]
        own = refs[total_in + total_out :]
        local, sems, rest = own[: len(buffers)], own[len(buffers)], own[len(buffers) + 1 :]
        seen = []
        used = 0
        for index, place in enumerate(list(places) + list(out_places)):
            if place in (HERE, PASS):
                seen.append(given[index])
                continue
            if place == WIDER:
                seen.append(Wider(given[index], sems.at[len(buffers)]))
                continue
            near = local[used]
            far = given[index]
            if isinstance(place, tuple):
                far = far.at[place[0] : place[1]]
            if index < total_in:
                copy = pltpu.make_async_copy(far, near, sems.at[used])
                copy.start()
                seen.append(Late(near, copy))
            else:
                seen.append(Out(near, pltpu.make_async_copy(near, far, sems.at[used])))
            used += 1
        kernel(*seen, *rest)
        for item in seen[:total_in]:
            if isinstance(item, Late):
                item.ready()
        for item in seen[total_in:]:
            if isinstance(item, Out):
                item.flush()
        for item in seen[total_in:]:
            if isinstance(item, (Out, Wider)):
                item.copy.wait()

    def spec(place):
        return pl.BlockSpec(memory_space=VMEM if place == HERE else pltpu.HBM)

    return pl.pallas_call(
        body,
        out_shape=out_shapes,
        in_specs=[spec(place) for place in places],
        out_specs=[spec(place) for place in out_places],
        scratch_shapes=buffers + [pltpu.SemaphoreType.DMA((len(buffers) + 1,))] + list(scratch),
        compiler_params=pltpu.CompilerParams(vmem_limit_bytes=limit),
        cost_estimate=pl.CostEstimate(flops=10**8, bytes_accessed=10**6, transcendentals=0),
        input_output_aliases=alias or {},
    )(*operands)


def shape_of(dims, kind):
    return jax.ShapeDtypeStruct(dims, kind)


def dot(left, right):
    return jnp.dot(left, right, preferred_element_type=F32)


def dot_nt(left, right):
    return lax.dot_general(left, right, (((1,), (1,)), ((), ())), preferred_element_type=F32)


def shifted(wide):
    lanes = wide.shape[1]
    lane = lax.broadcasted_iota(jnp.int32, wide.shape, 1)
    low = jnp.where(lane == 0, 0.0, pltpu.roll(wide, 1, 1))
    high = jnp.where(lane == lanes - 1, 0.0, pltpu.roll(wide, lanes - 1, 1))
    return low, wide, high


def put_columns(column_ref, row, plane, slices):
    channels = plane.shape[0] // slices
    block = 3 * plane.shape[0]
    for tap, moved in enumerate(shifted(plane.astype(F32))):
        moved = moved.astype(BF16)
        for z in range(slices):
            start = row * block + (z * 3 + tap) * channels
            column_ref[start : start + channels, :] = moved[z * channels : (z + 1) * channels]


def window(column_ref, row, block):
    return column_ref[(row - 1) * block : (row + 2) * block, :]


def sigmoid(values):
    return 1.0 / (1.0 + jnp.exp(-values))


def spread_lists(gradient, slices, taps_z=3):
    channels = gradient.shape[0] // slices
    parts = []
    for z_in in range(slices):
        rows = []
        for i in range(taps_z):
            z_out = z_in - i + 1
            if 0 <= z_out < slices:
                rows.append(gradient[z_out * channels : (z_out + 1) * channels])
            else:
                rows.append(jnp.zeros((channels, gradient.shape[1]), BF16))
        parts.append(jnp.concatenate(rows, axis=0))
    return parts


def state_wgrad(gradient, column_ref, row, slices):
    channels = gradient.shape[0] // slices
    parts = spread_lists(gradient, slices)
    block = 3 * channels * slices
    pieces = []
    for j in range(3):
        total = None
        for z in range(slices):
            start = (row + j - 1) * block + z * 3 * channels
            term = dot_nt(parts[z], column_ref[start : start + 3 * channels, :])
            total = term if total is None else total + term
        pieces.append(total)
    return pieces


def tap_of(i, j, l):
    return (i * 3 + j) * 3 + l


def forward_weight(weight_ref, slices, low, high, lane_major):
    rows = []
    for z in range(slices):
        pieces = []
        for j in range(3):
            pairs = [(zi, l) for zi in range(slices) for l in range(3)]
            if lane_major:
                pairs = [(zi, l) for l in range(3) for zi in range(slices)]
            for zi, l in pairs:
                i = zi - z + 1
                if 0 <= i < 3:
                    pieces.append(weight_ref[tap_of(i, j, l)].astype(F32)[:, low:high])
                else:
                    pieces.append(jnp.zeros((weight_ref.shape[1], high - low), F32))
        rows.append(jnp.concatenate(pieces, axis=1))
    return jnp.concatenate(rows, axis=0).astype(BF16)


def adjoint_weight(weight_ref, slices, low, high, first=0, last=None, lane_major=False):
    last = weight_ref.shape[1] if last is None else last
    rows = []
    for j in range(3):
        pairs = [(z, l) for z in range(slices) for l in range(3)]
        if lane_major:
            pairs = [(z, l) for l in range(3) for z in range(slices)]
        for z, l in pairs:
            pieces = []
            for zi in range(slices):
                i = zi - z + 1
                if 0 <= i < 3:
                    tap = weight_ref[tap_of(i, 2 - j, 2 - l)].astype(F32)
                    pieces.append(tap[first:last, low:high])
                else:
                    pieces.append(jnp.zeros((last - first, high - low), F32))
            rows.append(jnp.concatenate(pieces, axis=1))
    return jnp.concatenate(rows, axis=0).T.astype(BF16)


def arrived(*refs):
    return [ref.ready() if isinstance(ref, Late) else ref for ref in refs]


def as_column(values):
    count = values.shape[0]
    square = jnp.broadcast_to(values[None, :], (count, count))
    row = lax.broadcasted_iota(jnp.int32, square.shape, 0)
    col = lax.broadcasted_iota(jnp.int32, square.shape, 1)
    return jnp.sum(jnp.where(row == col, square, 0.0), axis=1, keepdims=True)


def invert_lists(tile_ref, table_ref, column_ref, count_ref, code_ref):
    tiles = tile_ref[...]
    live = lax.broadcasted_iota(jnp.int32, tiles.shape, 1).astype(F32) < as_column(
        count_ref[...].astype(F32)
    )
    codes = (table_ref[...] * 16 + column_ref[...] + 1).astype(F32)
    position = lax.axis_index("view")
    found = []
    for slot in range(3):
        hit = live & (tiles == position + slot - 1)
        found.append(jnp.sum(jnp.where(hit, codes, 0.0), axis=1, keepdims=True))
    code_ref[...] = (jnp.concatenate(found, axis=1) - 1.0).astype(jnp.int32)


def mixing_of(energy_ref, basis_ref, bins):
    (energy_ref,) = arrived(energy_ref)
    energies = basis_ref.shape[0]
    row = lax.broadcasted_iota(jnp.int32, (bins, energies), 0)
    col = lax.broadcasted_iota(jnp.int32, (bins, energies), 1)
    onehot = jnp.zeros((bins, energies), F32)
    for n in range(bins):
        onehot = jnp.where((row == n) & (col == energy_ref[n]), 1.0, onehot)
    return dot(onehot.astype(BF16), basis_ref[...])


def send_rays(images, footprint_ref, send_ref):
    for table in range(footprint_ref.shape[0]):
        rays = dot(images, footprint_ref[table]).astype(BF16)
        for target in range(send_ref.shape[0]):
            send_ref[target, table] = rays


def pack_kernel(
    volume_ref, cot_volume_ref, dual_ref, cot_dual_ref, sino_ref, pack_ref, cells_ref, near_ref
):
    channels, slices, rows_tile, _ = volume_ref.shape
    bins = sino_ref.shape[0]
    rows = slices * channels
    head = head_rows(rows, slices * bins)
    sino_rows = []
    for z in range(slices):
        at = z * channels
        pack_ref[at : at + channels, :] = dual_ref[:, z, :]
        at = head + z * channels
        pack_ref[at : at + channels, :] = cot_dual_ref[:, z, :]
        sino_rows.append(sino_ref[:, z, :].astype(F32))
    sino_rows.append(jnp.zeros((head - rows - slices * bins, sino_ref.shape[2]), F32))
    pack_ref[rows:head, :] = jnp.concatenate(sino_rows, axis=0).astype(BF16)
    near_ref.flush_from(pack_ref)
    pack_ref.flush()
    at = 0
    for source in (volume_ref, cot_volume_ref):
        for r in range(rows_tile):
            for z in range(slices):
                cells_ref[at : at + channels, :] = source[:, z, r, :]
                at += channels


def head_rows(rows, height):
    return rows + pl.cdiv(height, 16) * 16


def bins_kernel(
    slices,
    bins,
    rows_tile,
    energy_ref,
    basis_ref,
    volume_ref,
    footprint_ref,
    send_ref,
):
    channels = basis_ref.shape[1]
    mixing = mixing_of(energy_ref, basis_ref, bins).astype(BF16)
    images = []
    for z in range(slices):
        cells = []
        for r in range(rows_tile):
            at = (r * slices + z) * channels
            cells.append(dot(mixing, volume_ref[at : at + channels, :]))
        images.append(jnp.concatenate(cells, axis=1))
    send_rays(jnp.concatenate(images, axis=0).astype(BF16), footprint_ref, send_ref)


def join_kernel(beside_ref, near_in, near_ref, sem):
    del near_in
    first = near_ref.shape[0] - beside_ref.shape[0]
    copy = pltpu.make_async_copy(
        beside_ref.ready(), near_ref.at[first : near_ref.shape[0]], sem.at[0]
    )
    copy.start()
    copy.wait()


def weights_kernel(
    slices,
    tile_ref,
    table_ref,
    column_ref,
    count_ref,
    di,
    do,
    d1s,
    d1e,
    d2,
    code_ref,
):
    channels = do.shape[1]
    invert_lists(tile_ref, table_ref, column_ref, count_ref, code_ref)
    d1s[...] = forward_weight(di, slices, 0, channels, False)
    d1e[...] = forward_weight(di, slices, channels, di.shape[2], True)
    d2[...] = forward_weight(do, slices, 0, channels, False)


def ray_windows(rays_ref, tile_ref, table_ref, column_ref, count_ref, sums_ref, views):
    rays_ref, tile_ref, table_ref, column_ref, count_ref = arrived(
        rays_ref, tile_ref, table_ref, column_ref, count_ref
    )
    blocks = tile_ref.shape[0]
    columns = sums_ref.shape[0] // len(views)
    sums_ref[...] = jnp.zeros_like(sums_ref)
    for place, offset in enumerate(views):
        view = lax.rem(lax.axis_index("view") + offset + blocks, blocks)

        def each_entry(k, carry):
            at = place * columns + column_ref[view, k]
            sums_ref[at] += rays_ref[tile_ref[view, k], table_ref[view, k]].astype(F32)
            return carry

        lax.fori_loop(0, count_ref[view], each_entry, 0)
    return [
        jnp.concatenate([sums_ref[place * columns + c] for c in range(columns)], axis=1)
        for place in range(len(views))
    ]


def extra_rows(projected, sino, slices, bins):
    rows = []
    for z in range(slices):
        rows.append(projected[z * bins : (z + 1) * bins])
        rows.append(sino[z * bins : (z + 1) * bins])
    return jnp.concatenate(rows, axis=0)


def extra_columns(pieces):
    return jnp.concatenate([piece for triple in pieces for piece in triple], axis=0).astype(BF16)


def column_bias(bias_ref, slices):
    return jnp.concatenate([as_column(bias_ref[...])] * slices, axis=0)


def five_views(own, beside, across, two, over):
    even = lax.rem(lax.axis_index("view"), 2) == 0
    return (
        Choice(even, two, over),
        Choice(even, across, beside),
        own,
        Choice(even, beside, across),
        Choice(even, over, two),
    )


def three_views(own, beside, across):
    even = lax.rem(lax.axis_index("view"), 2) == 0
    return Choice(even, across, beside), own, Choice(even, beside, across)


class Valid:
    def __init__(self, valid, source):
        self.valid, self.source, self.shape = valid, source, source.shape

    def __getitem__(self, index):
        values = self.source[index]
        return jnp.where(self.valid, values.astype(F32), 0.0).astype(values.dtype)


def three_tiles(blocks, own, beside, across):
    even = lax.rem(lax.axis_index("view"), 2) == 0
    return (
        Valid(lax.axis_index("view") > 0, Choice(even, across, beside)),
        own,
        Valid(lax.axis_index("view") < blocks - 1, Choice(even, beside, across)),
    )


def dual_forward_kernel(
    slices,
    bins,
    tile_ref,
    table_ref,
    column_ref,
    count_ref,
    a0,
    a1,
    a2,
    a3,
    a4,
    w1s,
    rays_ref,
    w1e,
    w2,
    inner_bias,
    outer_bias,
    send_ref,
    slope_ref,
    hidden_ref,
    extra_ref,
    new_ref,
    sums_ref,
    columns_ref,
    hidden_columns,
):
    around = five_views(a0, a1, a2, a3, a4)
    channels = new_ref.shape[0]
    rows = channels * slices
    height = slices * bins
    bias_inner = column_bias(inner_bias, slices)
    bias_outer = column_bias(outer_bias, slices)
    for row in range(5):
        put_columns(columns_ref, row, around[row][0:rows, :], slices)
    projected = ray_windows(
        rays_ref, tile_ref, table_ref, column_ref, count_ref, sums_ref, (-2, -1, 0, 1, 2)
    )
    pieces = []
    for row in range(5):
        extra = extra_rows(
            projected[row].astype(BF16).astype(F32),
            around[row][rows : rows + height, :].astype(F32),
            slices,
            bins,
        )
        if 1 <= row <= 3:
            extra_ref[(row - 1) * extra.shape[0] : row * extra.shape[0], :] = extra.astype(BF16)
        pieces.append(shifted(extra))
    for row in range(3):
        at = row * rows
        pre = dot(w1s[...], window(columns_ref, row + 1, 3 * rows))
        pre = pre + dot(w1e[...], extra_columns(pieces[row : row + 3])) + bias_inner
        gate = sigmoid(pre)
        hidden = (pre * gate).astype(BF16)
        hidden_ref[at : at + rows, :] = hidden
        slope_ref[at : at + rows, :] = gate * (1.0 + pre * (1.0 - gate))
        put_columns(hidden_columns, row, hidden, slices)
    update = dot(w2[...], hidden_columns[...]) + bias_outer
    fresh = (around[2][0:rows, :].astype(F32) + update).astype(BF16)
    out = []
    for z in range(slices):
        plane = fresh[z * channels : (z + 1) * channels]
        new_ref[:, z, :] = plane
        out.append(plane.astype(F32)[:bins])
    out = jnp.concatenate(out, axis=0).astype(BF16)
    for target in range(send_ref.shape[0]):
        send_ref[target] = out
    send_ref.flush()


def gather_signals(signal_ref, code_ref, slots, footprint_ref, sums_ref, chosen=False):
    signal_ref, code_ref = arrived(signal_ref, code_ref)
    tables = footprint_ref.shape[0]
    spare = len(slots) * tables
    sums_ref[...] = jnp.zeros_like(sums_ref)

    def each_block(b, carry):
        for place, slot in enumerate(slots):
            code = code_ref[b, slot]
            live = code >= 0
            code = jnp.maximum(code, 0)
            at = jnp.where(live, place * tables + lax.div(code, 16), spare)
            lane = 0
            if not chosen:
                lane = pl.multiple_of(lax.rem(code, 16) * UW, UW)
            sums_ref[at] += signal_ref[b, :, pl.ds(lane, UW)].astype(F32)
        return carry

    lax.fori_loop(0, signal_ref.shape[0], each_block, 0)
    total = None
    for table in range(tables):
        grouped = jnp.concatenate(
            [sums_ref[place * tables + table] for place in range(len(slots))], axis=0
        )
        high = grouped.astype(BF16).astype(F32)
        both = jnp.concatenate([high, grouped - high], axis=0).astype(BF16)
        term = dot_nt(both, footprint_ref[table])
        total = term if total is None else total + term
    half = total.shape[0] // 2
    return total[:half] + total[half:]


def fold_lanes(array):
    full = array.shape[1] // TILE * TILE
    rest = array.shape[1] - full
    if rest == 0:
        return [array]
    copies = TILE // rest
    while array.shape[0] % (8 * copies):
        copies -= 1
    rows = array.shape[0] // copies
    side = [array[c * rows : (c + 1) * rows, full:] for c in range(copies)]
    side = jnp.concatenate(side, axis=1) if copies > 1 else side[0]
    return ([array[:, :full]] if full else []) + [side]


def fold_shapes(rows, width):
    full = width // TILE * TILE
    rest = width - full
    if rest == 0:
        return [(rows, width)], 1
    copies = TILE // rest
    while rows % (8 * copies):
        copies -= 1
    return ([(rows, full)] if full else []) + [(rows // copies, rest * copies)], copies


def tile_count(rows, width):
    shapes, _ = fold_shapes(rows, width)
    return sum(r // 8 * pl.cdiv(w, TILE) for r, w in shapes)


def put_payload(payload_ref, per, first, array):
    flat = first
    for part in fold_lanes(array):
        width = part.shape[1]
        for group in range(part.shape[0] // 8):
            for tile in range(pl.cdiv(width, TILE)):
                last = min(width, (tile + 1) * TILE)
                lane = (flat % per) * TILE
                payload_ref[flat // per, :, lane : lane + last - tile * TILE] = part[
                    group * 8 : group * 8 + 8, tile * TILE : last
                ].astype(BF16)
                flat += 1
    return flat


def take_payload(payload_ref, per, first, rows, width):
    flat = first
    shapes, copies = fold_shapes(rows, width)
    parts = []
    for part_rows, part_width in shapes:
        groups = []
        for _ in range(part_rows // 8):
            tiles = []
            for _ in range(pl.cdiv(part_width, TILE)):
                lane = (flat % per) * TILE
                tiles.append(payload_ref[flat // per, :, lane : lane + TILE].astype(F32))
                flat += 1
            groups.append(jnp.concatenate(tiles, axis=1) if len(tiles) > 1 else tiles[0])
        parts.append(jnp.concatenate(groups, axis=0))
    rest = width % TILE
    if rest:
        side = parts.pop()
        parts.append(
            jnp.concatenate([side[:, c * rest : (c + 1) * rest] for c in range(copies)], axis=0)
        )
    return (jnp.concatenate(parts, axis=1) if len(parts) > 1 else parts[0]), flat


def row_plane(tiles, row, which, rows, rows_tile):
    ref, r = tiles[row // rows_tile], row % rows_tile
    at = (which * rows_tile + r) * rows
    return ref[at : at + rows, :]


def primal_state_kernel(
    slices,
    rows_tile,
    blocks,
    v0,
    v1,
    v2,
    inner_ref,
    outer_ref,
    bias_ref,
    pre_ref,
    hidden_grad_ref,
    w1e,
    w1x,
    w2,
    w1t,
    columns_ref,
    cot_columns,
):
    tiles = three_tiles(blocks, v0, v1, v2)
    channels = outer_ref.shape[1]
    rows = channels * slices
    bins = inner_ref.shape[2] - channels
    w1s = forward_weight(inner_ref, slices, 0, channels, False)
    w2t = adjoint_weight(outer_ref, slices, 0, channels)
    w1e[...] = forward_weight(inner_ref, slices, channels, inner_ref.shape[2], True)
    w1x[...] = adjoint_weight(inner_ref, slices, channels, channels + bins)
    w2[...] = forward_weight(outer_ref, slices, 0, channels, False)
    w1t[...] = adjoint_weight(inner_ref, slices, 0, channels)
    bias = column_bias(bias_ref, slices)
    first = rows_tile - 2
    for row in range(rows_tile + 4):
        at = first + row
        put_columns(columns_ref, row, row_plane(tiles, at, 0, rows, rows_tile), slices)
        put_columns(cot_columns, row, row_plane(tiles, at, 1, rows, rows_tile), slices)
    for row in range(rows_tile + 2):
        pre = dot(w1s, window(columns_ref, row + 1, 3 * rows)) + bias
        pre_ref[row * rows : (row + 1) * rows, :] = pre
        gradient = dot(w2t, window(cot_columns, row + 1, 3 * rows))
        hidden_grad_ref[row * rows : (row + 1) * rows, :] = gradient


def primal_kernel(
    slices,
    bins,
    rows_tile,
    signal_ref,
    code_ref,
    footprint_ref,
    pre_ref,
    hidden_grad_ref,
    w1e,
    w1x,
    send_ref,
    hidden_ref,
    gradient_ref,
    extra_ref,
    sums_ref,
    grad_columns,
):
    blocks = send_ref.shape[0]
    lanes = pre_ref.shape[1]
    rows = w1e.shape[0]
    position = lax.axis_index("view")
    height = slices * bins
    back = gather_signals(signal_ref, code_ref, (0, 1, 2), footprint_ref, sums_ref)
    back = back.astype(BF16).astype(F32)
    pieces = []
    for row in range(rows_tile + 4):
        at = row + rows_tile - 2
        tile, r = at // rows_tile, at % rows_tile
        extra = back[tile * height : (tile + 1) * height, r * lanes : (r + 1) * lanes]
        extra_ref[row * height : (row + 1) * height, :] = extra
        pieces.append(shifted(extra))
    for row in range(rows_tile + 2):
        at = row * rows
        pre = pre_ref[at : at + rows, :] + dot(w1e[...], extra_columns(pieces[row : row + 3]))
        gate = sigmoid(pre)
        hidden = pre * gate
        gradient = hidden_grad_ref[at : at + rows, :] * (gate * (1.0 + pre * (1.0 - gate)))
        if row == 0:
            hidden = jnp.where(position > 0, hidden, 0.0)
            gradient = jnp.where(position > 0, gradient, 0.0)
        if row == rows_tile + 1:
            hidden = jnp.where(position < blocks - 1, hidden, 0.0)
            gradient = jnp.where(position < blocks - 1, gradient, 0.0)
        gradient = gradient.astype(BF16)
        hidden_ref[at : at + rows, :] = hidden.astype(BF16)
        gradient_ref[at : at + rows, :] = gradient
        put_columns(grad_columns, row, gradient, slices)
    parts = []
    for row in range(rows_tile):
        parts.append(dot(w1x[...], window(grad_columns, row + 1, 3 * rows)))
    send_rays(jnp.concatenate(parts, axis=1).astype(BF16), footprint_ref, send_ref)


def primal_rest_kernel(
    slices,
    rows_tile,
    blocks,
    hidden_ref,
    gradient_ref,
    v0,
    v1,
    v2,
    extra_ref,
    w2,
    w1t,
    bias_ref,
    new_ref,
    state_ref,
    payload_ref,
    columns_ref,
    hidden_columns,
    grad_columns,
    ready_ref,
    sem,
):
    tiles = three_tiles(blocks, v0, v1, v2)
    channels = new_ref.shape[0]
    rows = channels * slices
    height = extra_ref.shape[0] // (rows_tile + 4)
    bias = column_bias(bias_ref, slices)
    for row in range(rows_tile + 2):
        at = row * rows
        put_columns(hidden_columns, row, hidden_ref[at : at + rows, :], slices)
        put_columns(grad_columns, row, gradient_ref[at : at + rows, :], slices)
        plane = row_plane(tiles, rows_tile - 1 + row, 0, rows, rows_tile)
        put_columns(columns_ref, row, plane, slices)
    pieces = [
        shifted(extra_ref[row * height : (row + 1) * height, :])
        for row in range(1, rows_tile + 3)
    ]
    inner = None
    outer = None
    extra_total = None
    for r in range(rows_tile):
        at = (r + 1) * rows
        cot = row_plane(tiles, rows_tile + r, 1, rows, rows_tile)
        own = row_plane(tiles, rows_tile + r, 0, rows, rows_tile)
        gradient = gradient_ref[at : at + rows, :]
        state = dot(w1t[...], window(grad_columns, r + 1, 3 * rows)) + cot.astype(F32)
        update = dot(w2[...], window(hidden_columns, r + 1, 3 * rows)) + bias
        fresh = (own.astype(F32) + update).astype(BF16)
        state_ref[r * rows : (r + 1) * rows, :] = state
        for z in range(slices):
            new_ref[:, z, r, :] = fresh[z * channels : (z + 1) * channels]
        term = state_wgrad(gradient, columns_ref, r + 1, slices)
        inner = term if inner is None else [a + b for a, b in zip(inner, term)]
        term = state_wgrad(cot, hidden_columns, r + 1, slices)
        outer = term if outer is None else [a + b for a, b in zip(outer, term)]
        term = dot_nt(gradient, extra_columns(pieces[r : r + 3]))
        extra_total = term if extra_total is None else extra_total + term
    per = ready_ref.shape[2] // TILE
    flat = put_payload(ready_ref, per, 0, jnp.concatenate(inner + outer, axis=1))
    put_payload(ready_ref, per, flat, extra_total)
    copy = pltpu.make_async_copy(ready_ref, payload_ref.at[:, :, 0 : per * TILE], sem.at[0])
    copy.start()
    copy.wait()


def dual_cot_kernel(
    slices,
    bins,
    c0,
    c1,
    c2,
    c3,
    c4,
    inner_ref,
    outer_ref,
    part_ref,
    w2x,
    w1t,
    w1x,
    columns_ref,
):
    around = five_views(c0, c1, c2, c3, c4)
    rows = c0.shape[0]
    channels = rows // slices
    w2t = adjoint_weight(outer_ref, slices, 0, channels)
    w2x[...] = adjoint_weight(outer_ref, slices, 0, channels, 0, bins, True)
    w1t[...] = adjoint_weight(inner_ref, slices, 0, channels)
    w1x[...] = adjoint_weight(inner_ref, slices, channels, channels + bins)
    for row in range(5):
        plane = around[row][0:rows, :].astype(F32)
        channel = lax.broadcasted_iota(jnp.int32, plane.shape, 0)
        plane = jnp.where(lax.rem(channel, channels) < bins, 0.0, plane)
        put_columns(columns_ref, row, plane, slices)
    for row in range(3):
        at = row * rows
        part_ref[at : at + rows, :] = dot(w2t, window(columns_ref, row + 1, 3 * rows))


def dual_backward_kernel(
    slices,
    bins,
    per,
    tile_ref,
    table_ref,
    column_ref,
    count_ref,
    c0,
    c1,
    c2,
    c3,
    c4,
    rays_ref,
    a0,
    a1,
    a2,
    hidden_ref,
    w2x,
    part_ref,
    slope_ref,
    w1x,
    w1t,
    extra_ref,
    payload_in,
    grad_ref,
    payload_ref,
    sums_ref,
    grad_columns,
    state_columns,
    hidden_columns,
    windows_ref,
    ready_ref,
    sem,
):
    del payload_in
    around = five_views(c0, c1, c2, c3, c4)
    states = three_views(a0, a1, a2)
    channels = grad_ref.shape[0]
    rows = channels * slices
    toward = ray_windows(
        rays_ref, tile_ref, table_ref, column_ref, count_ref, sums_ref, (-2, -1, 0, 1, 2)
    )
    for row in range(3):
        put_columns(state_columns, row, states[row][0:rows, :], slices)
        put_columns(hidden_columns, row, hidden_ref[row * rows : (row + 1) * rows, :], slices)
    pieces = []
    own_head = None
    for row in range(5):
        head = jnp.concatenate(
            [
                around[row][z * channels : z * channels + 2 * bins, :].astype(F32)[:bins]
                for z in range(slices)
            ],
            axis=0,
        )
        head = head + toward[row]
        if row == 2:
            own_head = head
        pieces.append(shifted(head.astype(BF16).astype(F32)))
    spread = []
    lanes = own_head.shape[1]
    for z in range(slices):
        spread.append(own_head[z * bins : (z + 1) * bins])
        spread.append(around[2][z * channels : (z + 1) * channels, :].astype(F32)[bins:])
    own_total = jnp.concatenate(spread, axis=0)
    own_cot = own_total.astype(BF16)
    own_gradient = None
    for row in range(3):
        at = row * rows
        gradient = part_ref[at : at + rows, :] + dot(w2x[...], extra_columns(pieces[row : row + 3]))
        gradient = (gradient * slope_ref[at : at + rows, :]).astype(BF16)
        put_columns(grad_columns, row, gradient, slices)
        if row == 1:
            own_gradient = gradient
    out = dot(w1x[...], grad_columns[...]).astype(BF16)
    for column in range(lanes // UW):
        windows_ref[column] = out[:, column * UW : (column + 1) * UW]
    start = per * TILE
    ready_ref[:, :, start : start + UW] = jnp.zeros(
        (ready_ref.shape[0], ready_ref.shape[1], UW), BF16
    )
    view = lax.axis_index("view")
    tile_ref, column_ref, count_ref = arrived(tile_ref, column_ref, count_ref)

    def each_entry(k, carry):
        ready_ref[tile_ref[view, k], :, start : start + UW] = windows_ref[column_ref[view, k]]
        return carry

    lax.fori_loop(0, count_ref[view], each_entry, 0)
    inner = jnp.concatenate(state_wgrad(own_gradient, state_columns, 1, slices), axis=1)
    outer = jnp.concatenate(state_wgrad(own_cot, hidden_columns, 1, slices), axis=1)
    height = extra_ref.shape[0] // 3
    pieces = [
        shifted(extra_ref[row * height : (row + 1) * height, :].astype(F32)) for row in range(3)
    ]
    extra = dot_nt(own_gradient, extra_columns(pieces))
    flat = put_payload(ready_ref, per, 0, jnp.concatenate([inner, outer], axis=1))
    put_payload(ready_ref, per, flat, extra)
    total = payload_ref.shape[2]
    copy = pltpu.make_async_copy(
        ready_ref, payload_ref.at[:, :, total - ready_ref.shape[2] : total], sem.at[0]
    )
    copy.start()
    state = (dot(w1t[...], grad_columns[...]) + own_total).astype(BF16)
    for z in range(slices):
        grad_ref[:, z, :] = state[z * channels : (z + 1) * channels]
    grad_ref.flush()
    copy.wait()


def sum_kernel(payload_ref, send_ref, rays_ref):
    width = send_ref.shape[2]
    total = payload_ref[0, :, 0:width].astype(F32)
    for source in range(1, payload_ref.shape[0]):
        total = total + payload_ref[source, :, 0:width].astype(F32)
    total = total.astype(BF16)
    for target in range(send_ref.shape[0]):
        send_ref[target] = total
    rays_ref[...] = payload_ref[:, :, width:]


def volume_grad_kernel(
    slices,
    bins,
    signal_ref,
    code_ref,
    energy_ref,
    basis_ref,
    footprint_ref,
    state_ref,
    out_ref,
    sums_ref,
):
    back = gather_signals(
        signal_ref, code_ref, (1,), footprint_ref, sums_ref, chosen=True
    )
    mixing = mixing_of(energy_ref, basis_ref, bins)
    channels, _, rows_tile, lanes = out_ref.shape
    for z in range(slices):
        part = back[z * bins : (z + 1) * bins]
        high = part.astype(BF16).astype(F32)
        low = part - high
        spread = lax.dot_general(
            jnp.concatenate([mixing, mixing], axis=0).astype(BF16),
            jnp.concatenate([high, low], axis=0).astype(BF16),
            (((0,), (0,)), ((), ())),
            preferred_element_type=F32,
        )
        for r in range(rows_tile):
            at = (r * slices + z) * channels
            total = state_ref[at : at + channels, :] + spread[:, r * lanes : (r + 1) * lanes]
            out_ref[:, z, r, :] = total.astype(BF16)


class Region:
    def __init__(self, ref, first):
        self.ref, self.first = ref, first

    def __getitem__(self, index):
        chunk, rows, lanes = index
        return self.ref[chunk, rows, lanes.start + self.first : lanes.stop + self.first]


def unpack_kernel(
    slices, per_primal, per_dual, payload_ref, primal_inner, primal_outer, dual_inner, dual_outer
):
    channels = dual_outer.shape[1]
    for inner_ref, outer_ref, per, first in (
        (primal_inner, primal_outer, per_primal, 0),
        (dual_inner, dual_outer, per_dual, per_primal * TILE),
    ):
        region = Region(payload_ref, first)
        flat = 0
        extra_count = inner_ref.shape[2] - channels
        state, flat = take_payload(region, per, flat, 3 * channels, 18 * channels)
        extra, flat = take_payload(region, per, flat, slices * channels, 9 * slices * extra_count)
        for i in range(3):
            for j in range(3):
                for l in range(3):
                    tap = (i * 3 + j) * 3 + l
                    lane = (j * 3 + l) * channels
                    rows = state[i * channels : (i + 1) * channels]
                    more = None
                    for z in range(slices):
                        z_in = z + i - 1
                        if 0 <= z_in < slices:
                            at = ((j * 3 + l) * slices + z_in) * extra_count
                            term = extra[z * channels : (z + 1) * channels, at : at + extra_count]
                            more = term if more is None else more + term
                    inner_ref[tap] = jnp.concatenate(
                        [rows[:, lane : lane + channels], more], axis=1
                    )
                    lane = lane + 9 * channels
                    outer_ref[tap] = rows[:, lane : lane + channels]
        inner_ref.flush()
        outer_ref.flush()


def whole(
    volume,
    dual_state,
    sinogram,
    cot_volume,
    cot_dual,
    basis_table,
    bin_energy,
    footprint_table,
    hit_tile,
    hit_table,
    hit_column,
    hit_count,
    primal_inner,
    primal_inner_bias,
    primal_outer,
    primal_outer_bias,
    dual_inner,
    dual_inner_bias,
    dual_outer,
    dual_outer_bias,
):
    count = lax.axis_size("view")
    channels, slices, rows_tile, cells = volume.shape
    bins = sinogram.shape[0]
    detector = dual_state.shape[3]
    columns = detector // UW
    tables = footprint_table.shape[0]
    blocks, _ = hit_tile.shape
    height = slices * bins
    rows = slices * channels
    block = 3 * rows
    lists = (hit_tile, hit_table, hit_column, hit_count)
    list_places = (LISTS,) * 4

    def exchange(array):
        return lax.all_to_all(array, "view", split_axis=0, concat_axis=0)

    def swap(array):
        return lax.ppermute(array, "view", [(k, k ^ 1) for k in range(count)])

    def cross(array, periodic):
        pairs = []
        for k in range(1, count, 2):
            if periodic or k + 1 < count:
                pairs += [(k, (k + 1) % count), ((k + 1) % count, k)]
        return lax.ppermute(array, "view", pairs)

    head = head_rows(rows, height)
    near_rows = head + rows
    dual_flat = (channels, slices, detector)
    pack, tile, near = call(
        pack_kernel,
        (volume, cot_volume, dual_state.reshape(dual_flat), cot_dual.reshape(dual_flat))
        + (sinogram.reshape(bins, slices, detector),),
        (FAR,) * 5,
        [
            shape_of((near_rows, detector), BF16),
            shape_of((2 * rows_tile * rows, cells), BF16),
            shape_of((2 * near_rows, detector), BF16),
        ],
        [FAR, FAR, WIDER],
    )
    beside = swap(pack)
    (rays,) = call(
        functools.partial(bins_kernel, slices, bins, rows_tile),
        (bin_energy, basis_table, tile, footprint_table),
        (LISTS, FAR, (0, rows_tile * rows), FAR),
        [shape_of((count, tables, height, UW), BF16)],
        [FAR],
    )
    rays = exchange(rays)
    (near,) = call(
        join_kernel,
        (beside, near),
        (FAR, PASS),
        [shape_of(near.shape, BF16)],
        [PASS],
        [pltpu.SemaphoreType.DMA((1,))],
        alias={1: 0},
    )
    far = cross(near, True)
    tiles = (tile, swap(tile), cross(tile, False))
    over = swap(far)
    views = (pack, beside, far, far, over)

    def ranges(first, last):
        return (
            (first, last),
            (first, last),
            (first, last),
            (near_rows + first, near_rows + last),
            (first, last),
        )

    state_views = ranges(0, head)
    cot_views = ranges(head, head + rows)
    wide = shape_of((rows, 9 * rows), BF16)
    narrow = shape_of((height, 9 * rows), BF16)
    extra_dual = dual_inner.shape[2] - channels
    extra_primal = primal_inner.shape[2] - channels
    d1s, d1e, d2, codes = call(
        functools.partial(weights_kernel, slices),
        (*lists, dual_inner, dual_outer),
        (FAR,) * 6,
        [
            wide,
            shape_of((rows, 9 * slices * extra_dual), BF16),
            wide,
            shape_of((blocks, 3), jnp.int32),
        ],
        [FAR] * 4,
    )
    signal, slope, hidden, extras, new_dual = call(
        functools.partial(dual_forward_kernel, slices, bins),
        (*lists, *views, d1s, rays, d1e, d2, dual_inner_bias, dual_outer_bias),
        list_places + state_views + (FAR,) * 6,
        [
            shape_of((count, height, detector), BF16),
            shape_of((3 * rows, detector), F32),
            shape_of((3 * rows, detector), BF16),
            shape_of((3 * 2 * height, detector), BF16),
            shape_of(dual_flat, BF16),
        ],
        [FAR] * 5,
        [
            VMEM((5 * columns, height, UW), F32),
            VMEM((5 * block, detector), BF16),
            VMEM((3 * block, detector), BF16),
        ],
    )
    signal = exchange(signal)
    kept = (rows_tile + 2) * rows
    per_primal = tile_count(3 * channels, 18 * channels)
    per_dual = pl.cdiv(per_primal + tile_count(rows, 9 * slices * extra_dual), count)
    per_primal = pl.cdiv(per_primal + tile_count(rows, 9 * slices * extra_primal), count)
    width = (per_primal + per_dual) * TILE
    primal_pre, hidden_grad, p1e, p1x, p2, p1t = call(
        functools.partial(primal_state_kernel, slices, rows_tile, blocks),
        (*tiles, primal_inner, primal_outer, primal_inner_bias),
        (FAR,) * 6,
        [shape_of((kept, cells), F32)] * 2
        + [shape_of((rows, 9 * slices * extra_primal), BF16), narrow, wide, wide],
        [FAR] * 6,
        [VMEM(((rows_tile + 4) * block, cells), BF16)] * 2,
    )
    rays, primal_hidden, pre_grad, back = call(
        functools.partial(primal_kernel, slices, bins, rows_tile),
        (signal, codes, footprint_table, primal_pre, hidden_grad, p1e, p1x),
        (FAR, LISTS) + (FAR,) * 5,
        [
            shape_of((count, tables, height, UW), BF16),
            shape_of((kept, cells), BF16),
            shape_of((kept, cells), BF16),
            shape_of(((rows_tile + 4) * height, cells), F32),
        ],
        [FAR] * 4,
        [
            VMEM((3 * tables + 1, height, UW), F32),
            VMEM(((rows_tile + 2) * block, cells), BF16),
        ],
    )
    rays = exchange(rays)
    new_volume, state_grad, payload = call(
        functools.partial(primal_rest_kernel, slices, rows_tile, blocks),
        (primal_hidden, pre_grad, *tiles, back, p2, p1t, primal_outer_bias),
        (FAR,) * 9,
        [
            shape_of(volume.shape, BF16),
            shape_of((rows_tile * rows, cells), F32),
            shape_of((count, 8, (per_primal + per_dual) * TILE + UW), BF16),
        ],
        [FAR, FAR, PASS],
        [VMEM(((rows_tile + 2) * block, cells), BF16)] * 3
        + [VMEM((count, 8, per_primal * TILE), BF16), pltpu.SemaphoreType.DMA((1,))],
    )
    dual_part, d2x, d1t, d1x = call(
        functools.partial(dual_cot_kernel, slices, bins),
        (*views, dual_inner, dual_outer),
        cot_views + (FAR, FAR),
        [
            shape_of((3 * rows, detector), F32),
            shape_of((rows, 9 * height), BF16),
            wide,
            narrow,
        ],
        [FAR] * 4,
        [VMEM((5 * block, detector), BF16)],
    )
    dual_grad, payload = call(
        functools.partial(dual_backward_kernel, slices, bins, per_dual),
        (*lists, *views, rays, pack, beside, far, hidden, d2x, dual_part, slope, d1x, d1t, extras)
        + (payload,),
        list_places + cot_views + (FAR,) + ((0, rows),) * 3 + (FAR,) * 7 + (PASS,),
        [shape_of(dual_flat, BF16), shape_of(payload.shape, BF16)],
        [FAR, PASS],
        [
            VMEM((5 * columns, height, UW), F32),
            VMEM((3 * block, detector), BF16),
            VMEM((3 * block, detector), BF16),
            VMEM((3 * block, detector), BF16),
            VMEM((columns, height, UW), BF16),
            VMEM((count, 8, per_dual * TILE + UW), BF16),
            pltpu.SemaphoreType.DMA((1,)),
        ],
        alias={20: 1},
    )
    payload = exchange(payload)
    payload, signal = call(
        sum_kernel,
        (payload,),
        (HERE,),
        [shape_of((count, 8, width), BF16), shape_of((count, height, UW), BF16)],
        [HERE, HERE],
        limit=2 * 1024 * 1024,
    )
    payload = exchange(payload)
    (volume_grad,) = call(
        functools.partial(volume_grad_kernel, slices, bins),
        (signal, codes, bin_energy, basis_table, footprint_table, state_grad),
        (HERE, LISTS, LISTS, FAR, FAR, FAR),
        [shape_of(volume.shape, BF16)],
        [FAR],
        limit=4 * 1024 * 1024,
        scratch=[VMEM((tables + 1, height, UW), F32)],
    )
    gradients = call(
        functools.partial(unpack_kernel, slices, per_primal, per_dual),
        (payload,),
        (HERE,),
        [shape_of(w.shape, F32) for w in (primal_inner, primal_outer, dual_inner, dual_outer)],
        [FAR] * 4,
        limit=8 * 1024 * 1024,
    )
    return (
        new_volume,
        new_dual.reshape(dual_state.shape),
        volume_grad,
        dual_grad.reshape(dual_state.shape),
        *gradients,
    )


def solution(mesh):
    split = P(None, "parts", "view", None)
    in_specs = (split,) * 5 + (P(),) * 15
    out_specs = (split,) * 4 + (P("parts", None, None),) * 4
    return jax.shard_map(whole, mesh=mesh, in_specs=in_specs, out_specs=out_specs, check_vma=False)
```

```python
import functools

import jax
import jax.numpy as jnp
from jax import lax
from jax.experimental import pallas as pl
from jax.experimental.pallas import tpu as pltpu
from jax.sharding import PartitionSpec as P


UW = 128
TILE = 128
F32 = jnp.float32
BF16 = jnp.bfloat16
VMEM = pltpu.VMEM
SMEM = pltpu.SMEM


class Late:
    def __init__(self, ref, copy):
        self.ref, self.copy, self.shape = ref, copy, ref.shape

    def ready(self):
        if self.copy is not None:
            self.copy.wait()
            self.copy = None
        return self.ref

    def __getitem__(self, index):
        return self.ready()[index]


class Out:
    def __init__(self, ref, copy):
        self.ref, self.copy, self.shape, self.left = ref, copy, ref.shape, False

    def __getitem__(self, index):
        return self.ref[index]

    def __setitem__(self, index, value):
        self.ref[index] = value

    def flush(self):
        if not self.left:
            self.copy.start()
            self.left = True


class Wider:
    def __init__(self, far, sem):
        self.far, self.sem, self.copy = far, sem, None

    def flush_from(self, out):
        self.copy = pltpu.make_async_copy(out.ref, self.far.at[0 : out.shape[0]], self.sem)
        self.copy.start()


class Choice:
    def __init__(self, even, yes, no):
        self.even, self.yes, self.no, self.shape = even, yes, no, yes.shape

    def __getitem__(self, index):
        yes, no = self.yes[index], self.no[index]
        return jnp.where(self.even, yes.astype(F32), no.astype(F32)).astype(yes.dtype)


HERE = "vmem"
WIDER = "wider"
PASS = "pass"
LISTS = "smem"
FAR = "hbm"


def call(kernel, operands, places, out_shapes, out_places, scratch=(), limit=67_000_000, alias=None):
    total_in, total_out = len(operands), len(out_shapes)
    buffers = []
    for place, array in zip(list(places) + list(out_places), list(operands) + list(out_shapes)):
        if place not in (HERE, PASS, WIDER):
            kind = SMEM if place == LISTS else VMEM
            dims = array.shape
            if isinstance(place, tuple):
                dims = (place[1] - place[0],) + tuple(dims[1:])
            buffers.append(kind(dims, array.dtype))

    def body(*refs):
        given = refs[: total_in + total_out]
        own = refs[total_in + total_out :]
        local, sems, rest = own[: len(buffers)], own[len(buffers)], own[len(buffers) + 1 :]
        seen = []
        used = 0
        for index, place in enumerate(list(places) + list(out_places)):
            if place in (HERE, PASS):
                seen.append(given[index])
                continue
            if place == WIDER:
                seen.append(Wider(given[index], sems.at[len(buffers)]))
                continue
            near = local[used]
            far = given[index]
            if isinstance(place, tuple):
                far = far.at[place[0] : place[1]]
            if index < total_in:
                copy = pltpu.make_async_copy(far, near, sems.at[used])
                copy.start()
                seen.append(Late(near, copy))
            else:
                seen.append(Out(near, pltpu.make_async_copy(near, far, sems.at[used])))
            used += 1
        kernel(*seen, *rest)
        for item in seen[:total_in]:
            if isinstance(item, Late):
                item.ready()
        for item in seen[total_in:]:
            if isinstance(item, Out):
                item.flush()
        for item in seen[total_in:]:
            if isinstance(item, (Out, Wider)):
                item.copy.wait()

    def spec(place):
        return pl.BlockSpec(memory_space=VMEM if place == HERE else pltpu.HBM)

    return pl.pallas_call(
        body,
        out_shape=out_shapes,
        in_specs=[spec(place) for place in places],
        out_specs=[spec(place) for place in out_places],
        scratch_shapes=buffers + [pltpu.SemaphoreType.DMA((len(buffers) + 1,))] + list(scratch),
        compiler_params=pltpu.CompilerParams(vmem_limit_bytes=limit),
        cost_estimate=pl.CostEstimate(flops=10**8, bytes_accessed=10**6, transcendentals=0),
        input_output_aliases=alias or {},
    )(*operands)


def shape_of(dims, kind):
    return jax.ShapeDtypeStruct(dims, kind)


def dot(left, right):
    return jnp.dot(left, right, preferred_element_type=F32)


def dot_nt(left, right):
    return lax.dot_general(left, right, (((1,), (1,)), ((), ())), preferred_element_type=F32)


def shifted(wide):
    lanes = wide.shape[1]
    lane = lax.broadcasted_iota(jnp.int32, wide.shape, 1)
    low = jnp.where(lane == 0, 0.0, pltpu.roll(wide, 1, 1))
    high = jnp.where(lane == lanes - 1, 0.0, pltpu.roll(wide, lanes - 1, 1))
    return low, wide, high


def put_columns(column_ref, row, plane, slices):
    channels = plane.shape[0] // slices
    block = 3 * plane.shape[0]
    for tap, moved in enumerate(shifted(plane.astype(F32))):
        moved = moved.astype(BF16)
        for z in range(slices):
            start = row * block + (z * 3 + tap) * channels
            column_ref[start : start + channels, :] = moved[z * channels : (z + 1) * channels]


def window(column_ref, row, block):
    return column_ref[(row - 1) * block : (row + 2) * block, :]


def sigmoid(values):
    return 1.0 / (1.0 + jnp.exp(-values))


def spread_lists(gradient, slices, taps_z=3):
    channels = gradient.shape[0] // slices
    parts = []
    for z_in in range(slices):
        rows = []
        for i in range(taps_z):
            z_out = z_in - i + 1
            if 0 <= z_out < slices:
                rows.append(gradient[z_out * channels : (z_out + 1) * channels])
            else:
                rows.append(jnp.zeros((channels, gradient.shape[1]), BF16))
        parts.append(jnp.concatenate(rows, axis=0))
    return parts


def moved_gradient(gradient, slices):
    low, here, high = shifted(gradient.astype(F32))
    versions = [spread_lists(part.astype(BF16), slices) for part in (high, here, low)]
    return [
        jnp.concatenate([version[z] for version in versions], axis=0) for z in range(slices)
    ]


def state_wgrad(moved, planes, slices):
    channels = planes[0].shape[0] // slices
    total = None
    for z in range(slices):
        around = jnp.concatenate(
            [plane[z * channels : (z + 1) * channels] for plane in planes], axis=0
        )
        term = dot_nt(moved[z], around)
        total = term if total is None else total + term
    return total


def tap_of(i, j, l):
    return (i * 3 + j) * 3 + l


def forward_weight(weight_ref, slices, low, high, lane_major):
    rows = []
    for z in range(slices):
        pieces = []
        for j in range(3):
            pairs = [(zi, l) for zi in range(slices) for l in range(3)]
            if lane_major:
                pairs = [(zi, l) for l in range(3) for zi in range(slices)]
            for zi, l in pairs:
                i = zi - z + 1
                if 0 <= i < 3:
                    pieces.append(weight_ref[tap_of(i, j, l)].astype(F32)[:, low:high])
                else:
                    pieces.append(jnp.zeros((weight_ref.shape[1], high - low), F32))
        rows.append(jnp.concatenate(pieces, axis=1))
    return jnp.concatenate(rows, axis=0).astype(BF16)


def adjoint_weight(weight_ref, slices, low, high, first=0, last=None, lane_major=False):
    last = weight_ref.shape[1] if last is None else last
    rows = []
    for j in range(3):
        pairs = [(z, l) for z in range(slices) for l in range(3)]
        if lane_major:
            pairs = [(z, l) for l in range(3) for z in range(slices)]
        for z, l in pairs:
            pieces = []
            for zi in range(slices):
                i = zi - z + 1
                if 0 <= i < 3:
                    tap = weight_ref[tap_of(i, 2 - j, 2 - l)].astype(F32)
                    pieces.append(tap[first:last, low:high])
                else:
                    pieces.append(jnp.zeros((last - first, high - low), F32))
            rows.append(jnp.concatenate(pieces, axis=1))
    return jnp.concatenate(rows, axis=0).T.astype(BF16)


def arrived(*refs):
    return [ref.ready() if isinstance(ref, Late) else ref for ref in refs]


def as_column(values):
    count = values.shape[0]
    square = jnp.broadcast_to(values[None, :], (count, count))
    row = lax.broadcasted_iota(jnp.int32, square.shape, 0)
    col = lax.broadcasted_iota(jnp.int32, square.shape, 1)
    return jnp.sum(jnp.where(row == col, square, 0.0), axis=1, keepdims=True)


def code_hits(tile_ref, table_ref, column_ref, count_ref):
    tiles = tile_ref[...]
    count = as_column(count_ref[...].astype(F32))
    live = lax.broadcasted_iota(jnp.int32, tiles.shape, 1).astype(F32) < count
    codes = table_ref[...] * 16 + column_ref[...]
    position = lax.axis_index("view")
    found = [(tiles * 256 + codes).astype(F32), count]
    for slot in range(3):
        hit = live & (tiles == position + slot - 1)
        found.append(
            jnp.sum(jnp.where(hit, codes.astype(F32) + 1.0, 0.0), axis=1, keepdims=True) - 1.0
        )
    return jnp.concatenate(found, axis=1).astype(jnp.int32)


def mixing_of(energy_ref, basis_ref, bins):
    (energy_ref,) = arrived(energy_ref)
    energies = basis_ref.shape[0]
    row = lax.broadcasted_iota(jnp.int32, (bins, energies), 0)
    col = lax.broadcasted_iota(jnp.int32, (bins, energies), 1)
    onehot = jnp.zeros((bins, energies), F32)
    for n in range(bins):
        onehot = jnp.where((row == n) & (col == energy_ref[n]), 1.0, onehot)
    return dot(onehot.astype(BF16), basis_ref[...])


def send_rays(images, footprint_ref, send_ref):
    for table in range(footprint_ref.shape[0]):
        rays = dot(images, footprint_ref[table]).astype(BF16)
        for target in range(send_ref.shape[0]):
            send_ref[target, table] = rays


def pack_kernel(
    dual_ref,
    cot_dual_ref,
    sino_ref,
    volume_ref,
    energy_ref,
    basis_ref,
    footprint_ref,
    cot_volume_ref,
    pack_ref,
    near_ref,
    send_ref,
    cells_ref,
):
    channels, slices, rows_tile, _ = volume_ref.shape
    bins = sino_ref.shape[0]
    rows = slices * channels
    head = head_rows(rows, slices * bins)
    sino_rows = []
    for z in range(slices):
        at = z * channels
        pack_ref[at : at + channels, :] = dual_ref[:, z, :]
        at = head + z * channels
        pack_ref[at : at + channels, :] = cot_dual_ref[:, z, :]
        sino_rows.append(sino_ref[:, z, :].astype(F32))
    sino_rows.append(jnp.zeros((head - rows - slices * bins, sino_ref.shape[2]), F32))
    pack_ref[rows:head, :] = jnp.concatenate(sino_rows, axis=0).astype(BF16)
    near_ref.flush_from(pack_ref)
    pack_ref.flush()
    at = 0
    for source in (volume_ref, cot_volume_ref):
        for r in range(rows_tile):
            for z in range(slices):
                cells_ref[at : at + channels, :] = source[:, z, r, :]
                at += channels
        if source is volume_ref:
            mixing = mixing_of(energy_ref, basis_ref, bins).astype(BF16)
            images = []
            for z in range(slices):
                line = []
                for r in range(rows_tile):
                    first = (r * slices + z) * channels
                    line.append(dot(mixing, cells_ref[first : first + channels, :]))
                images.append(jnp.concatenate(line, axis=1))
            send_rays(jnp.concatenate(images, axis=0).astype(BF16), footprint_ref, send_ref)
            send_ref.flush()


def head_rows(rows, height):
    return rows + pl.cdiv(height, 16) * 16


def weights_kernel(
    slices,
    tile_ref,
    table_ref,
    column_ref,
    count_ref,
    di,
    do,
    bias_0,
    bias_1,
    bias_2,
    bias_3,
    weight_ref,
    bias_ref,
    hits_ref,
):
    channels = do.shape[1]
    hits_ref[...] = code_hits(tile_ref, table_ref, column_ref, count_ref)
    columns = [column_bias(bias, slices) for bias in (bias_0, bias_1, bias_2, bias_3)]
    bias_ref[...] = jnp.concatenate(columns, axis=1)
    weight_ref[...] = jnp.concatenate(
        [
            forward_weight(di, slices, 0, channels, False),
            forward_weight(do, slices, 0, channels, False),
            forward_weight(di, slices, channels, di.shape[2], True),
        ],
        axis=1,
    )


def ray_windows(rays_ref, hits_ref, sums_ref, views):
    rays_ref, hits_ref = arrived(rays_ref, hits_ref)
    blocks, entries = hits_ref.shape[0], hits_ref.shape[1] - 4
    columns = sums_ref.shape[0] // len(views)
    sums_ref[...] = jnp.zeros_like(sums_ref)
    for place, offset in enumerate(views):
        view = lax.rem(lax.axis_index("view") + offset + blocks, blocks)

        def each_entry(k, carry):
            code = hits_ref[view, k]
            at = place * columns + lax.rem(code, 16)
            table = lax.rem(lax.div(code, 16), 16)
            sums_ref[at] += rays_ref[lax.div(code, 256), table].astype(F32)
            return carry

        lax.fori_loop(0, hits_ref[view, entries], each_entry, 0)
    return [
        jnp.concatenate([sums_ref[place * columns + c] for c in range(columns)], axis=1)
        for place in range(len(views))
    ]


def extra_rows(projected, sino, slices, bins):
    rows = []
    for z in range(slices):
        rows.append(projected[z * bins : (z + 1) * bins])
        rows.append(sino[z * bins : (z + 1) * bins])
    return jnp.concatenate(rows, axis=0)


def extra_columns(pieces):
    return jnp.concatenate([piece for triple in pieces for piece in triple], axis=0).astype(BF16)


def column_bias(bias_ref, slices):
    return jnp.concatenate([as_column(bias_ref[...])] * slices, axis=0)


def five_views(own, beside, far, over, low, gap):
    even = lax.rem(lax.axis_index("view"), 2) == 0
    own, beside, across = Rows(own, low), Rows(beside, low), Rows(far, low)
    two, over = Rows(far, low + gap), Rows(over, low)
    return (
        Choice(even, two, over),
        Choice(even, across, beside),
        own,
        Choice(even, beside, across),
        Choice(even, over, two),
    )


class Rows:
    def __init__(self, source, first):
        self.source, self.first, self.shape = source, first, source.shape

    def __getitem__(self, index):
        rows, lanes = index
        return self.source[rows.start + self.first : rows.stop + self.first, lanes]


class Valid:
    def __init__(self, valid, source):
        self.valid, self.source, self.shape = valid, source, source.shape

    def __getitem__(self, index):
        values = self.source[index]
        return jnp.where(self.valid, values.astype(F32), 0.0).astype(values.dtype)


def three_tiles(blocks, own, beside, across):
    even = lax.rem(lax.axis_index("view"), 2) == 0
    return (
        Valid(lax.axis_index("view") > 0, Choice(even, across, beside)),
        own,
        Valid(lax.axis_index("view") < blocks - 1, Choice(even, beside, across)),
    )


def dual_forward_kernel(
    slices,
    bins,
    gap,
    pack_ref,
    beside_ref,
    far_ref,
    over_ref,
    rays_ref,
    hits_ref,
    weight_ref,
    bias_ref,
    send_ref,
    slope_ref,
    hidden_ref,
    new_ref,
    sums_ref,
    columns_ref,
    hidden_columns,
):
    around = five_views(pack_ref, beside_ref, far_ref, over_ref, 0, gap)
    channels = new_ref.shape[0]
    rows = channels * slices
    height = slices * bins
    for row in range(5):
        put_columns(columns_ref, row, around[row][0:rows, :], slices)
    projected = ray_windows(rays_ref, hits_ref, sums_ref, (-2, -1, 0, 1, 2))
    bias_inner, bias_outer = bias_ref[:, 0:1], bias_ref[:, 1:2]
    w1s = weight_ref[:, 0 : 9 * rows]
    w2 = weight_ref[:, 9 * rows : 18 * rows]
    w1e = weight_ref[:, 18 * rows :]
    pieces = []
    for row in range(5):
        extra = extra_rows(
            projected[row].astype(BF16).astype(F32),
            around[row][rows : rows + height, :].astype(F32),
            slices,
            bins,
        )
        if 1 <= row <= 3:
            at = 3 * rows + (row - 1) * extra.shape[0]
            hidden_ref[at : at + extra.shape[0], :] = extra.astype(BF16)
        pieces.append(shifted(extra))
    for row in range(3):
        at = row * rows
        pre = dot(w1s, window(columns_ref, row + 1, 3 * rows))
        pre = pre + dot(w1e, extra_columns(pieces[row : row + 3])) + bias_inner
        gate = sigmoid(pre)
        hidden = (pre * gate).astype(BF16)
        hidden_ref[at : at + rows, :] = hidden
        slope_ref[at : at + rows, :] = gate * (1.0 + pre * (1.0 - gate))
        put_columns(hidden_columns, row, hidden, slices)
    slope_ref.flush()
    hidden_ref.flush()
    update = dot(w2, hidden_columns[...]) + bias_outer
    fresh = (around[2][0:rows, :].astype(F32) + update).astype(BF16)
    out = []
    for z in range(slices):
        plane = fresh[z * channels : (z + 1) * channels]
        new_ref[:, z, :] = plane
        out.append(plane.astype(F32)[:bins])
    new_ref.flush()
    out = jnp.concatenate(out, axis=0).astype(BF16)
    for target in range(send_ref.shape[0]):
        send_ref[target] = out
    send_ref.flush()


def gather_signals(signal_ref, code_ref, slots, footprint_ref, sums_ref, chosen=False):
    signal_ref, code_ref = arrived(signal_ref, code_ref)
    first = code_ref.shape[1] - 3
    tables = footprint_ref.shape[0]
    spare = len(slots) * tables
    sums_ref[...] = jnp.zeros_like(sums_ref)

    def each_block(b, carry):
        for place, slot in enumerate(slots):
            code = code_ref[b, first + slot]
            live = code >= 0
            code = jnp.maximum(code, 0)
            at = jnp.where(live, place * tables + lax.div(code, 16), spare)
            lane = 0
            if not chosen:
                lane = pl.multiple_of(lax.rem(code, 16) * UW, UW)
            sums_ref[at] += signal_ref[b, :, pl.ds(lane, UW)].astype(F32)
        return carry

    lax.fori_loop(0, signal_ref.shape[0], each_block, 0)
    total = None
    for table in range(tables):
        grouped = jnp.concatenate(
            [sums_ref[place * tables + table] for place in range(len(slots))], axis=0
        )
        high = grouped.astype(BF16).astype(F32)
        both = jnp.concatenate([high, grouped - high], axis=0).astype(BF16)
        term = dot_nt(both, footprint_ref[table])
        total = term if total is None else total + term
    half = total.shape[0] // 2
    return total[:half] + total[half:]


def fold_lanes(array):
    full = array.shape[1] // TILE * TILE
    rest = array.shape[1] - full
    if rest == 0:
        return [array]
    copies = TILE // rest
    while array.shape[0] % (8 * copies):
        copies -= 1
    rows = array.shape[0] // copies
    side = [array[c * rows : (c + 1) * rows, full:] for c in range(copies)]
    side = jnp.concatenate(side, axis=1) if copies > 1 else side[0]
    return ([array[:, :full]] if full else []) + [side]


def fold_shapes(rows, width):
    full = width // TILE * TILE
    rest = width - full
    if rest == 0:
        return [(rows, width)], 1
    copies = TILE // rest
    while rows % (8 * copies):
        copies -= 1
    return ([(rows, full)] if full else []) + [(rows // copies, rest * copies)], copies


def tile_count(rows, width):
    shapes, _ = fold_shapes(rows, width)
    return sum(r // 8 * pl.cdiv(w, TILE) for r, w in shapes)


def put_payload(payload_ref, per, first, array):
    flat = first
    for part in fold_lanes(array):
        width = part.shape[1]
        for group in range(part.shape[0] // 8):
            for tile in range(pl.cdiv(width, TILE)):
                last = min(width, (tile + 1) * TILE)
                lane = (flat % per) * TILE
                payload_ref[flat // per, :, lane : lane + last - tile * TILE] = part[
                    group * 8 : group * 8 + 8, tile * TILE : last
                ].astype(BF16)
                flat += 1
    return flat


def take_payload(payload_ref, per, first, rows, width):
    flat = first
    shapes, copies = fold_shapes(rows, width)
    parts = []
    for part_rows, part_width in shapes:
        groups = []
        for _ in range(part_rows // 8):
            tiles = []
            for _ in range(pl.cdiv(part_width, TILE)):
                lane = (flat % per) * TILE
                tiles.append(payload_ref[flat // per, :, lane : lane + TILE].astype(F32))
                flat += 1
            groups.append(jnp.concatenate(tiles, axis=1) if len(tiles) > 1 else tiles[0])
        parts.append(jnp.concatenate(groups, axis=0))
    rest = width % TILE
    if rest:
        side = parts.pop()
        parts.append(
            jnp.concatenate([side[:, c * rest : (c + 1) * rest] for c in range(copies)], axis=0)
        )
    return (jnp.concatenate(parts, axis=1) if len(parts) > 1 else parts[0]), flat


def row_plane(tiles, row, which, rows, rows_tile):
    ref, r = tiles[row // rows_tile], row % rows_tile
    at = (which * rows_tile + r) * rows
    return ref[at : at + rows, :]


def primal_state_kernel(
    slices,
    rows_tile,
    blocks,
    v0,
    v1,
    v2,
    inner_ref,
    outer_ref,
    bias_ref,
    state_ref,
    near_weight,
    rest_weight,
    columns_ref,
    cot_columns,
):
    tiles = three_tiles(blocks, v0, v1, v2)
    channels = outer_ref.shape[1]
    rows = channels * slices
    bins = inner_ref.shape[2] - channels
    w1s = forward_weight(inner_ref, slices, 0, channels, False)
    w2t = adjoint_weight(outer_ref, slices, 0, channels)
    thin = slices * bins
    near_weight[0:thin, :] = adjoint_weight(inner_ref, slices, channels, channels + bins)
    near_weight[thin : thin + rows, 0 : 9 * thin] = forward_weight(
        inner_ref, slices, channels, inner_ref.shape[2], True
    )
    rest_weight[0:rows, :] = forward_weight(outer_ref, slices, 0, channels, False)
    rest_weight[rows : 2 * rows, :] = adjoint_weight(inner_ref, slices, 0, channels)
    bias = bias_ref[:, 2:3]
    kept = (rows_tile + 2) * rows
    first = rows_tile - 2
    for row in range(rows_tile + 4):
        at = first + row
        put_columns(columns_ref, row, row_plane(tiles, at, 0, rows, rows_tile), slices)
        put_columns(cot_columns, row, row_plane(tiles, at, 1, rows, rows_tile), slices)
    for row in range(rows_tile + 2):
        pre = dot(w1s, window(columns_ref, row + 1, 3 * rows)) + bias
        state_ref[row * rows : (row + 1) * rows, :] = pre
        gradient = dot(w2t, window(cot_columns, row + 1, 3 * rows))
        state_ref[kept + row * rows : kept + (row + 1) * rows, :] = gradient


def primal_kernel(
    slices,
    bins,
    rows_tile,
    signal_ref,
    code_ref,
    footprint_ref,
    weight_ref,
    state_ref,
    send_ref,
    mixed_ref,
    sums_ref,
    grad_columns,
):
    blocks = send_ref.shape[0]
    lanes = state_ref.shape[1]
    thin = slices * bins
    rows = weight_ref.shape[0] - thin
    kept = (rows_tile + 2) * rows
    position = lax.axis_index("view")
    height = slices * bins
    back = gather_signals(signal_ref, code_ref, (0, 1, 2), footprint_ref, sums_ref)
    back = back.astype(BF16).astype(F32)
    pieces = []
    for row in range(rows_tile + 4):
        at = row + rows_tile - 2
        tile, r = at // rows_tile, at % rows_tile
        extra = back[tile * height : (tile + 1) * height, r * lanes : (r + 1) * lanes]
        at = 2 * kept + row * height
        mixed_ref[at : at + height, :] = extra.astype(BF16)
        pieces.append(shifted(extra))
    w1x = weight_ref[0:thin, :]
    w1e = weight_ref[thin : thin + rows, 0 : 9 * thin]
    for row in range(rows_tile + 2):
        at = row * rows
        pre = state_ref[at : at + rows, :] + dot(w1e, extra_columns(pieces[row : row + 3]))
        gate = sigmoid(pre)
        hidden = pre * gate
        gradient = state_ref[kept + at : kept + at + rows, :] * (gate * (1.0 + pre * (1.0 - gate)))
        if row == 0:
            hidden = jnp.where(position > 0, hidden, 0.0)
            gradient = jnp.where(position > 0, gradient, 0.0)
        if row == rows_tile + 1:
            hidden = jnp.where(position < blocks - 1, hidden, 0.0)
            gradient = jnp.where(position < blocks - 1, gradient, 0.0)
        gradient = gradient.astype(BF16)
        mixed_ref[at : at + rows, :] = hidden.astype(BF16)
        mixed_ref[kept + at : kept + at + rows, :] = gradient
        put_columns(grad_columns, row, gradient, slices)
    mixed_ref.flush()
    parts = []
    for row in range(rows_tile):
        parts.append(dot(w1x, window(grad_columns, row + 1, 3 * rows)))
    send_rays(jnp.concatenate(parts, axis=1).astype(BF16), footprint_ref, send_ref)


def primal_rest_kernel(
    slices,
    rows_tile,
    blocks,
    mixed_ref,
    v0,
    v1,
    v2,
    weight_ref,
    bias_ref,
    new_ref,
    state_ref,
    payload_ref,
    hidden_columns,
    grad_columns,
    ready_ref,
    sem,
):
    tiles = three_tiles(blocks, v0, v1, v2)
    channels = new_ref.shape[0]
    rows = channels * slices
    kept = (rows_tile + 2) * rows
    height = (mixed_ref.shape[0] - 2 * kept) // (rows_tile + 4)
    hidden_ref, gradient_ref = mixed_ref, Rows(mixed_ref, kept)
    bias = bias_ref[:, 3:4]
    w2 = weight_ref[0:rows, :]
    w1t = weight_ref[rows : 2 * rows, :]
    for row in range(rows_tile + 2):
        at = row * rows
        put_columns(hidden_columns, row, hidden_ref[at : at + rows, :], slices)
        put_columns(grad_columns, row, gradient_ref[at : at + rows, :], slices)
    pieces = [
        shifted(
            mixed_ref[2 * kept + row * height : 2 * kept + (row + 1) * height, :].astype(F32)
        )
        for row in range(1, rows_tile + 3)
    ]
    inner = None
    outer = None
    extra_total = None
    for r in range(rows_tile):
        at = (r + 1) * rows
        cot = row_plane(tiles, rows_tile + r, 1, rows, rows_tile)
        own = row_plane(tiles, rows_tile + r, 0, rows, rows_tile)
        gradient = gradient_ref[at : at + rows, :]
        state = dot(w1t, window(grad_columns, r + 1, 3 * rows)) + cot.astype(F32)
        update = dot(w2, window(hidden_columns, r + 1, 3 * rows)) + bias
        fresh = (own.astype(F32) + update).astype(BF16)
        state_ref[r * rows : (r + 1) * rows, :] = state
        for z in range(slices):
            new_ref[:, z, r, :] = fresh[z * channels : (z + 1) * channels]
        planes = [
            row_plane(tiles, rows_tile - 1 + r + j, 0, rows, rows_tile) for j in range(3)
        ]
        term = state_wgrad(moved_gradient(gradient, slices), planes, slices)
        inner = term if inner is None else inner + term
        planes = [hidden_ref[(r + j) * rows : (r + j + 1) * rows, :] for j in range(3)]
        term = state_wgrad(moved_gradient(cot, slices), planes, slices)
        outer = term if outer is None else outer + term
        term = dot_nt(gradient, extra_columns(pieces[r : r + 3]))
        extra_total = term if extra_total is None else extra_total + term
    per = ready_ref.shape[2] // TILE
    flat = put_payload(ready_ref, per, 0, jnp.concatenate([inner, outer], axis=1))
    put_payload(ready_ref, per, flat, extra_total)
    copy = pltpu.make_async_copy(ready_ref, payload_ref.at[:, :, 0 : per * TILE], sem.at[0])
    copy.start()
    copy.wait()


def dual_cot_kernel(
    slices,
    bins,
    gap,
    c0,
    c1,
    c2,
    c3,
    inner_ref,
    outer_ref,
    part_ref,
    weight_ref,
    columns_ref,
):
    around = five_views(c0, c1, c2, c3, 0, gap)
    rows = c0.shape[0]
    thin = slices * bins
    channels = rows // slices
    w2t = adjoint_weight(outer_ref, slices, 0, channels)
    weight_ref[0:rows, :] = adjoint_weight(inner_ref, slices, 0, channels)
    weight_ref[rows : rows + thin, :] = adjoint_weight(inner_ref, slices, channels, channels + bins)
    weight_ref[rows + thin : 2 * rows + thin, 0 : 9 * thin] = adjoint_weight(
        outer_ref, slices, 0, channels, 0, bins, True
    )
    for row in range(5):
        plane = around[row][0:rows, :].astype(F32)
        channel = lax.broadcasted_iota(jnp.int32, plane.shape, 0)
        plane = jnp.where(lax.rem(channel, channels) < bins, 0.0, plane)
        put_columns(columns_ref, row, plane, slices)
    for row in range(3):
        at = row * rows
        part_ref[at : at + rows, :] = dot(w2t, window(columns_ref, row + 1, 3 * rows))


def dual_backward_kernel(
    slices,
    bins,
    per,
    low,
    gap,
    pack_ref,
    beside_ref,
    far_ref,
    over_ref,
    rays_ref,
    hits_ref,
    weight_ref,
    part_ref,
    slope_ref,
    hidden_ref,
    payload_in,
    grad_ref,
    payload_ref,
    sums_ref,
    grad_columns,
    windows_ref,
    ready_ref,
    sem,
):
    del payload_in
    around = five_views(pack_ref, beside_ref, far_ref, over_ref, low, gap)
    states = five_views(pack_ref, beside_ref, far_ref, over_ref, 0, gap)[1:4]
    channels = grad_ref.shape[0]
    rows = channels * slices
    thin = slices * bins
    toward = ray_windows(rays_ref, hits_ref, sums_ref, (-2, -1, 0, 1, 2))
    w1t = weight_ref[0:rows, :]
    w1x = weight_ref[rows : rows + thin, :]
    w2x = weight_ref[rows + thin : 2 * rows + thin, 0 : 9 * thin]
    pieces = []
    own_head = None
    for row in range(5):
        head = jnp.concatenate(
            [
                around[row][z * channels : z * channels + 2 * bins, :].astype(F32)[:bins]
                for z in range(slices)
            ],
            axis=0,
        )
        head = head + toward[row]
        if row == 2:
            own_head = head
        pieces.append(shifted(head.astype(BF16).astype(F32)))
    spread = []
    lanes = own_head.shape[1]
    for z in range(slices):
        spread.append(own_head[z * bins : (z + 1) * bins])
        spread.append(around[2][z * channels : (z + 1) * channels, :].astype(F32)[bins:])
    own_total = jnp.concatenate(spread, axis=0)
    own_cot = own_total.astype(BF16)
    own_gradient = None
    for row in range(3):
        at = row * rows
        gradient = part_ref[at : at + rows, :] + dot(w2x, extra_columns(pieces[row : row + 3]))
        gradient = (gradient * slope_ref[at : at + rows, :]).astype(BF16)
        put_columns(grad_columns, row, gradient, slices)
        if row == 1:
            own_gradient = gradient
    out = dot(w1x, grad_columns[...]).astype(BF16)
    for column in range(lanes // UW):
        windows_ref[column] = out[:, column * UW : (column + 1) * UW]
    start = per * TILE
    ready_ref[:, :, start : start + UW] = jnp.zeros(
        (ready_ref.shape[0], ready_ref.shape[1], UW), BF16
    )
    view = lax.axis_index("view")
    (hits,) = arrived(hits_ref)

    def each_entry(k, carry):
        code = hits[view, k]
        ready_ref[lax.div(code, 256), :, start : start + UW] = windows_ref[lax.rem(code, 16)]
        return carry

    lax.fori_loop(0, hits[view, hits.shape[1] - 4], each_entry, 0)
    planes = [states[row][0:rows, :] for row in range(3)]
    inner = state_wgrad(moved_gradient(own_gradient, slices), planes, slices)
    planes = [hidden_ref[row * rows : (row + 1) * rows, :] for row in range(3)]
    outer = state_wgrad(moved_gradient(own_cot, slices), planes, slices)
    height = (hidden_ref.shape[0] - 3 * rows) // 3
    pieces = []
    for row in range(3):
        at = 3 * rows + row * height
        pieces.append(shifted(hidden_ref[at : at + height, :].astype(F32)))
    extra = dot_nt(own_gradient, extra_columns(pieces))
    flat = put_payload(ready_ref, per, 0, jnp.concatenate([inner, outer], axis=1))
    put_payload(ready_ref, per, flat, extra)
    total = payload_ref.shape[2]
    copy = pltpu.make_async_copy(
        ready_ref, payload_ref.at[:, :, total - ready_ref.shape[2] : total], sem.at[0]
    )
    copy.start()
    state = (dot(w1t, grad_columns[...]) + own_total).astype(BF16)
    for z in range(slices):
        grad_ref[:, z, :] = state[z * channels : (z + 1) * channels]
    grad_ref.flush()
    copy.wait()


def sum_kernel(payload_ref, send_ref, rays_ref):
    width = send_ref.shape[2]
    total = payload_ref[0, :, 0:width].astype(F32)
    for source in range(1, payload_ref.shape[0]):
        total = total + payload_ref[source, :, 0:width].astype(F32)
    total = total.astype(BF16)
    for target in range(send_ref.shape[0]):
        send_ref[target] = total
    rays_ref[...] = payload_ref[:, :, width:]


def volume_grad_kernel(
    slices,
    bins,
    signal_ref,
    code_ref,
    energy_ref,
    basis_ref,
    footprint_ref,
    state_ref,
    out_ref,
    sums_ref,
):
    back = gather_signals(
        signal_ref, code_ref, (1,), footprint_ref, sums_ref, chosen=True
    )
    mixing = mixing_of(energy_ref, basis_ref, bins)
    channels, _, rows_tile, lanes = out_ref.shape
    for z in range(slices):
        part = back[z * bins : (z + 1) * bins]
        high = part.astype(BF16).astype(F32)
        low = part - high
        spread = lax.dot_general(
            jnp.concatenate([mixing, mixing], axis=0).astype(BF16),
            jnp.concatenate([high, low], axis=0).astype(BF16),
            (((0,), (0,)), ((), ())),
            preferred_element_type=F32,
        )
        for r in range(rows_tile):
            at = (r * slices + z) * channels
            total = state_ref[at : at + channels, :] + spread[:, r * lanes : (r + 1) * lanes]
            out_ref[:, z, r, :] = total.astype(BF16)


class Region:
    def __init__(self, ref, first):
        self.ref, self.first = ref, first

    def __getitem__(self, index):
        chunk, rows, lanes = index
        return self.ref[chunk, rows, lanes.start + self.first : lanes.stop + self.first]


def unpack_kernel(
    slices, per_primal, per_dual, payload_ref, primal_inner, primal_outer, dual_inner, dual_outer
):
    channels = dual_outer.shape[1]
    for inner_ref, outer_ref, per, first in (
        (primal_inner, primal_outer, per_primal, 0),
        (dual_inner, dual_outer, per_dual, per_primal * TILE),
    ):
        region = Region(payload_ref, first)
        flat = 0
        extra_count = inner_ref.shape[2] - channels
        state, flat = take_payload(region, per, flat, 9 * channels, 6 * channels)
        extra, flat = take_payload(region, per, flat, slices * channels, 9 * slices * extra_count)
        for i in range(3):
            for j in range(3):
                for l in range(3):
                    tap = (i * 3 + j) * 3 + l
                    lane = j * channels
                    rows = state[(l * 3 + i) * channels : (l * 3 + i + 1) * channels]
                    more = None
                    for z in range(slices):
                        z_in = z + i - 1
                        if 0 <= z_in < slices:
                            at = ((j * 3 + l) * slices + z_in) * extra_count
                            term = extra[z * channels : (z + 1) * channels, at : at + extra_count]
                            more = term if more is None else more + term
                    inner_ref[tap] = jnp.concatenate(
                        [rows[:, lane : lane + channels], more], axis=1
                    )
                    lane = lane + 3 * channels
                    outer_ref[tap] = rows[:, lane : lane + channels]
        inner_ref.flush()
        outer_ref.flush()


def whole(
    volume,
    dual_state,
    sinogram,
    cot_volume,
    cot_dual,
    basis_table,
    bin_energy,
    footprint_table,
    hit_tile,
    hit_table,
    hit_column,
    hit_count,
    primal_inner,
    primal_inner_bias,
    primal_outer,
    primal_outer_bias,
    dual_inner,
    dual_inner_bias,
    dual_outer,
    dual_outer_bias,
):
    count = lax.axis_size("view")
    channels, slices, rows_tile, cells = volume.shape
    bins = sinogram.shape[0]
    detector = dual_state.shape[3]
    columns = detector // UW
    tables = footprint_table.shape[0]
    blocks, entries = hit_tile.shape
    height = slices * bins
    rows = slices * channels
    block = 3 * rows
    lists = (hit_tile, hit_table, hit_column, hit_count)
    list_places = (LISTS,) * 4

    def exchange(array):
        return lax.all_to_all(array, "view", split_axis=0, concat_axis=0)

    def swap(array):
        return lax.ppermute(array, "view", [(k, k ^ 1) for k in range(count)])

    def cross(array, periodic):
        pairs = []
        for k in range(1, count, 2):
            if periodic or k + 1 < count:
                pairs += [(k, (k + 1) % count), ((k + 1) % count, k)]
        return lax.ppermute(array, "view", pairs)

    head = head_rows(rows, height)
    near_rows = head + rows
    dual_flat = (channels, slices, detector)
    pack, near, rays, tile = call(
        pack_kernel,
        (dual_state.reshape(dual_flat), cot_dual.reshape(dual_flat))
        + (sinogram.reshape(bins, slices, detector), volume, bin_energy, basis_table)
        + (footprint_table, cot_volume),
        (FAR,) * 4 + (LISTS,) + (FAR,) * 3,
        [
            shape_of((near_rows, detector), BF16),
            shape_of((2 * near_rows, detector), BF16),
            shape_of((count, tables, height, UW), BF16),
            shape_of((2 * rows_tile * rows, cells), BF16),
        ],
        [FAR, WIDER, FAR, FAR],
    )
    beside = swap(pack)
    rays = exchange(rays)
    near = lax.dynamic_update_slice(near, beside, (near_rows, 0))
    far = cross(near, True)
    tiles = (tile, swap(tile), cross(tile, False))
    over = swap(far)
    views = (pack, beside, far, over)

    def ranges(first, last):
        return ((first, last), (first, last), (first, near_rows + last), (first, last))

    wide = shape_of((rows, 9 * rows), BF16)
    extra_dual = dual_inner.shape[2] - channels
    extra_primal = primal_inner.shape[2] - channels
    dual_weight, biases, hits = call(
        functools.partial(weights_kernel, slices),
        (*lists, dual_inner, dual_outer, dual_inner_bias, dual_outer_bias)
        + (primal_inner_bias, primal_outer_bias),
        (FAR,) * 10,
        [
            shape_of((rows, 18 * rows + 9 * slices * extra_dual), BF16),
            shape_of((rows, 4), F32),
            shape_of((blocks, entries + 4), jnp.int32),
        ],
        [FAR] * 3,
    )
    signal, slope, hidden, new_dual = call(
        functools.partial(dual_forward_kernel, slices, bins, near_rows),
        (*views, rays, hits, dual_weight, biases),
        ranges(0, head) + (FAR, LISTS, FAR, FAR),
        [
            shape_of((count, height, detector), BF16),
            shape_of((3 * rows, detector), F32),
            shape_of((3 * (rows + 2 * height), detector), BF16),
            shape_of(dual_flat, BF16),
        ],
        [FAR] * 4,
        [
            VMEM((5 * columns, height, UW), F32),
            VMEM((5 * block, detector), BF16),
            VMEM((3 * block, detector), BF16),
        ],
    )
    signal = exchange(signal)
    kept = (rows_tile + 2) * rows
    per_primal = tile_count(9 * channels, 6 * channels)
    per_dual = pl.cdiv(per_primal + tile_count(rows, 9 * slices * extra_dual), count)
    per_primal = pl.cdiv(per_primal + tile_count(rows, 9 * slices * extra_primal), count)
    width = (per_primal + per_dual) * TILE
    primal_state, near_weight, rest_weight = call(
        functools.partial(primal_state_kernel, slices, rows_tile, blocks),
        (*tiles, primal_inner, primal_outer, biases),
        (FAR,) * 6,
        [
            shape_of((2 * kept, cells), F32),
            shape_of((height + rows, 9 * rows), BF16),
            shape_of((2 * rows, 9 * rows), BF16),
        ],
        [FAR] * 3,
        [VMEM(((rows_tile + 4) * block, cells), BF16)] * 2,
    )
    rays, mixed = call(
        functools.partial(primal_kernel, slices, bins, rows_tile),
        (signal, hits, footprint_table, near_weight, primal_state),
        (FAR, LISTS) + (FAR,) * 3,
        [
            shape_of((count, tables, height, UW), BF16),
            shape_of((2 * kept + (rows_tile + 4) * height, cells), BF16),
        ],
        [FAR] * 2,
        [
            VMEM((3 * tables + 1, height, UW), F32),
            VMEM(((rows_tile + 2) * block, cells), BF16),
        ],
    )
    rays = exchange(rays)
    new_volume, state_grad, payload = call(
        functools.partial(primal_rest_kernel, slices, rows_tile, blocks),
        (mixed, *tiles, rest_weight, biases),
        (FAR,) * 6,
        [
            shape_of(volume.shape, BF16),
            shape_of((rows_tile * rows, cells), F32),
            shape_of((count, 8, (per_primal + per_dual) * TILE + UW), BF16),
        ],
        [FAR, FAR, PASS],
        [VMEM(((rows_tile + 2) * block, cells), BF16)] * 2
        + [VMEM((count, 8, per_primal * TILE), BF16), pltpu.SemaphoreType.DMA((1,))],
    )
    dual_part, back_weight = call(
        functools.partial(dual_cot_kernel, slices, bins, near_rows),
        (*views, dual_inner, dual_outer),
        ranges(head, head + rows) + (FAR, FAR),
        [
            shape_of((3 * rows, detector), F32),
            shape_of((2 * rows + height, 9 * rows), BF16),
        ],
        [FAR] * 2,
        [VMEM((5 * block, detector), BF16)],
    )
    dual_grad, payload = call(
        functools.partial(dual_backward_kernel, slices, bins, per_dual, head, near_rows),
        (*views, rays, hits, back_weight, dual_part, slope, hidden, payload),
        ranges(0, near_rows) + (FAR, LISTS) + (FAR,) * 4 + (PASS,),
        [shape_of(dual_flat, BF16), shape_of(payload.shape, BF16)],
        [FAR, PASS],
        [
            VMEM((5 * columns, height, UW), F32),
            VMEM((3 * block, detector), BF16),
            VMEM((columns, height, UW), BF16),
            VMEM((count, 8, per_dual * TILE + UW), BF16),
            pltpu.SemaphoreType.DMA((1,)),
        ],
        alias={10: 1},
    )
    payload = exchange(payload)
    payload, signal = call(
        sum_kernel,
        (payload,),
        (HERE,),
        [shape_of((count, 8, width), BF16), shape_of((count, height, UW), BF16)],
        [HERE, HERE],
        limit=2 * 1024 * 1024,
    )
    payload = exchange(payload)
    (volume_grad,) = call(
        functools.partial(volume_grad_kernel, slices, bins),
        (signal, hits, bin_energy, basis_table, footprint_table, state_grad),
        (HERE, LISTS, LISTS, FAR, FAR, FAR),
        [shape_of(volume.shape, BF16)],
        [FAR],
        limit=4 * 1024 * 1024,
        scratch=[VMEM((tables + 1, height, UW), F32)],
    )
    gradients = call(
        functools.partial(unpack_kernel, slices, per_primal, per_dual),
        (payload,),
        (HERE,),
        [shape_of(w.shape, F32) for w in (primal_inner, primal_outer, dual_inner, dual_outer)],
        [FAR] * 4,
        limit=8 * 1024 * 1024,
    )
    return (
        new_volume,
        new_dual.reshape(dual_state.shape),
        volume_grad,
        dual_grad.reshape(dual_state.shape),
        *gradients,
    )


def solution(mesh):
    split = P(None, "parts", "view", None)
    in_specs = (split,) * 5 + (P(),) * 15
    out_specs = (split,) * 4 + (P("parts", None, None),) * 4
    return jax.shard_map(whole, mesh=mesh, in_specs=in_specs, out_specs=out_specs, check_vma=False)
```

```python
import functools

import jax
import jax.numpy as jnp
from jax import lax
from jax.experimental import pallas as pl
from jax.experimental.pallas import tpu as pltpu
from jax.sharding import PartitionSpec as P


UW = 128
TILE = 128
F32 = jnp.float32
BF16 = jnp.bfloat16
VMEM = pltpu.VMEM
SMEM = pltpu.SMEM


class Late:
    def __init__(self, ref, copy):
        self.ref, self.copy, self.shape = ref, copy, ref.shape

    def ready(self):
        if self.copy is not None:
            self.copy.wait()
            self.copy = None
        return self.ref

    def __getitem__(self, index):
        return self.ready()[index]


class Out:
    def __init__(self, ref, copy):
        self.ref, self.copy, self.shape, self.left = ref, copy, ref.shape, False

    def __getitem__(self, index):
        return self.ref[index]

    def __setitem__(self, index, value):
        self.ref[index] = value

    def flush(self):
        if not self.left:
            self.copy.start()
            self.left = True


class Wider:
    def __init__(self, far, sem):
        self.far, self.sem, self.copy = far, sem, None

    def flush_from(self, out):
        self.copy = pltpu.make_async_copy(out.ref, self.far.at[0 : out.shape[0]], self.sem)
        self.copy.start()


class Choice:
    def __init__(self, even, yes, no):
        self.even, self.yes, self.no, self.shape = even, yes, no, yes.shape

    def __getitem__(self, index):
        yes, no = self.yes[index], self.no[index]
        return jnp.where(self.even, yes.astype(F32), no.astype(F32)).astype(yes.dtype)


HERE = "vmem"
WIDER = "wider"
PASS = "pass"
LISTS = "smem"
FAR = "hbm"


def call(kernel, operands, places, out_shapes, out_places, scratch=(), limit=67_000_000, alias=None):
    total_in, total_out = len(operands), len(out_shapes)
    buffers = []
    for place, array in zip(list(places) + list(out_places), list(operands) + list(out_shapes)):
        if place not in (HERE, PASS, WIDER):
            kind = SMEM if place == LISTS else VMEM
            dims = array.shape
            if isinstance(place, tuple):
                dims = (place[1] - place[0],) + tuple(dims[1:])
            buffers.append(kind(dims, array.dtype))

    def body(*refs):
        given = refs[: total_in + total_out]
        own = refs[total_in + total_out :]
        local, sems, rest = own[: len(buffers)], own[len(buffers)], own[len(buffers) + 1 :]
        seen = []
        used = 0
        for index, place in enumerate(list(places) + list(out_places)):
            if place in (HERE, PASS):
                seen.append(given[index])
                continue
            if place == WIDER:
                seen.append(Wider(given[index], sems.at[len(buffers)]))
                continue
            near = local[used]
            far = given[index]
            if isinstance(place, tuple):
                far = far.at[place[0] : place[1]]
            if index < total_in:
                copy = pltpu.make_async_copy(far, near, sems.at[used])
                copy.start()
                seen.append(Late(near, copy))
            else:
                seen.append(Out(near, pltpu.make_async_copy(near, far, sems.at[used])))
            used += 1
        kernel(*seen, *rest)
        for item in seen[:total_in]:
            if isinstance(item, Late):
                item.ready()
        for item in seen[total_in:]:
            if isinstance(item, Out):
                item.flush()
        for item in seen[total_in:]:
            if isinstance(item, (Out, Wider)):
                item.copy.wait()

    def spec(place):
        return pl.BlockSpec(memory_space=VMEM if place == HERE else pltpu.HBM)

    return pl.pallas_call(
        body,
        out_shape=out_shapes,
        in_specs=[spec(place) for place in places],
        out_specs=[spec(place) for place in out_places],
        scratch_shapes=buffers + [pltpu.SemaphoreType.DMA((len(buffers) + 1,))] + list(scratch),
        compiler_params=pltpu.CompilerParams(vmem_limit_bytes=limit),
        cost_estimate=pl.CostEstimate(flops=10**8, bytes_accessed=10**6, transcendentals=0),
        input_output_aliases=alias or {},
    )(*operands)


def shape_of(dims, kind):
    return jax.ShapeDtypeStruct(dims, kind)


def dot(left, right):
    return jnp.dot(left, right, preferred_element_type=F32)


def dot_nt(left, right):
    return lax.dot_general(left, right, (((1,), (1,)), ((), ())), preferred_element_type=F32)


def shifted(wide):
    lanes = wide.shape[1]
    lane = lax.broadcasted_iota(jnp.int32, wide.shape, 1)
    low = jnp.where(lane == 0, 0.0, pltpu.roll(wide, 1, 1))
    high = jnp.where(lane == lanes - 1, 0.0, pltpu.roll(wide, lanes - 1, 1))
    return low, wide, high


def put_columns(column_ref, row, plane, slices):
    channels = plane.shape[0] // slices
    block = 3 * plane.shape[0]
    for tap, moved in enumerate(shifted(plane.astype(F32))):
        moved = moved.astype(BF16)
        for z in range(slices):
            start = row * block + (z * 3 + tap) * channels
            column_ref[start : start + channels, :] = moved[z * channels : (z + 1) * channels]


def window(column_ref, row, block):
    return column_ref[(row - 1) * block : (row + 2) * block, :]


def sigmoid(values):
    return 1.0 / (1.0 + jnp.exp(-values))


def spread_lists(gradient, slices, taps_z=3):
    channels = gradient.shape[0] // slices
    parts = []
    for z_in in range(slices):
        rows = []
        for i in range(taps_z):
            z_out = z_in - i + 1
            if 0 <= z_out < slices:
                rows.append(gradient[z_out * channels : (z_out + 1) * channels])
            else:
                rows.append(jnp.zeros((channels, gradient.shape[1]), BF16))
        parts.append(jnp.concatenate(rows, axis=0))
    return parts


def moved_gradient(gradient, slices):
    low, here, high = shifted(gradient.astype(F32))
    versions = [spread_lists(part.astype(BF16), slices) for part in (high, here, low)]
    return [
        jnp.concatenate([version[z] for version in versions], axis=0) for z in range(slices)
    ]


def state_wgrad(moved, planes, slices):
    channels = planes[0].shape[0] // slices
    total = None
    for z in range(slices):
        around = jnp.concatenate(
            [plane[z * channels : (z + 1) * channels] for plane in planes], axis=0
        )
        term = dot_nt(moved[z], around)
        total = term if total is None else total + term
    return total


def tap_of(i, j, l):
    return (i * 3 + j) * 3 + l


def forward_weight(weight_ref, slices, low, high, lane_major):
    rows = []
    for z in range(slices):
        pieces = []
        for j in range(3):
            pairs = [(zi, l) for zi in range(slices) for l in range(3)]
            if lane_major:
                pairs = [(zi, l) for l in range(3) for zi in range(slices)]
            for zi, l in pairs:
                i = zi - z + 1
                if 0 <= i < 3:
                    pieces.append(weight_ref[tap_of(i, j, l)].astype(F32)[:, low:high])
                else:
                    pieces.append(jnp.zeros((weight_ref.shape[1], high - low), F32))
        rows.append(jnp.concatenate(pieces, axis=1))
    return jnp.concatenate(rows, axis=0).astype(BF16)


def adjoint_weight(weight_ref, slices, low, high, first=0, last=None, lane_major=False):
    last = weight_ref.shape[1] if last is None else last
    rows = []
    for j in range(3):
        pairs = [(z, l) for z in range(slices) for l in range(3)]
        if lane_major:
            pairs = [(z, l) for l in range(3) for z in range(slices)]
        for z, l in pairs:
            pieces = []
            for zi in range(slices):
                i = zi - z + 1
                if 0 <= i < 3:
                    tap = weight_ref[tap_of(i, 2 - j, 2 - l)].astype(F32)
                    pieces.append(tap[first:last, low:high])
                else:
                    pieces.append(jnp.zeros((last - first, high - low), F32))
            rows.append(jnp.concatenate(pieces, axis=1))
    return jnp.concatenate(rows, axis=0).T.astype(BF16)


def arrived(*refs):
    return [ref.ready() if isinstance(ref, Late) else ref for ref in refs]


def as_column(values):
    count = values.shape[0]
    square = jnp.broadcast_to(values[None, :], (count, count))
    row = lax.broadcasted_iota(jnp.int32, square.shape, 0)
    col = lax.broadcasted_iota(jnp.int32, square.shape, 1)
    return jnp.sum(jnp.where(row == col, square, 0.0), axis=1, keepdims=True)


def code_hits(tile_ref, table_ref, column_ref, count_ref):
    tiles = tile_ref[...]
    count = as_column(count_ref[...].astype(F32))
    live = lax.broadcasted_iota(jnp.int32, tiles.shape, 1).astype(F32) < count
    codes = table_ref[...] * 16 + column_ref[...]
    position = lax.axis_index("view")
    found = [(tiles * 256 + codes).astype(F32), count]
    for slot in range(3):
        hit = live & (tiles == position + slot - 1)
        found.append(
            jnp.sum(jnp.where(hit, codes.astype(F32) + 1.0, 0.0), axis=1, keepdims=True) - 1.0
        )
    return jnp.concatenate(found, axis=1).astype(jnp.int32)


def mixing_of(energy_ref, basis_ref, bins):
    (energy_ref,) = arrived(energy_ref)
    energies = basis_ref.shape[0]
    row = lax.broadcasted_iota(jnp.int32, (bins, energies), 0)
    col = lax.broadcasted_iota(jnp.int32, (bins, energies), 1)
    onehot = jnp.zeros((bins, energies), F32)
    for n in range(bins):
        onehot = jnp.where((row == n) & (col == energy_ref[n]), 1.0, onehot)
    return dot(onehot.astype(BF16), basis_ref[...])


def send_rays(images, footprint_ref, send_ref):
    for table in range(footprint_ref.shape[0]):
        rays = dot(images, footprint_ref[table]).astype(BF16)
        for target in range(send_ref.shape[0]):
            send_ref[target, table] = rays


def pack_kernel(
    dual_ref,
    cot_dual_ref,
    sino_ref,
    volume_ref,
    energy_ref,
    basis_ref,
    footprint_ref,
    cot_volume_ref,
    pack_ref,
    near_ref,
    send_ref,
    cells_ref,
):
    channels, slices, rows_tile, _ = volume_ref.shape
    bins = sino_ref.shape[0]
    rows = slices * channels
    head = head_rows(rows, slices * bins)
    sino_rows = []
    for z in range(slices):
        at = z * channels
        pack_ref[at : at + channels, :] = dual_ref[:, z, :]
        at = head + z * channels
        pack_ref[at : at + channels, :] = cot_dual_ref[:, z, :]
        sino_rows.append(sino_ref[:, z, :].astype(F32))
    sino_rows.append(jnp.zeros((head - rows - slices * bins, sino_ref.shape[2]), F32))
    pack_ref[rows:head, :] = jnp.concatenate(sino_rows, axis=0).astype(BF16)
    near_ref.flush_from(pack_ref)
    pack_ref.flush()
    at = 0
    for source in (volume_ref, cot_volume_ref):
        for r in range(rows_tile):
            for z in range(slices):
                cells_ref[at : at + channels, :] = source[:, z, r, :]
                at += channels
        if source is volume_ref:
            mixing = mixing_of(energy_ref, basis_ref, bins).astype(BF16)
            images = []
            for z in range(slices):
                line = []
                for r in range(rows_tile):
                    first = (r * slices + z) * channels
                    line.append(dot(mixing, cells_ref[first : first + channels, :]))
                images.append(jnp.concatenate(line, axis=1))
            send_rays(jnp.concatenate(images, axis=0).astype(BF16), footprint_ref, send_ref)
            send_ref.flush()


def head_rows(rows, height):
    return rows + pl.cdiv(height, 16) * 16


def weights_kernel(
    slices,
    tile_ref,
    table_ref,
    column_ref,
    count_ref,
    di,
    do,
    bias_0,
    bias_1,
    bias_2,
    bias_3,
    weight_ref,
    bias_ref,
    hits_ref,
):
    channels = do.shape[1]
    hits_ref[...] = code_hits(tile_ref, table_ref, column_ref, count_ref)
    columns = [column_bias(bias, slices) for bias in (bias_0, bias_1, bias_2, bias_3)]
    bias_ref[...] = jnp.concatenate(columns, axis=1)
    weight_ref[...] = jnp.concatenate(
        [
            forward_weight(di, slices, 0, channels, False),
            forward_weight(do, slices, 0, channels, False),
            forward_weight(di, slices, channels, di.shape[2], True),
        ],
        axis=1,
    )


def ray_windows(rays_ref, hits_ref, sums_ref, views):
    rays_ref, hits_ref = arrived(rays_ref, hits_ref)
    blocks, entries = hits_ref.shape[0], hits_ref.shape[1] - 4
    columns = sums_ref.shape[0] // len(views)
    sums_ref[...] = jnp.zeros_like(sums_ref)
    for place, offset in enumerate(views):
        view = lax.rem(lax.axis_index("view") + offset + blocks, blocks)

        def each_entry(k, carry):
            code = hits_ref[view, k]
            at = place * columns + lax.rem(code, 16)
            table = lax.rem(lax.div(code, 16), 16)
            sums_ref[at] += rays_ref[lax.div(code, 256), table].astype(F32)
            return carry

        lax.fori_loop(0, hits_ref[view, entries], each_entry, 0)
    return [
        jnp.concatenate([sums_ref[place * columns + c] for c in range(columns)], axis=1)
        for place in range(len(views))
    ]


def extra_rows(projected, sino, slices, bins):
    rows = []
    for z in range(slices):
        rows.append(projected[z * bins : (z + 1) * bins])
        rows.append(sino[z * bins : (z + 1) * bins])
    return jnp.concatenate(rows, axis=0)


def extra_columns(pieces):
    return jnp.concatenate([piece for triple in pieces for piece in triple], axis=0).astype(BF16)


def column_bias(bias_ref, slices):
    return jnp.concatenate([as_column(bias_ref[...])] * slices, axis=0)


def five_views(own, beside, far, over, low, gap):
    even = lax.rem(lax.axis_index("view"), 2) == 0
    own, beside, across = Rows(own, low), Rows(beside, low), Rows(far, low)
    two, over = Rows(far, low + gap), Rows(over, low)
    return (
        Choice(even, two, over),
        Choice(even, across, beside),
        own,
        Choice(even, beside, across),
        Choice(even, over, two),
    )


class Rows:
    def __init__(self, source, first):
        self.source, self.first, self.shape = source, first, source.shape

    def __getitem__(self, index):
        rows, lanes = index
        return self.source[rows.start + self.first : rows.stop + self.first, lanes]


class Valid:
    def __init__(self, valid, source):
        self.valid, self.source, self.shape = valid, source, source.shape

    def __getitem__(self, index):
        values = self.source[index]
        return jnp.where(self.valid, values.astype(F32), 0.0).astype(values.dtype)


def three_tiles(blocks, own, beside, across):
    even = lax.rem(lax.axis_index("view"), 2) == 0
    return (
        Valid(lax.axis_index("view") > 0, Choice(even, across, beside)),
        own,
        Valid(lax.axis_index("view") < blocks - 1, Choice(even, beside, across)),
    )


def dual_forward_kernel(
    slices,
    bins,
    gap,
    pack_ref,
    beside_ref,
    far_ref,
    over_ref,
    rays_ref,
    hits_ref,
    weight_ref,
    bias_ref,
    send_ref,
    slope_ref,
    hidden_ref,
    new_ref,
    sums_ref,
    columns_ref,
    hidden_columns,
    windows_ref,
    ready_ref,
    sem,
):
    around = five_views(pack_ref, beside_ref, far_ref, over_ref, 0, gap)
    channels = new_ref.shape[0]
    rows = channels * slices
    height = slices * bins
    for row in range(5):
        put_columns(columns_ref, row, around[row][0:rows, :], slices)
    projected = ray_windows(rays_ref, hits_ref, sums_ref, (-2, -1, 0, 1, 2))
    bias_inner, bias_outer = bias_ref[:, 0:1], bias_ref[:, 1:2]
    w1s = weight_ref[:, 0 : 9 * rows]
    w2 = weight_ref[:, 9 * rows : 18 * rows]
    w1e = weight_ref[:, 18 * rows :]
    pieces = []
    for row in range(5):
        extra = extra_rows(
            projected[row].astype(BF16).astype(F32),
            around[row][rows : rows + height, :].astype(F32),
            slices,
            bins,
        )
        if 1 <= row <= 3:
            at = 3 * rows + (row - 1) * extra.shape[0]
            hidden_ref[at : at + extra.shape[0], :] = extra.astype(BF16)
        pieces.append(shifted(extra))
    for row in range(3):
        at = row * rows
        pre = dot(w1s, window(columns_ref, row + 1, 3 * rows))
        pre = pre + dot(w1e, extra_columns(pieces[row : row + 3])) + bias_inner
        gate = sigmoid(pre)
        hidden = (pre * gate).astype(BF16)
        hidden_ref[at : at + rows, :] = hidden
        slope_ref[at : at + rows, :] = gate * (1.0 + pre * (1.0 - gate))
        put_columns(hidden_columns, row, hidden, slices)
    slope_ref.flush()
    hidden_ref.flush()
    update = dot(w2, hidden_columns[...]) + bias_outer
    fresh = (around[2][0:rows, :].astype(F32) + update).astype(BF16)
    out = []
    for z in range(slices):
        plane = fresh[z * channels : (z + 1) * channels]
        new_ref[:, z, :] = plane
        out.append(plane.astype(F32)[:bins])
    new_ref.flush()
    out = jnp.concatenate(out, axis=0).astype(BF16)
    for column in range(out.shape[1] // UW):
        windows_ref[column] = out[:, column * UW : (column + 1) * UW]
    (hits,) = arrived(hits_ref)
    view = lax.axis_index("view")

    def each_entry(k, carry):
        code = hits[view, k]
        tile = lax.div(code, 256)
        values = windows_ref[lax.rem(code, 16)]
        for slot in range(3):
            ready_ref[tile + 2 - slot, slot] = values
        return carry

    lax.fori_loop(0, hits[view, hits.shape[1] - 4], each_entry, 0)
    copy = pltpu.make_async_copy(ready_ref.at[1 : 1 + send_ref.shape[0]], send_ref, sem.at[0])
    copy.start()
    copy.wait()


def gather_signals(signal_ref, code_ref, slots, footprint_ref, sums_ref, chosen=False):
    signal_ref, code_ref = arrived(signal_ref, code_ref)
    first = code_ref.shape[1] - 3
    tables = footprint_ref.shape[0]
    spare = len(slots) * tables
    sums_ref[...] = jnp.zeros_like(sums_ref)

    def each_block(b, carry):
        for place, slot in enumerate(slots):
            code = code_ref[b, first + slot]
            live = code >= 0
            code = jnp.maximum(code, 0)
            at = jnp.where(live, place * tables + lax.div(code, 16), spare)
            sums_ref[at] += (signal_ref[b] if chosen else signal_ref[b, slot]).astype(F32)
        return carry

    lax.fori_loop(0, signal_ref.shape[0], each_block, 0)
    total = None
    for table in range(tables):
        grouped = jnp.concatenate(
            [sums_ref[place * tables + table] for place in range(len(slots))], axis=0
        )
        high = grouped.astype(BF16).astype(F32)
        both = jnp.concatenate([high, grouped - high], axis=0).astype(BF16)
        term = dot_nt(both, footprint_ref[table])
        total = term if total is None else total + term
    half = total.shape[0] // 2
    return total[:half] + total[half:]


def fold_lanes(array):
    full = array.shape[1] // TILE * TILE
    rest = array.shape[1] - full
    if rest == 0:
        return [array]
    copies = TILE // rest
    while array.shape[0] % (8 * copies):
        copies -= 1
    rows = array.shape[0] // copies
    side = [array[c * rows : (c + 1) * rows, full:] for c in range(copies)]
    side = jnp.concatenate(side, axis=1) if copies > 1 else side[0]
    return ([array[:, :full]] if full else []) + [side]


def fold_shapes(rows, width):
    full = width // TILE * TILE
    rest = width - full
    if rest == 0:
        return [(rows, width)], 1
    copies = TILE // rest
    while rows % (8 * copies):
        copies -= 1
    return ([(rows, full)] if full else []) + [(rows // copies, rest * copies)], copies


def tile_count(rows, width):
    shapes, _ = fold_shapes(rows, width)
    return sum(r // 8 * pl.cdiv(w, TILE) for r, w in shapes)


def put_payload(payload_ref, per, first, array):
    flat = first
    for part in fold_lanes(array):
        width = part.shape[1]
        for group in range(part.shape[0] // 8):
            for tile in range(pl.cdiv(width, TILE)):
                last = min(width, (tile + 1) * TILE)
                lane = (flat % per) * TILE
                payload_ref[flat // per, :, lane : lane + last - tile * TILE] = part[
                    group * 8 : group * 8 + 8, tile * TILE : last
                ].astype(BF16)
                flat += 1
    return flat


def take_payload(payload_ref, per, first, rows, width):
    flat = first
    shapes, copies = fold_shapes(rows, width)
    parts = []
    for part_rows, part_width in shapes:
        groups = []
        for _ in range(part_rows // 8):
            tiles = []
            for _ in range(pl.cdiv(part_width, TILE)):
                lane = (flat % per) * TILE
                tiles.append(payload_ref[flat // per, :, lane : lane + TILE].astype(F32))
                flat += 1
            groups.append(jnp.concatenate(tiles, axis=1) if len(tiles) > 1 else tiles[0])
        parts.append(jnp.concatenate(groups, axis=0))
    rest = width % TILE
    if rest:
        side = parts.pop()
        parts.append(
            jnp.concatenate([side[:, c * rest : (c + 1) * rest] for c in range(copies)], axis=0)
        )
    return (jnp.concatenate(parts, axis=1) if len(parts) > 1 else parts[0]), flat


def row_plane(tiles, row, which, rows, rows_tile):
    ref, r = tiles[row // rows_tile], row % rows_tile
    at = (which * rows_tile + r) * rows
    return ref[at : at + rows, :]


def primal_state_kernel(
    slices,
    rows_tile,
    blocks,
    v0,
    v1,
    v2,
    inner_ref,
    outer_ref,
    bias_ref,
    state_ref,
    near_weight,
    columns_ref,
    cot_columns,
):
    tiles = three_tiles(blocks, v0, v1, v2)
    channels = outer_ref.shape[1]
    rows = channels * slices
    bins = inner_ref.shape[2] - channels
    w1s = forward_weight(inner_ref, slices, 0, channels, False)
    w2t = adjoint_weight(outer_ref, slices, 0, channels)
    thin = slices * bins
    near_weight[0:thin, :] = adjoint_weight(inner_ref, slices, channels, channels + bins)
    near_weight[thin : thin + rows, 0 : 9 * thin] = forward_weight(
        inner_ref, slices, channels, inner_ref.shape[2], True
    )
    bias = bias_ref[:, 2:3]
    kept = (rows_tile + 2) * rows
    first = rows_tile - 2
    for row in range(rows_tile + 4):
        at = first + row
        put_columns(columns_ref, row, row_plane(tiles, at, 0, rows, rows_tile), slices)
        put_columns(cot_columns, row, row_plane(tiles, at, 1, rows, rows_tile), slices)
    for row in range(rows_tile + 2):
        pre = dot(w1s, window(columns_ref, row + 1, 3 * rows)) + bias
        state_ref[row * rows : (row + 1) * rows, :] = pre
        gradient = dot(w2t, window(cot_columns, row + 1, 3 * rows))
        state_ref[kept + row * rows : kept + (row + 1) * rows, :] = gradient


def primal_kernel(
    slices,
    bins,
    rows_tile,
    signal_ref,
    code_ref,
    footprint_ref,
    weight_ref,
    state_ref,
    send_ref,
    mixed_ref,
    sums_ref,
    grad_columns,
):
    blocks = send_ref.shape[0]
    lanes = state_ref.shape[1]
    thin = slices * bins
    rows = weight_ref.shape[0] - thin
    kept = (rows_tile + 2) * rows
    position = lax.axis_index("view")
    height = slices * bins
    back = gather_signals(signal_ref, code_ref, (0, 1, 2), footprint_ref, sums_ref)
    back = back.astype(BF16).astype(F32)
    pieces = []
    for row in range(rows_tile + 4):
        at = row + rows_tile - 2
        tile, r = at // rows_tile, at % rows_tile
        extra = back[tile * height : (tile + 1) * height, r * lanes : (r + 1) * lanes]
        at = 2 * kept + row * height
        mixed_ref[at : at + height, :] = extra.astype(BF16)
        pieces.append(shifted(extra))
    w1x = weight_ref[0:thin, :]
    w1e = weight_ref[thin : thin + rows, 0 : 9 * thin]
    for row in range(rows_tile + 2):
        at = row * rows
        pre = state_ref[at : at + rows, :] + dot(w1e, extra_columns(pieces[row : row + 3]))
        gate = sigmoid(pre)
        hidden = pre * gate
        gradient = state_ref[kept + at : kept + at + rows, :] * (gate * (1.0 + pre * (1.0 - gate)))
        if row == 0:
            hidden = jnp.where(position > 0, hidden, 0.0)
            gradient = jnp.where(position > 0, gradient, 0.0)
        if row == rows_tile + 1:
            hidden = jnp.where(position < blocks - 1, hidden, 0.0)
            gradient = jnp.where(position < blocks - 1, gradient, 0.0)
        gradient = gradient.astype(BF16)
        mixed_ref[at : at + rows, :] = hidden.astype(BF16)
        mixed_ref[kept + at : kept + at + rows, :] = gradient
        put_columns(grad_columns, row, gradient, slices)
    mixed_ref.flush()
    parts = []
    for row in range(rows_tile):
        parts.append(dot(w1x, window(grad_columns, row + 1, 3 * rows)))
    send_rays(jnp.concatenate(parts, axis=1).astype(BF16), footprint_ref, send_ref)


def primal_rest_kernel(
    slices, rows_tile, blocks, rows, mixed_ref, v0, v1, v2, payload_ref, ready_ref, sem
):
    tiles = three_tiles(blocks, v0, v1, v2)
    kept = (rows_tile + 2) * rows
    height = (mixed_ref.shape[0] - 2 * kept) // (rows_tile + 4)
    hidden_ref, gradient_ref = mixed_ref, Rows(mixed_ref, kept)
    pieces = [
        shifted(
            mixed_ref[2 * kept + row * height : 2 * kept + (row + 1) * height, :].astype(F32)
        )
        for row in range(1, rows_tile + 3)
    ]
    inner = None
    outer = None
    extra_total = None
    for r in range(rows_tile):
        at = (r + 1) * rows
        cot = row_plane(tiles, rows_tile + r, 1, rows, rows_tile)
        gradient = gradient_ref[at : at + rows, :]
        planes = [
            row_plane(tiles, rows_tile - 1 + r + j, 0, rows, rows_tile) for j in range(3)
        ]
        term = state_wgrad(moved_gradient(gradient, slices), planes, slices)
        inner = term if inner is None else inner + term
        planes = [hidden_ref[(r + j) * rows : (r + j + 1) * rows, :] for j in range(3)]
        term = state_wgrad(moved_gradient(cot, slices), planes, slices)
        outer = term if outer is None else outer + term
        term = dot_nt(gradient, extra_columns(pieces[r : r + 3]))
        extra_total = term if extra_total is None else extra_total + term
    per = ready_ref.shape[2] // TILE
    flat = put_payload(ready_ref, per, 0, jnp.concatenate([inner, outer], axis=1))
    put_payload(ready_ref, per, flat, extra_total)
    copy = pltpu.make_async_copy(ready_ref, payload_ref.at[:, :, 0 : per * TILE], sem.at[0])
    copy.start()
    copy.wait()


def dual_cot_kernel(
    slices,
    bins,
    gap,
    c0,
    c1,
    c2,
    c3,
    inner_ref,
    outer_ref,
    part_ref,
    weight_ref,
    columns_ref,
):
    around = five_views(c0, c1, c2, c3, 0, gap)
    rows = c0.shape[0]
    thin = slices * bins
    channels = rows // slices
    w2t = adjoint_weight(outer_ref, slices, 0, channels)
    weight_ref[0:rows, :] = adjoint_weight(inner_ref, slices, 0, channels)
    weight_ref[rows : rows + thin, :] = adjoint_weight(inner_ref, slices, channels, channels + bins)
    weight_ref[rows + thin : 2 * rows + thin, 0 : 9 * thin] = adjoint_weight(
        outer_ref, slices, 0, channels, 0, bins, True
    )
    for row in range(5):
        plane = around[row][0:rows, :].astype(F32)
        channel = lax.broadcasted_iota(jnp.int32, plane.shape, 0)
        plane = jnp.where(lax.rem(channel, channels) < bins, 0.0, plane)
        put_columns(columns_ref, row, plane, slices)
    for row in range(3):
        at = row * rows
        part_ref[at : at + rows, :] = dot(w2t, window(columns_ref, row + 1, 3 * rows))


def dual_backward_kernel(
    slices,
    bins,
    per,
    low,
    gap,
    pack_ref,
    beside_ref,
    far_ref,
    over_ref,
    rays_ref,
    hits_ref,
    weight_ref,
    part_ref,
    slope_ref,
    hidden_ref,
    payload_in,
    grad_ref,
    payload_ref,
    sums_ref,
    grad_columns,
    windows_ref,
    ready_ref,
    sem,
):
    del payload_in
    around = five_views(pack_ref, beside_ref, far_ref, over_ref, low, gap)
    states = five_views(pack_ref, beside_ref, far_ref, over_ref, 0, gap)[1:4]
    channels = grad_ref.shape[0]
    rows = channels * slices
    thin = slices * bins
    toward = ray_windows(rays_ref, hits_ref, sums_ref, (-2, -1, 0, 1, 2))
    w1t = weight_ref[0:rows, :]
    w1x = weight_ref[rows : rows + thin, :]
    w2x = weight_ref[rows + thin : 2 * rows + thin, 0 : 9 * thin]
    pieces = []
    own_head = None
    for row in range(5):
        head = jnp.concatenate(
            [
                around[row][z * channels : z * channels + 2 * bins, :].astype(F32)[:bins]
                for z in range(slices)
            ],
            axis=0,
        )
        head = head + toward[row]
        if row == 2:
            own_head = head
        pieces.append(shifted(head.astype(BF16).astype(F32)))
    spread = []
    lanes = own_head.shape[1]
    for z in range(slices):
        spread.append(own_head[z * bins : (z + 1) * bins])
        spread.append(around[2][z * channels : (z + 1) * channels, :].astype(F32)[bins:])
    own_total = jnp.concatenate(spread, axis=0)
    own_cot = own_total.astype(BF16)
    own_gradient = None
    for row in range(3):
        at = row * rows
        gradient = part_ref[at : at + rows, :] + dot(w2x, extra_columns(pieces[row : row + 3]))
        gradient = (gradient * slope_ref[at : at + rows, :]).astype(BF16)
        put_columns(grad_columns, row, gradient, slices)
        if row == 1:
            own_gradient = gradient
    out = dot(w1x, grad_columns[...]).astype(BF16)
    for column in range(lanes // UW):
        windows_ref[column] = out[:, column * UW : (column + 1) * UW]
    start = per * TILE
    ready_ref[:, :, start : start + UW] = jnp.zeros(
        (ready_ref.shape[0], ready_ref.shape[1], UW), BF16
    )
    view = lax.axis_index("view")
    (hits,) = arrived(hits_ref)

    def each_entry(k, carry):
        code = hits[view, k]
        ready_ref[lax.div(code, 256), :, start : start + UW] = windows_ref[lax.rem(code, 16)]
        return carry

    lax.fori_loop(0, hits[view, hits.shape[1] - 4], each_entry, 0)
    planes = [states[row][0:rows, :] for row in range(3)]
    inner = state_wgrad(moved_gradient(own_gradient, slices), planes, slices)
    planes = [hidden_ref[row * rows : (row + 1) * rows, :] for row in range(3)]
    outer = state_wgrad(moved_gradient(own_cot, slices), planes, slices)
    height = (hidden_ref.shape[0] - 3 * rows) // 3
    pieces = []
    for row in range(3):
        at = 3 * rows + row * height
        pieces.append(shifted(hidden_ref[at : at + height, :].astype(F32)))
    extra = dot_nt(own_gradient, extra_columns(pieces))
    flat = put_payload(ready_ref, per, 0, jnp.concatenate([inner, outer], axis=1))
    put_payload(ready_ref, per, flat, extra)
    total = payload_ref.shape[2]
    copy = pltpu.make_async_copy(
        ready_ref, payload_ref.at[:, :, total - ready_ref.shape[2] : total], sem.at[0]
    )
    copy.start()
    state = (dot(w1t, grad_columns[...]) + own_total).astype(BF16)
    for z in range(slices):
        grad_ref[:, z, :] = state[z * channels : (z + 1) * channels]
    grad_ref.flush()
    copy.wait()


def sum_kernel(payload_ref, send_ref, rays_ref):
    width = send_ref.shape[2]
    total = payload_ref[0, :, 0:width].astype(F32)
    for source in range(1, payload_ref.shape[0]):
        total = total + payload_ref[source, :, 0:width].astype(F32)
    total = total.astype(BF16)
    for target in range(send_ref.shape[0]):
        send_ref[target] = total
    rays_ref[...] = payload_ref[:, :, width:]


def volume_grad_kernel(
    slices,
    bins,
    rows_tile,
    mixed_ref,
    cells_ref,
    inner_ref,
    outer_ref,
    bias_ref,
    footprint_ref,
    energy_ref,
    basis_ref,
    signal_ref,
    code_ref,
    new_ref,
    out_ref,
    hidden_columns,
    grad_columns,
    state_ref,
    sums_ref,
):
    channels = new_ref.shape[0]
    rows = channels * slices
    lanes = mixed_ref.shape[1]
    kept = (rows_tile + 2) * rows
    for row in range(rows_tile + 2):
        at = row * rows
        put_columns(hidden_columns, row, mixed_ref[at : at + rows, :], slices)
        put_columns(grad_columns, row, mixed_ref[kept + at : kept + at + rows, :], slices)
    w2 = forward_weight(outer_ref, slices, 0, channels, False)
    w1t = adjoint_weight(inner_ref, slices, 0, channels)
    bias = bias_ref[:, 3:4]
    for r in range(rows_tile):
        at = r * rows
        update = dot(w2, window(hidden_columns, r + 1, 3 * rows)) + bias
        fresh = (cells_ref[at : at + rows, :].astype(F32) + update).astype(BF16)
        for z in range(slices):
            new_ref[:, z, r, :] = fresh[z * channels : (z + 1) * channels]
        cot = cells_ref[rows_tile * rows + at : rows_tile * rows + at + rows, :].astype(F32)
        state_ref[at : at + rows, :] = dot(w1t, window(grad_columns, r + 1, 3 * rows)) + cot
    new_ref.flush()
    back = gather_signals(signal_ref, code_ref, (1,), footprint_ref, sums_ref, chosen=True)
    mixing = mixing_of(energy_ref, basis_ref, bins)
    for z in range(slices):
        part = back[z * bins : (z + 1) * bins]
        high = part.astype(BF16).astype(F32)
        low = part - high
        spread = lax.dot_general(
            jnp.concatenate([mixing, mixing], axis=0).astype(BF16),
            jnp.concatenate([high, low], axis=0).astype(BF16),
            (((0,), (0,)), ((), ())),
            preferred_element_type=F32,
        )
        for r in range(rows_tile):
            at = (r * slices + z) * channels
            total = state_ref[at : at + channels, :] + spread[:, r * lanes : (r + 1) * lanes]
            out_ref[:, z, r, :] = total.astype(BF16)


class Region:
    def __init__(self, ref, first):
        self.ref, self.first = ref, first

    def __getitem__(self, index):
        chunk, rows, lanes = index
        return self.ref[chunk, rows, lanes.start + self.first : lanes.stop + self.first]


def unpack_kernel(
    slices, per_primal, per_dual, payload_ref, primal_inner, primal_outer, dual_inner, dual_outer
):
    channels = dual_outer.shape[1]
    for inner_ref, outer_ref, per, first in (
        (primal_inner, primal_outer, per_primal, 0),
        (dual_inner, dual_outer, per_dual, per_primal * TILE),
    ):
        region = Region(payload_ref, first)
        flat = 0
        extra_count = inner_ref.shape[2] - channels
        state, flat = take_payload(region, per, flat, 9 * channels, 6 * channels)
        extra, flat = take_payload(region, per, flat, slices * channels, 9 * slices * extra_count)
        for i in range(3):
            for j in range(3):
                for l in range(3):
                    tap = (i * 3 + j) * 3 + l
                    lane = j * channels
                    rows = state[(l * 3 + i) * channels : (l * 3 + i + 1) * channels]
                    more = None
                    for z in range(slices):
                        z_in = z + i - 1
                        if 0 <= z_in < slices:
                            at = ((j * 3 + l) * slices + z_in) * extra_count
                            term = extra[z * channels : (z + 1) * channels, at : at + extra_count]
                            more = term if more is None else more + term
                    inner_ref[tap] = jnp.concatenate(
                        [rows[:, lane : lane + channels], more], axis=1
                    )
                    lane = lane + 3 * channels
                    outer_ref[tap] = rows[:, lane : lane + channels]
        inner_ref.flush()
        outer_ref.flush()


def whole(
    volume,
    dual_state,
    sinogram,
    cot_volume,
    cot_dual,
    basis_table,
    bin_energy,
    footprint_table,
    hit_tile,
    hit_table,
    hit_column,
    hit_count,
    primal_inner,
    primal_inner_bias,
    primal_outer,
    primal_outer_bias,
    dual_inner,
    dual_inner_bias,
    dual_outer,
    dual_outer_bias,
):
    count = lax.axis_size("view")
    channels, slices, rows_tile, cells = volume.shape
    bins = sinogram.shape[0]
    detector = dual_state.shape[3]
    columns = detector // UW
    tables = footprint_table.shape[0]
    blocks, entries = hit_tile.shape
    height = slices * bins
    rows = slices * channels
    block = 3 * rows
    lists = (hit_tile, hit_table, hit_column, hit_count)
    list_places = (LISTS,) * 4

    def exchange(array):
        return lax.all_to_all(array, "view", split_axis=0, concat_axis=0)

    def swap(array):
        return lax.ppermute(array, "view", [(k, k ^ 1) for k in range(count)])

    def cross(array, periodic):
        pairs = []
        for k in range(1, count, 2):
            if periodic or k + 1 < count:
                pairs += [(k, (k + 1) % count), ((k + 1) % count, k)]
        return lax.ppermute(array, "view", pairs)

    head = head_rows(rows, height)
    near_rows = head + rows
    dual_flat = (channels, slices, detector)
    pack, near, rays, tile = call(
        pack_kernel,
        (dual_state.reshape(dual_flat), cot_dual.reshape(dual_flat))
        + (sinogram.reshape(bins, slices, detector), volume, bin_energy, basis_table)
        + (footprint_table, cot_volume),
        (FAR,) * 4 + (LISTS,) + (FAR,) * 3,
        [
            shape_of((near_rows, detector), BF16),
            shape_of((2 * near_rows, detector), BF16),
            shape_of((count, tables, height, UW), BF16),
            shape_of((2 * rows_tile * rows, cells), BF16),
        ],
        [FAR, WIDER, FAR, FAR],
    )
    beside = swap(pack)
    rays = exchange(rays)
    near = lax.dynamic_update_slice(near, beside, (near_rows, 0))
    far = cross(near, True)
    tiles = (tile, swap(tile), cross(tile, False))
    over = swap(far)
    views = (pack, beside, far, over)

    def ranges(first, last):
        return ((first, last), (first, last), (first, near_rows + last), (first, last))

    wide = shape_of((rows, 9 * rows), BF16)
    extra_dual = dual_inner.shape[2] - channels
    extra_primal = primal_inner.shape[2] - channels
    dual_weight, biases, hits = call(
        functools.partial(weights_kernel, slices),
        (*lists, dual_inner, dual_outer, dual_inner_bias, dual_outer_bias)
        + (primal_inner_bias, primal_outer_bias),
        (FAR,) * 10,
        [
            shape_of((rows, 18 * rows + 9 * slices * extra_dual), BF16),
            shape_of((rows, 4), F32),
            shape_of((blocks, entries + 4), jnp.int32),
        ],
        [FAR] * 3,
    )
    signal, slope, hidden, new_dual = call(
        functools.partial(dual_forward_kernel, slices, bins, near_rows),
        (*views, rays, hits, dual_weight, biases),
        ranges(0, head) + (FAR, LISTS, FAR, FAR),
        [
            shape_of((count, 3, height, UW), BF16),
            shape_of((3 * rows, detector), F32),
            shape_of((3 * (rows + 2 * height), detector), BF16),
            shape_of(dual_flat, BF16),
        ],
        [PASS] + [FAR] * 3,
        [
            VMEM((5 * columns, height, UW), F32),
            VMEM((5 * block, detector), BF16),
            VMEM((3 * block, detector), BF16),
            VMEM((columns, height, UW), BF16),
            VMEM((count + 2, 3, height, UW), BF16),
            pltpu.SemaphoreType.DMA((1,)),
        ],
    )
    signal = exchange(signal)
    kept = (rows_tile + 2) * rows
    per_primal = tile_count(9 * channels, 6 * channels)
    per_dual = pl.cdiv(per_primal + tile_count(rows, 9 * slices * extra_dual), count)
    per_primal = pl.cdiv(per_primal + tile_count(rows, 9 * slices * extra_primal), count)
    width = (per_primal + per_dual) * TILE
    primal_state, near_weight = call(
        functools.partial(primal_state_kernel, slices, rows_tile, blocks),
        (*tiles, primal_inner, primal_outer, biases),
        (FAR,) * 6,
        [
            shape_of((2 * kept, cells), F32),
            shape_of((height + rows, 9 * rows), BF16),
        ],
        [FAR] * 2,
        [VMEM(((rows_tile + 4) * block, cells), BF16)] * 2,
    )
    rays, mixed = call(
        functools.partial(primal_kernel, slices, bins, rows_tile),
        (signal, hits, footprint_table, near_weight, primal_state),
        (FAR, LISTS) + (FAR,) * 3,
        [
            shape_of((count, tables, height, UW), BF16),
            shape_of((2 * kept + (rows_tile + 4) * height, cells), BF16),
        ],
        [FAR] * 2,
        [
            VMEM((3 * tables + 1, height, UW), F32),
            VMEM(((rows_tile + 2) * block, cells), BF16),
        ],
    )
    rays = exchange(rays)
    (payload,) = call(
        functools.partial(primal_rest_kernel, slices, rows_tile, blocks, rows),
        (mixed, *tiles),
        (FAR,) * 4,
        [shape_of((count, 8, (per_primal + per_dual) * TILE + UW), BF16)],
        [PASS],
        [VMEM((count, 8, per_primal * TILE), BF16), pltpu.SemaphoreType.DMA((1,))],
    )
    dual_part, back_weight = call(
        functools.partial(dual_cot_kernel, slices, bins, near_rows),
        (*views, dual_inner, dual_outer),
        ranges(head, head + rows) + (FAR, FAR),
        [
            shape_of((3 * rows, detector), F32),
            shape_of((2 * rows + height, 9 * rows), BF16),
        ],
        [FAR] * 2,
        [VMEM((5 * block, detector), BF16)],
    )
    dual_grad, payload = call(
        functools.partial(dual_backward_kernel, slices, bins, per_dual, head, near_rows),
        (*views, rays, hits, back_weight, dual_part, slope, hidden, payload),
        ranges(0, near_rows) + (FAR, LISTS) + (FAR,) * 4 + (PASS,),
        [shape_of(dual_flat, BF16), shape_of(payload.shape, BF16)],
        [FAR, PASS],
        [
            VMEM((5 * columns, height, UW), F32),
            VMEM((3 * block, detector), BF16),
            VMEM((columns, height, UW), BF16),
            VMEM((count, 8, per_dual * TILE + UW), BF16),
            pltpu.SemaphoreType.DMA((1,)),
        ],
        alias={10: 1},
    )
    payload = exchange(payload)
    payload, signal = call(
        sum_kernel,
        (payload,),
        (HERE,),
        [shape_of((count, 8, width), BF16), shape_of((count, height, UW), BF16)],
        [HERE, HERE],
        limit=2 * 1024 * 1024,
    )
    payload = exchange(payload)
    new_volume, volume_grad = call(
        functools.partial(volume_grad_kernel, slices, bins, rows_tile),
        (mixed, tile, primal_inner, primal_outer, biases, footprint_table)
        + (bin_energy, basis_table, signal, hits),
        (FAR,) * 6 + (LISTS, FAR, HERE, LISTS),
        [shape_of(volume.shape, BF16)] * 2,
        [FAR] * 2,
        [VMEM(((rows_tile + 2) * block, cells), BF16)] * 2
        + [VMEM((rows_tile * rows, cells), F32), VMEM((tables + 1, height, UW), F32)],
        limit=16 * 1024 * 1024,
    )
    gradients = call(
        functools.partial(unpack_kernel, slices, per_primal, per_dual),
        (payload,),
        (HERE,),
        [shape_of(w.shape, F32) for w in (primal_inner, primal_outer, dual_inner, dual_outer)],
        [FAR] * 4,
        limit=8 * 1024 * 1024,
    )
    return (
        new_volume,
        new_dual.reshape(dual_state.shape),
        volume_grad,
        dual_grad.reshape(dual_state.shape),
        *gradients,
    )


def solution(mesh):
    split = P(None, "parts", "view", None)
    in_specs = (split,) * 5 + (P(),) * 15
    out_specs = (split,) * 4 + (P("parts", None, None),) * 4
    return jax.shard_map(whole, mesh=mesh, in_specs=in_specs, out_specs=out_specs, check_vma=False)
```

```python
import functools

import jax
import jax.numpy as jnp
from jax import lax
from jax.experimental import pallas as pl
from jax.experimental.pallas import tpu as pltpu
from jax.sharding import PartitionSpec as P


UW = 128
TILE = 128
F32 = jnp.float32
BF16 = jnp.bfloat16
VMEM = pltpu.VMEM
SMEM = pltpu.SMEM


class Late:
    def __init__(self, ref, copy):
        self.ref, self.copy, self.shape = ref, copy, ref.shape

    def ready(self):
        if self.copy is not None:
            self.copy.wait()
            self.copy = None
        return self.ref

    def __getitem__(self, index):
        return self.ready()[index]


class Out:
    def __init__(self, ref, copy):
        self.ref, self.copy, self.shape, self.left = ref, copy, ref.shape, False

    def __getitem__(self, index):
        return self.ref[index]

    def __setitem__(self, index, value):
        self.ref[index] = value

    def flush(self):
        if not self.left:
            self.copy.start()
            self.left = True


class Wider:
    def __init__(self, far, sem):
        self.far, self.sem, self.copy = far, sem, None

    def flush_from(self, out):
        self.copy = pltpu.make_async_copy(out.ref, self.far.at[0 : out.shape[0]], self.sem)
        self.copy.start()


class Choice:
    def __init__(self, even, yes, no):
        self.even, self.yes, self.no, self.shape = even, yes, no, yes.shape

    def __getitem__(self, index):
        yes, no = self.yes[index], self.no[index]
        return jnp.where(self.even, yes.astype(F32), no.astype(F32)).astype(yes.dtype)


HERE = "vmem"
WIDER = "wider"
PASS = "pass"
LISTS = "smem"
FAR = "hbm"


def call(kernel, operands, places, out_shapes, out_places, scratch=(), limit=67_000_000, alias=None):
    total_in, total_out = len(operands), len(out_shapes)
    buffers = []
    for place, array in zip(list(places) + list(out_places), list(operands) + list(out_shapes)):
        if place not in (HERE, PASS, WIDER):
            kind = SMEM if place == LISTS else VMEM
            dims = array.shape
            if isinstance(place, tuple):
                dims = (place[1] - place[0],) + tuple(dims[1:])
            buffers.append(kind(dims, array.dtype))

    def body(*refs):
        given = refs[: total_in + total_out]
        own = refs[total_in + total_out :]
        local, sems, rest = own[: len(buffers)], own[len(buffers)], own[len(buffers) + 1 :]
        seen = []
        used = 0
        for index, place in enumerate(list(places) + list(out_places)):
            if place in (HERE, PASS):
                seen.append(given[index])
                continue
            if place == WIDER:
                seen.append(Wider(given[index], sems.at[len(buffers)]))
                continue
            near = local[used]
            far = given[index]
            if isinstance(place, tuple):
                far = far.at[place[0] : place[1]]
            if index < total_in:
                copy = pltpu.make_async_copy(far, near, sems.at[used])
                copy.start()
                seen.append(Late(near, copy))
            else:
                seen.append(Out(near, pltpu.make_async_copy(near, far, sems.at[used])))
            used += 1
        kernel(*seen, *rest)
        for item in seen[:total_in]:
            if isinstance(item, Late):
                item.ready()
        for item in seen[total_in:]:
            if isinstance(item, Out):
                item.flush()
        for item in seen[total_in:]:
            if isinstance(item, (Out, Wider)):
                item.copy.wait()

    def spec(place):
        return pl.BlockSpec(memory_space=VMEM if place == HERE else pltpu.HBM)

    return pl.pallas_call(
        body,
        out_shape=out_shapes,
        in_specs=[spec(place) for place in places],
        out_specs=[spec(place) for place in out_places],
        scratch_shapes=buffers + [pltpu.SemaphoreType.DMA((len(buffers) + 1,))] + list(scratch),
        compiler_params=pltpu.CompilerParams(vmem_limit_bytes=limit),
        cost_estimate=pl.CostEstimate(flops=10**8, bytes_accessed=10**6, transcendentals=0),
        input_output_aliases=alias or {},
    )(*operands)


def shape_of(dims, kind):
    return jax.ShapeDtypeStruct(dims, kind)


def dot(left, right):
    return jnp.dot(left, right, preferred_element_type=F32)


def dot_nt(left, right):
    return lax.dot_general(left, right, (((1,), (1,)), ((), ())), preferred_element_type=F32)


def shifted(wide):
    lanes = wide.shape[1]
    lane = lax.broadcasted_iota(jnp.int32, wide.shape, 1)
    low = jnp.where(lane == 0, 0.0, pltpu.roll(wide, 1, 1))
    high = jnp.where(lane == lanes - 1, 0.0, pltpu.roll(wide, lanes - 1, 1))
    return low, wide, high


def put_columns(column_ref, row, plane, slices):
    channels = plane.shape[0] // slices
    block = 3 * plane.shape[0]
    for tap, moved in enumerate(shifted(plane.astype(F32))):
        moved = moved.astype(BF16)
        for z in range(slices):
            start = row * block + (z * 3 + tap) * channels
            column_ref[start : start + channels, :] = moved[z * channels : (z + 1) * channels]


def window(column_ref, row, block):
    return column_ref[(row - 1) * block : (row + 2) * block, :]


def sigmoid(values):
    return 1.0 / (1.0 + jnp.exp(-values))


def spread_lists(gradient, slices, taps_z=3):
    channels = gradient.shape[0] // slices
    parts = []
    for z_in in range(slices):
        rows = []
        for i in range(taps_z):
            z_out = z_in - i + 1
            if 0 <= z_out < slices:
                rows.append(gradient[z_out * channels : (z_out + 1) * channels])
            else:
                rows.append(jnp.zeros((channels, gradient.shape[1]), BF16))
        parts.append(jnp.concatenate(rows, axis=0))
    return parts


def moved_gradient(gradient, slices):
    low, here, high = shifted(gradient.astype(F32))
    versions = [spread_lists(part.astype(BF16), slices) for part in (high, here, low)]
    return [
        jnp.concatenate([version[z] for version in versions], axis=0) for z in range(slices)
    ]


def state_wgrad(moved, planes, slices):
    channels = planes[0].shape[0] // slices
    total = None
    for z in range(slices):
        around = jnp.concatenate(
            [plane[z * channels : (z + 1) * channels] for plane in planes], axis=0
        )
        term = dot_nt(moved[z], around)
        total = term if total is None else total + term
    return total


def tap_of(i, j, l):
    return (i * 3 + j) * 3 + l


def forward_weight(weight_ref, slices, low, high, lane_major):
    rows = []
    for z in range(slices):
        pieces = []
        for j in range(3):
            pairs = [(zi, l) for zi in range(slices) for l in range(3)]
            if lane_major:
                pairs = [(zi, l) for l in range(3) for zi in range(slices)]
            for zi, l in pairs:
                i = zi - z + 1
                if 0 <= i < 3:
                    pieces.append(weight_ref[tap_of(i, j, l)].astype(F32)[:, low:high])
                else:
                    pieces.append(jnp.zeros((weight_ref.shape[1], high - low), F32))
        rows.append(jnp.concatenate(pieces, axis=1))
    return jnp.concatenate(rows, axis=0).astype(BF16)


def adjoint_weight(weight_ref, slices, low, high, first=0, last=None, lane_major=False):
    last = weight_ref.shape[1] if last is None else last
    rows = []
    for j in range(3):
        pairs = [(z, l) for z in range(slices) for l in range(3)]
        if lane_major:
            pairs = [(z, l) for l in range(3) for z in range(slices)]
        for z, l in pairs:
            pieces = []
            for zi in range(slices):
                i = zi - z + 1
                if 0 <= i < 3:
                    tap = weight_ref[tap_of(i, 2 - j, 2 - l)].astype(F32)
                    pieces.append(tap[first:last, low:high])
                else:
                    pieces.append(jnp.zeros((last - first, high - low), F32))
            rows.append(jnp.concatenate(pieces, axis=1))
    return jnp.concatenate(rows, axis=0).T.astype(BF16)


def arrived(*refs):
    return [ref.ready() if isinstance(ref, Late) else ref for ref in refs]


def as_column(values):
    count = values.shape[0]
    square = jnp.broadcast_to(values[None, :], (count, count))
    row = lax.broadcasted_iota(jnp.int32, square.shape, 0)
    col = lax.broadcasted_iota(jnp.int32, square.shape, 1)
    return jnp.sum(jnp.where(row == col, square, 0.0), axis=1, keepdims=True)


def code_hits(tile_ref, table_ref, column_ref, count_ref):
    tiles = tile_ref[...]
    count = as_column(count_ref[...].astype(F32))
    live = lax.broadcasted_iota(jnp.int32, tiles.shape, 1).astype(F32) < count
    codes = table_ref[...] * 16 + column_ref[...]
    position = lax.axis_index("view")
    found = [(tiles * 256 + codes).astype(F32), count]
    for slot in range(3):
        hit = live & (tiles == position + slot - 1)
        found.append(
            jnp.sum(jnp.where(hit, codes.astype(F32) + 1.0, 0.0), axis=1, keepdims=True) - 1.0
        )
    return jnp.concatenate(found, axis=1).astype(jnp.int32)


def mixing_of(energy_ref, basis_ref, bins):
    (energy_ref,) = arrived(energy_ref)
    energies = basis_ref.shape[0]
    row = lax.broadcasted_iota(jnp.int32, (bins, energies), 0)
    col = lax.broadcasted_iota(jnp.int32, (bins, energies), 1)
    onehot = jnp.zeros((bins, energies), F32)
    for n in range(bins):
        onehot = jnp.where((row == n) & (col == energy_ref[n]), 1.0, onehot)
    return dot(onehot.astype(BF16), basis_ref[...])


def send_rays(images, footprint_ref, send_ref):
    for table in range(footprint_ref.shape[0]):
        rays = dot(images, footprint_ref[table]).astype(BF16)
        for target in range(send_ref.shape[0]):
            send_ref[target, table] = rays


def pack_kernel(
    dual_ref,
    cot_dual_ref,
    sino_ref,
    volume_ref,
    energy_ref,
    basis_ref,
    footprint_ref,
    cot_volume_ref,
    pack_ref,
    near_ref,
    send_ref,
    cells_ref,
):
    channels, slices, rows_tile, _ = volume_ref.shape
    bins = sino_ref.shape[0]
    rows = slices * channels
    head = head_rows(rows, slices * bins)
    sino_rows = []
    for z in range(slices):
        at = z * channels
        pack_ref[at : at + channels, :] = dual_ref[:, z, :]
        at = head + z * channels
        pack_ref[at : at + channels, :] = cot_dual_ref[:, z, :]
        sino_rows.append(sino_ref[:, z, :].astype(F32))
    sino_rows.append(jnp.zeros((head - rows - slices * bins, sino_ref.shape[2]), F32))
    pack_ref[rows:head, :] = jnp.concatenate(sino_rows, axis=0).astype(BF16)
    near_ref.flush_from(pack_ref)
    pack_ref.flush()
    at = 0
    for source in (volume_ref, cot_volume_ref):
        for r in range(rows_tile):
            for z in range(slices):
                cells_ref[at : at + channels, :] = source[:, z, r, :]
                at += channels
        if source is volume_ref:
            mixing = mixing_of(energy_ref, basis_ref, bins).astype(BF16)
            images = []
            for z in range(slices):
                line = []
                for r in range(rows_tile):
                    first = (r * slices + z) * channels
                    line.append(dot(mixing, cells_ref[first : first + channels, :]))
                images.append(jnp.concatenate(line, axis=1))
            send_rays(jnp.concatenate(images, axis=0).astype(BF16), footprint_ref, send_ref)
            send_ref.flush()


def head_rows(rows, height):
    return rows + pl.cdiv(height, 16) * 16


def weights_kernel(
    slices,
    tile_ref,
    table_ref,
    column_ref,
    count_ref,
    di,
    do,
    bias_0,
    bias_1,
    bias_2,
    bias_3,
    weight_ref,
    bias_ref,
    hits_ref,
):
    channels = do.shape[1]
    hits_ref[...] = code_hits(tile_ref, table_ref, column_ref, count_ref)
    columns = [column_bias(bias, slices) for bias in (bias_0, bias_1, bias_2, bias_3)]
    bias_ref[...] = jnp.concatenate(columns, axis=1)
    weight_ref[...] = jnp.concatenate(
        [
            forward_weight(di, slices, 0, channels, False),
            forward_weight(do, slices, 0, channels, False),
            forward_weight(di, slices, channels, di.shape[2], True),
        ],
        axis=1,
    )


def ray_windows(rays_ref, hits_ref, sums_ref, views):
    rays_ref, hits_ref = arrived(rays_ref, hits_ref)
    blocks, entries = hits_ref.shape[0], hits_ref.shape[1] - 4
    columns = sums_ref.shape[0] // len(views)
    sums_ref[...] = jnp.zeros_like(sums_ref)
    for place, offset in enumerate(views):
        view = lax.rem(lax.axis_index("view") + offset + blocks, blocks)

        def each_entry(k, carry):
            code = hits_ref[view, k]
            at = place * columns + lax.rem(code, 16)
            table = lax.rem(lax.div(code, 16), 16)
            sums_ref[at] += rays_ref[lax.div(code, 256), table].astype(F32)
            return carry

        lax.fori_loop(0, hits_ref[view, entries], each_entry, 0)
    return [
        jnp.concatenate([sums_ref[place * columns + c] for c in range(columns)], axis=1)
        for place in range(len(views))
    ]


def extra_rows(projected, sino, slices, bins):
    rows = []
    for z in range(slices):
        rows.append(projected[z * bins : (z + 1) * bins])
        rows.append(sino[z * bins : (z + 1) * bins])
    return jnp.concatenate(rows, axis=0)


def extra_columns(pieces):
    return jnp.concatenate([piece for triple in pieces for piece in triple], axis=0).astype(BF16)


def column_bias(bias_ref, slices):
    return jnp.concatenate([as_column(bias_ref[...])] * slices, axis=0)


def five_views(own, beside, far, over, low, gap):
    even = lax.rem(lax.axis_index("view"), 2) == 0
    own, beside, across = Rows(own, low), Rows(beside, low), Rows(far, low)
    two, over = Rows(far, low + gap), Rows(over, low)
    return (
        Choice(even, two, over),
        Choice(even, across, beside),
        own,
        Choice(even, beside, across),
        Choice(even, over, two),
    )


class Rows:
    def __init__(self, source, first):
        self.source, self.first, self.shape = source, first, source.shape

    def __getitem__(self, index):
        rows, lanes = index
        return self.source[rows.start + self.first : rows.stop + self.first, lanes]


class Valid:
    def __init__(self, valid, source):
        self.valid, self.source, self.shape = valid, source, source.shape

    def __getitem__(self, index):
        values = self.source[index]
        return jnp.where(self.valid, values.astype(F32), 0.0).astype(values.dtype)


def three_tiles(blocks, own, beside, across):
    even = lax.rem(lax.axis_index("view"), 2) == 0
    return (
        Valid(lax.axis_index("view") > 0, Choice(even, across, beside)),
        own,
        Valid(lax.axis_index("view") < blocks - 1, Choice(even, beside, across)),
    )


def dual_forward_kernel(
    slices,
    bins,
    gap,
    pack_ref,
    beside_ref,
    far_ref,
    over_ref,
    rays_ref,
    hits_ref,
    weight_ref,
    bias_ref,
    send_ref,
    slope_ref,
    hidden_ref,
    new_ref,
    sums_ref,
    columns_ref,
    hidden_columns,
    windows_ref,
    ready_ref,
    sem,
):
    around = five_views(pack_ref, beside_ref, far_ref, over_ref, 0, gap)
    channels = new_ref.shape[0]
    rows = channels * slices
    height = slices * bins
    for row in range(5):
        put_columns(columns_ref, row, around[row][0:rows, :], slices)
    projected = ray_windows(rays_ref, hits_ref, sums_ref, (-2, -1, 0, 1, 2))
    bias_inner, bias_outer = bias_ref[:, 0:1], bias_ref[:, 1:2]
    w1s = weight_ref[:, 0 : 9 * rows]
    w2 = weight_ref[:, 9 * rows : 18 * rows]
    w1e = weight_ref[:, 18 * rows :]
    pieces = []
    for row in range(5):
        extra = extra_rows(
            projected[row].astype(BF16).astype(F32),
            around[row][rows : rows + height, :].astype(F32),
            slices,
            bins,
        )
        if 1 <= row <= 3:
            at = 3 * rows + (row - 1) * extra.shape[0]
            hidden_ref[at : at + extra.shape[0], :] = extra.astype(BF16)
        pieces.append(shifted(extra))
    for row in range(3):
        at = row * rows
        pre = dot(w1s, window(columns_ref, row + 1, 3 * rows))
        pre = pre + dot(w1e, extra_columns(pieces[row : row + 3])) + bias_inner
        gate = sigmoid(pre)
        hidden = (pre * gate).astype(BF16)
        hidden_ref[at : at + rows, :] = hidden
        slope_ref[at : at + rows, :] = gate * (1.0 + pre * (1.0 - gate))
        put_columns(hidden_columns, row, hidden, slices)
    slope_ref.flush()
    hidden_ref.flush()
    update = dot(w2, hidden_columns[...]) + bias_outer
    fresh = (around[2][0:rows, :].astype(F32) + update).astype(BF16)
    out = []
    for z in range(slices):
        plane = fresh[z * channels : (z + 1) * channels]
        new_ref[:, z, :] = plane
        out.append(plane.astype(F32)[:bins])
    new_ref.flush()
    out = jnp.concatenate(out, axis=0).astype(BF16)
    for column in range(out.shape[1] // UW):
        windows_ref[column] = out[:, column * UW : (column + 1) * UW]
    (hits,) = arrived(hits_ref)
    view = lax.axis_index("view")

    def each_entry(k, carry):
        code = hits[view, k]
        tile = lax.div(code, 256)
        values = windows_ref[lax.rem(code, 16)]
        for slot in range(3):
            ready_ref[tile + 2 - slot, slot] = values
        return carry

    lax.fori_loop(0, hits[view, hits.shape[1] - 4], each_entry, 0)
    copy = pltpu.make_async_copy(ready_ref.at[1 : 1 + send_ref.shape[0]], send_ref, sem.at[0])
    copy.start()
    copy.wait()


def gather_signals(signal_ref, code_ref, slots, footprint_ref, sums_ref, chosen=False):
    signal_ref, code_ref = arrived(signal_ref, code_ref)
    first = code_ref.shape[1] - 3
    tables = footprint_ref.shape[0]
    spare = len(slots) * tables
    sums_ref[...] = jnp.zeros_like(sums_ref)

    def each_block(b, carry):
        for place, slot in enumerate(slots):
            code = code_ref[b, first + slot]
            live = code >= 0
            code = jnp.maximum(code, 0)
            at = jnp.where(live, place * tables + lax.div(code, 16), spare)
            sums_ref[at] += (signal_ref[b] if chosen else signal_ref[b, slot]).astype(F32)
        return carry

    lax.fori_loop(0, signal_ref.shape[0], each_block, 0)
    total = None
    for table in range(tables):
        grouped = jnp.concatenate(
            [sums_ref[place * tables + table] for place in range(len(slots))], axis=0
        )
        high = grouped.astype(BF16).astype(F32)
        both = jnp.concatenate([high, grouped - high], axis=0).astype(BF16)
        term = dot_nt(both, footprint_ref[table])
        total = term if total is None else total + term
    half = total.shape[0] // 2
    return total[:half] + total[half:]


def fold_lanes(array):
    full = array.shape[1] // TILE * TILE
    rest = array.shape[1] - full
    if rest == 0:
        return [array]
    copies = TILE // rest
    while array.shape[0] % (8 * copies):
        copies -= 1
    rows = array.shape[0] // copies
    side = [array[c * rows : (c + 1) * rows, full:] for c in range(copies)]
    side = jnp.concatenate(side, axis=1) if copies > 1 else side[0]
    return ([array[:, :full]] if full else []) + [side]


def fold_shapes(rows, width):
    full = width // TILE * TILE
    rest = width - full
    if rest == 0:
        return [(rows, width)], 1
    copies = TILE // rest
    while rows % (8 * copies):
        copies -= 1
    return ([(rows, full)] if full else []) + [(rows // copies, rest * copies)], copies


def tile_count(rows, width):
    shapes, _ = fold_shapes(rows, width)
    return sum(r // 8 * pl.cdiv(w, TILE) for r, w in shapes)


def put_payload(payload_ref, per, first, array):
    flat = first
    for part in fold_lanes(array):
        width = part.shape[1]
        for group in range(part.shape[0] // 8):
            for tile in range(pl.cdiv(width, TILE)):
                last = min(width, (tile + 1) * TILE)
                lane = (flat % per) * TILE
                payload_ref[flat // per, :, lane : lane + last - tile * TILE] = part[
                    group * 8 : group * 8 + 8, tile * TILE : last
                ].astype(BF16)
                flat += 1
    return flat


def take_payload(payload_ref, per, first, rows, width):
    flat = first
    shapes, copies = fold_shapes(rows, width)
    parts = []
    for part_rows, part_width in shapes:
        groups = []
        for _ in range(part_rows // 8):
            tiles = []
            for _ in range(pl.cdiv(part_width, TILE)):
                lane = (flat % per) * TILE
                tiles.append(payload_ref[flat // per, :, lane : lane + TILE].astype(F32))
                flat += 1
            groups.append(jnp.concatenate(tiles, axis=1) if len(tiles) > 1 else tiles[0])
        parts.append(jnp.concatenate(groups, axis=0))
    rest = width % TILE
    if rest:
        side = parts.pop()
        parts.append(
            jnp.concatenate([side[:, c * rest : (c + 1) * rest] for c in range(copies)], axis=0)
        )
    return (jnp.concatenate(parts, axis=1) if len(parts) > 1 else parts[0]), flat


def row_plane(tiles, row, which, rows, rows_tile):
    ref, r = tiles[row // rows_tile], row % rows_tile
    at = (which * rows_tile + r) * rows
    return ref[at : at + rows, :]


def primal_state_kernel(
    slices,
    rows_tile,
    blocks,
    v0,
    v1,
    v2,
    inner_ref,
    outer_ref,
    bias_ref,
    dual_inner,
    dual_outer,
    state_ref,
    near_weight,
    back_weight,
    columns_ref,
    cot_columns,
):
    tiles = three_tiles(blocks, v0, v1, v2)
    channels = outer_ref.shape[1]
    rows = channels * slices
    bins = inner_ref.shape[2] - channels
    w1s = forward_weight(inner_ref, slices, 0, channels, False)
    w2t = adjoint_weight(outer_ref, slices, 0, channels)
    thin = slices * bins
    near_weight[0:thin, :] = adjoint_weight(inner_ref, slices, channels, channels + bins)
    near_weight[thin : thin + rows, 0 : 9 * thin] = forward_weight(
        inner_ref, slices, channels, inner_ref.shape[2], True
    )
    back_weight[0:rows, :] = adjoint_weight(dual_inner, slices, 0, channels)
    back_weight[rows : rows + thin, :] = adjoint_weight(dual_inner, slices, channels, channels + bins)
    back_weight[rows + thin : 2 * rows + thin, 0 : 9 * thin] = adjoint_weight(
        dual_outer, slices, 0, channels, 0, bins, True
    )
    back_weight[2 * rows + thin : 3 * rows + thin, :] = adjoint_weight(
        dual_outer, slices, 0, channels
    )
    bias = bias_ref[:, 2:3]
    kept = (rows_tile + 2) * rows
    first = rows_tile - 2
    for row in range(rows_tile + 4):
        at = first + row
        put_columns(columns_ref, row, row_plane(tiles, at, 0, rows, rows_tile), slices)
        put_columns(cot_columns, row, row_plane(tiles, at, 1, rows, rows_tile), slices)
    for row in range(rows_tile + 2):
        pre = dot(w1s, window(columns_ref, row + 1, 3 * rows)) + bias
        state_ref[row * rows : (row + 1) * rows, :] = pre
        gradient = dot(w2t, window(cot_columns, row + 1, 3 * rows))
        state_ref[kept + row * rows : kept + (row + 1) * rows, :] = gradient


def primal_kernel(
    slices,
    bins,
    rows_tile,
    signal_ref,
    code_ref,
    footprint_ref,
    weight_ref,
    state_ref,
    send_ref,
    mixed_ref,
    sums_ref,
    grad_columns,
):
    blocks = send_ref.shape[0]
    lanes = state_ref.shape[1]
    thin = slices * bins
    rows = weight_ref.shape[0] - thin
    kept = (rows_tile + 2) * rows
    position = lax.axis_index("view")
    height = slices * bins
    back = gather_signals(signal_ref, code_ref, (0, 1, 2), footprint_ref, sums_ref)
    back = back.astype(BF16).astype(F32)
    pieces = []
    for row in range(rows_tile + 4):
        at = row + rows_tile - 2
        tile, r = at // rows_tile, at % rows_tile
        extra = back[tile * height : (tile + 1) * height, r * lanes : (r + 1) * lanes]
        at = 2 * kept + row * height
        mixed_ref[at : at + height, :] = extra.astype(BF16)
        pieces.append(shifted(extra))
    w1x = weight_ref[0:thin, :]
    w1e = weight_ref[thin : thin + rows, 0 : 9 * thin]
    for row in range(rows_tile + 2):
        at = row * rows
        pre = state_ref[at : at + rows, :] + dot(w1e, extra_columns(pieces[row : row + 3]))
        gate = sigmoid(pre)
        hidden = pre * gate
        gradient = state_ref[kept + at : kept + at + rows, :] * (gate * (1.0 + pre * (1.0 - gate)))
        if row == 0:
            hidden = jnp.where(position > 0, hidden, 0.0)
            gradient = jnp.where(position > 0, gradient, 0.0)
        if row == rows_tile + 1:
            hidden = jnp.where(position < blocks - 1, hidden, 0.0)
            gradient = jnp.where(position < blocks - 1, gradient, 0.0)
        gradient = gradient.astype(BF16)
        mixed_ref[at : at + rows, :] = hidden.astype(BF16)
        mixed_ref[kept + at : kept + at + rows, :] = gradient
        put_columns(grad_columns, row, gradient, slices)
    mixed_ref.flush()
    parts = []
    for row in range(rows_tile):
        parts.append(dot(w1x, window(grad_columns, row + 1, 3 * rows)))
    send_rays(jnp.concatenate(parts, axis=1).astype(BF16), footprint_ref, send_ref)


def primal_rest_kernel(
    slices, rows_tile, blocks, rows, mixed_ref, v0, v1, v2, payload_ref, ready_ref, sem
):
    tiles = three_tiles(blocks, v0, v1, v2)
    kept = (rows_tile + 2) * rows
    height = (mixed_ref.shape[0] - 2 * kept) // (rows_tile + 4)
    hidden_ref, gradient_ref = mixed_ref, Rows(mixed_ref, kept)
    pieces = [
        shifted(
            mixed_ref[2 * kept + row * height : 2 * kept + (row + 1) * height, :].astype(F32)
        )
        for row in range(1, rows_tile + 3)
    ]
    inner = None
    outer = None
    extra_total = None
    for r in range(rows_tile):
        at = (r + 1) * rows
        cot = row_plane(tiles, rows_tile + r, 1, rows, rows_tile)
        gradient = gradient_ref[at : at + rows, :]
        planes = [
            row_plane(tiles, rows_tile - 1 + r + j, 0, rows, rows_tile) for j in range(3)
        ]
        term = state_wgrad(moved_gradient(gradient, slices), planes, slices)
        inner = term if inner is None else inner + term
        planes = [hidden_ref[(r + j) * rows : (r + j + 1) * rows, :] for j in range(3)]
        term = state_wgrad(moved_gradient(cot, slices), planes, slices)
        outer = term if outer is None else outer + term
        term = dot_nt(gradient, extra_columns(pieces[r : r + 3]))
        extra_total = term if extra_total is None else extra_total + term
    per = ready_ref.shape[2] // TILE
    flat = put_payload(ready_ref, per, 0, jnp.concatenate([inner, outer], axis=1))
    put_payload(ready_ref, per, flat, extra_total)
    copy = pltpu.make_async_copy(ready_ref, payload_ref.at[:, :, 0 : per * TILE], sem.at[0])
    copy.start()
    copy.wait()


def dual_cot_kernel(
    slices,
    bins,
    gap,
    c0,
    c1,
    c2,
    c3,
    weight_ref,
    part_ref,
    columns_ref,
):
    around = five_views(c0, c1, c2, c3, 0, gap)
    rows = c0.shape[0]
    thin = slices * bins
    channels = rows // slices
    w2t = weight_ref[...]
    for row in range(5):
        plane = around[row][0:rows, :].astype(F32)
        channel = lax.broadcasted_iota(jnp.int32, plane.shape, 0)
        plane = jnp.where(lax.rem(channel, channels) < bins, 0.0, plane)
        put_columns(columns_ref, row, plane, slices)
    for row in range(3):
        at = row * rows
        part_ref[at : at + rows, :] = dot(w2t, window(columns_ref, row + 1, 3 * rows))


def dual_backward_kernel(
    slices,
    bins,
    per,
    low,
    gap,
    pack_ref,
    beside_ref,
    far_ref,
    over_ref,
    rays_ref,
    hits_ref,
    weight_ref,
    part_ref,
    slope_ref,
    hidden_ref,
    payload_in,
    grad_ref,
    payload_ref,
    sums_ref,
    grad_columns,
    windows_ref,
    ready_ref,
    sem,
):
    del payload_in
    around = five_views(pack_ref, beside_ref, far_ref, over_ref, low, gap)
    states = five_views(pack_ref, beside_ref, far_ref, over_ref, 0, gap)[1:4]
    channels = grad_ref.shape[0]
    rows = channels * slices
    thin = slices * bins
    toward = ray_windows(rays_ref, hits_ref, sums_ref, (-2, -1, 0, 1, 2))
    w1t = weight_ref[0:rows, :]
    w1x = weight_ref[rows : rows + thin, :]
    w2x = weight_ref[rows + thin : 2 * rows + thin, 0 : 9 * thin]
    pieces = []
    own_head = None
    for row in range(5):
        head = jnp.concatenate(
            [
                around[row][z * channels : z * channels + 2 * bins, :].astype(F32)[:bins]
                for z in range(slices)
            ],
            axis=0,
        )
        head = head + toward[row]
        if row == 2:
            own_head = head
        pieces.append(shifted(head.astype(BF16).astype(F32)))
    spread = []
    lanes = own_head.shape[1]
    for z in range(slices):
        spread.append(own_head[z * bins : (z + 1) * bins])
        spread.append(around[2][z * channels : (z + 1) * channels, :].astype(F32)[bins:])
    own_total = jnp.concatenate(spread, axis=0)
    own_cot = own_total.astype(BF16)
    own_gradient = None
    for row in range(3):
        at = row * rows
        gradient = part_ref[at : at + rows, :] + dot(w2x, extra_columns(pieces[row : row + 3]))
        gradient = (gradient * slope_ref[at : at + rows, :]).astype(BF16)
        put_columns(grad_columns, row, gradient, slices)
        if row == 1:
            own_gradient = gradient
    out = dot(w1x, grad_columns[...]).astype(BF16)
    for column in range(lanes // UW):
        windows_ref[column] = out[:, column * UW : (column + 1) * UW]
    start = per * TILE
    ready_ref[:, :, start : start + UW] = jnp.zeros(
        (ready_ref.shape[0], ready_ref.shape[1], UW), BF16
    )
    view = lax.axis_index("view")
    (hits,) = arrived(hits_ref)

    def each_entry(k, carry):
        code = hits[view, k]
        ready_ref[lax.div(code, 256), :, start : start + UW] = windows_ref[lax.rem(code, 16)]
        return carry

    lax.fori_loop(0, hits[view, hits.shape[1] - 4], each_entry, 0)
    planes = [states[row][0:rows, :] for row in range(3)]
    inner = state_wgrad(moved_gradient(own_gradient, slices), planes, slices)
    planes = [hidden_ref[row * rows : (row + 1) * rows, :] for row in range(3)]
    outer = state_wgrad(moved_gradient(own_cot, slices), planes, slices)
    height = (hidden_ref.shape[0] - 3 * rows) // 3
    pieces = []
    for row in range(3):
        at = 3 * rows + row * height
        pieces.append(shifted(hidden_ref[at : at + height, :].astype(F32)))
    extra = dot_nt(own_gradient, extra_columns(pieces))
    flat = put_payload(ready_ref, per, 0, jnp.concatenate([inner, outer], axis=1))
    put_payload(ready_ref, per, flat, extra)
    total = payload_ref.shape[2]
    copy = pltpu.make_async_copy(
        ready_ref, payload_ref.at[:, :, total - ready_ref.shape[2] : total], sem.at[0]
    )
    copy.start()
    state = (dot(w1t, grad_columns[...]) + own_total).astype(BF16)
    for z in range(slices):
        grad_ref[:, z, :] = state[z * channels : (z + 1) * channels]
    grad_ref.flush()
    copy.wait()


def sum_kernel(payload_ref, send_ref, rays_ref):
    width = send_ref.shape[2]
    total = payload_ref[0, :, 0:width].astype(F32)
    for source in range(1, payload_ref.shape[0]):
        total = total + payload_ref[source, :, 0:width].astype(F32)
    total = total.astype(BF16)
    for target in range(send_ref.shape[0]):
        send_ref[target] = total
    rays_ref[...] = payload_ref[:, :, width:]


def volume_grad_kernel(
    slices,
    bins,
    rows_tile,
    mixed_ref,
    cells_ref,
    inner_ref,
    outer_ref,
    bias_ref,
    footprint_ref,
    energy_ref,
    basis_ref,
    signal_ref,
    code_ref,
    new_ref,
    out_ref,
    hidden_columns,
    grad_columns,
    state_ref,
    sums_ref,
):
    channels = new_ref.shape[0]
    rows = channels * slices
    lanes = mixed_ref.shape[1]
    kept = (rows_tile + 2) * rows
    for row in range(rows_tile + 2):
        at = row * rows
        put_columns(hidden_columns, row, mixed_ref[at : at + rows, :], slices)
        put_columns(grad_columns, row, mixed_ref[kept + at : kept + at + rows, :], slices)
    w2 = forward_weight(outer_ref, slices, 0, channels, False)
    w1t = adjoint_weight(inner_ref, slices, 0, channels)
    bias = bias_ref[:, 3:4]
    for r in range(rows_tile):
        at = r * rows
        update = dot(w2, window(hidden_columns, r + 1, 3 * rows)) + bias
        fresh = (cells_ref[at : at + rows, :].astype(F32) + update).astype(BF16)
        for z in range(slices):
            new_ref[:, z, r, :] = fresh[z * channels : (z + 1) * channels]
        cot = cells_ref[rows_tile * rows + at : rows_tile * rows + at + rows, :].astype(F32)
        state_ref[at : at + rows, :] = dot(w1t, window(grad_columns, r + 1, 3 * rows)) + cot
    new_ref.flush()
    back = gather_signals(signal_ref, code_ref, (1,), footprint_ref, sums_ref, chosen=True)
    mixing = mixing_of(energy_ref, basis_ref, bins)
    for z in range(slices):
        part = back[z * bins : (z + 1) * bins]
        high = part.astype(BF16).astype(F32)
        low = part - high
        spread = lax.dot_general(
            jnp.concatenate([mixing, mixing], axis=0).astype(BF16),
            jnp.concatenate([high, low], axis=0).astype(BF16),
            (((0,), (0,)), ((), ())),
            preferred_element_type=F32,
        )
        for r in range(rows_tile):
            at = (r * slices + z) * channels
            total = state_ref[at : at + channels, :] + spread[:, r * lanes : (r + 1) * lanes]
            out_ref[:, z, r, :] = total.astype(BF16)


class Region:
    def __init__(self, ref, first):
        self.ref, self.first = ref, first

    def __getitem__(self, index):
        chunk, rows, lanes = index
        return self.ref[chunk, rows, lanes.start + self.first : lanes.stop + self.first]


def unpack_kernel(
    slices, per_primal, per_dual, payload_ref, primal_inner, primal_outer, dual_inner, dual_outer
):
    channels = dual_outer.shape[1]
    for inner_ref, outer_ref, per, first in (
        (primal_inner, primal_outer, per_primal, 0),
        (dual_inner, dual_outer, per_dual, per_primal * TILE),
    ):
        region = Region(payload_ref, first)
        flat = 0
        extra_count = inner_ref.shape[2] - channels
        state, flat = take_payload(region, per, flat, 9 * channels, 6 * channels)
        extra, flat = take_payload(region, per, flat, slices * channels, 9 * slices * extra_count)
        for i in range(3):
            for j in range(3):
                for l in range(3):
                    tap = (i * 3 + j) * 3 + l
                    lane = j * channels
                    rows = state[(l * 3 + i) * channels : (l * 3 + i + 1) * channels]
                    more = None
                    for z in range(slices):
                        z_in = z + i - 1
                        if 0 <= z_in < slices:
                            at = ((j * 3 + l) * slices + z_in) * extra_count
                            term = extra[z * channels : (z + 1) * channels, at : at + extra_count]
                            more = term if more is None else more + term
                    inner_ref[tap] = jnp.concatenate(
                        [rows[:, lane : lane + channels], more], axis=1
                    )
                    lane = lane + 3 * channels
                    outer_ref[tap] = rows[:, lane : lane + channels]


def whole(
    volume,
    dual_state,
    sinogram,
    cot_volume,
    cot_dual,
    basis_table,
    bin_energy,
    footprint_table,
    hit_tile,
    hit_table,
    hit_column,
    hit_count,
    primal_inner,
    primal_inner_bias,
    primal_outer,
    primal_outer_bias,
    dual_inner,
    dual_inner_bias,
    dual_outer,
    dual_outer_bias,
):
    count = lax.axis_size("view")
    channels, slices, rows_tile, cells = volume.shape
    bins = sinogram.shape[0]
    detector = dual_state.shape[3]
    columns = detector // UW
    tables = footprint_table.shape[0]
    blocks, entries = hit_tile.shape
    height = slices * bins
    rows = slices * channels
    block = 3 * rows
    lists = (hit_tile, hit_table, hit_column, hit_count)
    list_places = (LISTS,) * 4

    def exchange(array):
        return lax.all_to_all(array, "view", split_axis=0, concat_axis=0)

    def swap(array):
        return lax.ppermute(array, "view", [(k, k ^ 1) for k in range(count)])

    def cross(array, periodic):
        pairs = []
        for k in range(1, count, 2):
            if periodic or k + 1 < count:
                pairs += [(k, (k + 1) % count), ((k + 1) % count, k)]
        return lax.ppermute(array, "view", pairs)

    head = head_rows(rows, height)
    near_rows = head + rows
    dual_flat = (channels, slices, detector)
    pack, near, rays, tile = call(
        pack_kernel,
        (dual_state.reshape(dual_flat), cot_dual.reshape(dual_flat))
        + (sinogram.reshape(bins, slices, detector), volume, bin_energy, basis_table)
        + (footprint_table, cot_volume),
        (FAR,) * 4 + (LISTS,) + (FAR,) * 3,
        [
            shape_of((near_rows, detector), BF16),
            shape_of((2 * near_rows, detector), BF16),
            shape_of((count, tables, height, UW), BF16),
            shape_of((2 * rows_tile * rows, cells), BF16),
        ],
        [FAR, WIDER, FAR, FAR],
    )
    beside = swap(pack)
    rays = exchange(rays)
    near = lax.dynamic_update_slice(near, beside, (near_rows, 0))
    far = cross(near, True)
    tiles = (tile, swap(tile), cross(tile, False))
    over = swap(far)
    views = (pack, beside, far, over)

    def ranges(first, last):
        return ((first, last), (first, last), (first, near_rows + last), (first, last))

    wide = shape_of((rows, 9 * rows), BF16)
    extra_dual = dual_inner.shape[2] - channels
    extra_primal = primal_inner.shape[2] - channels
    dual_weight, biases, hits = call(
        functools.partial(weights_kernel, slices),
        (*lists, dual_inner, dual_outer, dual_inner_bias, dual_outer_bias)
        + (primal_inner_bias, primal_outer_bias),
        (FAR,) * 10,
        [
            shape_of((rows, 18 * rows + 9 * slices * extra_dual), BF16),
            shape_of((rows, 4), F32),
            shape_of((blocks, entries + 4), jnp.int32),
        ],
        [FAR] * 3,
    )
    signal, slope, hidden, new_dual = call(
        functools.partial(dual_forward_kernel, slices, bins, near_rows),
        (*views, rays, hits, dual_weight, biases),
        ranges(0, head) + (FAR, LISTS, FAR, FAR),
        [
            shape_of((count, 3, height, UW), BF16),
            shape_of((3 * rows, detector), F32),
            shape_of((3 * (rows + 2 * height), detector), BF16),
            shape_of(dual_flat, BF16),
        ],
        [PASS] + [FAR] * 3,
        [
            VMEM((5 * columns, height, UW), F32),
            VMEM((5 * block, detector), BF16),
            VMEM((3 * block, detector), BF16),
            VMEM((columns, height, UW), BF16),
            VMEM((count + 2, 3, height, UW), BF16),
            pltpu.SemaphoreType.DMA((1,)),
        ],
    )
    signal = exchange(signal)
    kept = (rows_tile + 2) * rows
    per_primal = tile_count(9 * channels, 6 * channels)
    per_dual = pl.cdiv(per_primal + tile_count(rows, 9 * slices * extra_dual), count)
    per_primal = pl.cdiv(per_primal + tile_count(rows, 9 * slices * extra_primal), count)
    width = (per_primal + per_dual) * TILE
    primal_state, near_weight, back_weight = call(
        functools.partial(primal_state_kernel, slices, rows_tile, blocks),
        (*tiles, primal_inner, primal_outer, biases, dual_inner, dual_outer),
        (FAR,) * 8,
        [
            shape_of((2 * kept, cells), F32),
            shape_of((height + rows, 9 * rows), BF16),
            shape_of((3 * rows + height, 9 * rows), BF16),
        ],
        [FAR] * 3,
        [VMEM(((rows_tile + 4) * block, cells), BF16)] * 2,
    )
    rays, mixed = call(
        functools.partial(primal_kernel, slices, bins, rows_tile),
        (signal, hits, footprint_table, near_weight, primal_state),
        (FAR, LISTS) + (FAR,) * 3,
        [
            shape_of((count, tables, height, UW), BF16),
            shape_of((2 * kept + (rows_tile + 4) * height, cells), BF16),
        ],
        [FAR] * 2,
        [
            VMEM((3 * tables + 1, height, UW), F32),
            VMEM(((rows_tile + 2) * block, cells), BF16),
        ],
    )
    rays = exchange(rays)
    (payload,) = call(
        functools.partial(primal_rest_kernel, slices, rows_tile, blocks, rows),
        (mixed, *tiles),
        (FAR,) * 4,
        [shape_of((count, 8, (per_primal + per_dual) * TILE + UW), BF16)],
        [PASS],
        [VMEM((count, 8, per_primal * TILE), BF16), pltpu.SemaphoreType.DMA((1,))],
    )
    (dual_part,) = call(
        functools.partial(dual_cot_kernel, slices, bins, near_rows),
        (*views, back_weight),
        ranges(head, head + rows) + ((2 * rows + height, 3 * rows + height),),
        [shape_of((3 * rows, detector), F32)],
        [FAR],
        [VMEM((5 * block, detector), BF16)],
    )
    dual_grad, payload = call(
        functools.partial(dual_backward_kernel, slices, bins, per_dual, head, near_rows),
        (*views, rays, hits, back_weight, dual_part, slope, hidden, payload),
        ranges(0, near_rows) + (FAR, LISTS, (0, 2 * rows + height)) + (FAR,) * 3 + (PASS,),
        [shape_of(dual_flat, BF16), shape_of(payload.shape, BF16)],
        [FAR, PASS],
        [
            VMEM((5 * columns, height, UW), F32),
            VMEM((3 * block, detector), BF16),
            VMEM((columns, height, UW), BF16),
            VMEM((count, 8, per_dual * TILE + UW), BF16),
            pltpu.SemaphoreType.DMA((1,)),
        ],
        alias={10: 1},
    )
    payload = exchange(payload)
    payload, signal = call(
        sum_kernel,
        (payload,),
        (HERE,),
        [shape_of((count, 8, width), BF16), shape_of((count, height, UW), BF16)],
        [HERE, HERE],
        limit=2 * 1024 * 1024,
    )
    payload = exchange(payload)
    new_volume, volume_grad = call(
        functools.partial(volume_grad_kernel, slices, bins, rows_tile),
        (mixed, tile, primal_inner, primal_outer, biases, footprint_table)
        + (bin_energy, basis_table, signal, hits),
        (FAR,) * 6 + (LISTS, FAR, HERE, LISTS),
        [shape_of(volume.shape, BF16)] * 2,
        [FAR] * 2,
        [VMEM(((rows_tile + 2) * block, cells), BF16)] * 2
        + [VMEM((rows_tile * rows, cells), F32), VMEM((tables + 1, height, UW), F32)],
        limit=16 * 1024 * 1024,
    )
    gradients = call(
        functools.partial(unpack_kernel, slices, per_primal, per_dual),
        (payload,),
        (HERE,),
        [shape_of(w.shape, F32) for w in (primal_inner, primal_outer, dual_inner, dual_outer)],
        [HERE] * 4,
        limit=8 * 1024 * 1024,
    )
    return (
        new_volume,
        new_dual.reshape(dual_state.shape),
        volume_grad,
        dual_grad.reshape(dual_state.shape),
        *gradients,
    )


def solution(mesh):
    split = P(None, "parts", "view", None)
    in_specs = (split,) * 5 + (P(),) * 15
    out_specs = (split,) * 4 + (P("parts", None, None),) * 4
    return jax.shard_map(whole, mesh=mesh, in_specs=in_specs, out_specs=out_specs, check_vma=False)
```
